512 devices in a mesh: rows: 64 (over y, z), cols: 8 (over x, core).
Axes of the slice: x: 4, y: 4, z: 16, core: 2. Of those that a mesh axis runs over, the one named last changes fastest.
Arguments:
- vectors: float32 [512, 131072], P(None, ('rows', 'cols')), may hold values from -80 to 80
- offsets: int32 [16, 131072], P(None, ('rows', 'cols')), may hold values from -256 to 256, as said below
- counts: int32 [131072], P(('rows', 'cols')), may hold values from 8 to 16
- labels: int32 [2, 131072], P(None, ('rows', 'cols')), may hold values from 0 to 1
- cosines: float32 [16, 131072], P(None, ('rows', 'cols')), may hold values from -1 to 1
- distances: float32 [16, 131072], P(None, ('rows', 'cols')), may hold values from 1 to 3
Outputs:
- basis: float32 [512, 131072], P('cols', 'rows')
The draws below stay inside these ranges and needn't reach their ends.
Inputs may be any that keep to these rules, and one draw needn't show every extreme that they name: `offsets`: each offset is nonzero and at most 256 in magnitude; both -256 and 256 occur. Offsets follow a lattice: small in-row steps, steps near half of 256, and steps near 256.
All inputs are finite; a program needn't handle non-finite values.
Results may differ from the reference program's by a relative error of at most 0.00012.
Values sent between devices are 32-bit elements; how exact they have to be, the bound alone decides.
No kernel may reach another device: no remote copies, remote signals or barrier semaphores. Data moves between devices by JAX's collectives and lax.ppermute only.
A program may use at most 64 MiB of HBM per device.

```python
import math
import jax
import jax.numpy as jnp
from jax import lax

BLOCK = 64
SLOTS = 16
REACH = 256
NV = 512
ATOMS = 131072
STEPS = 3


def geometry(key):
    base_key = jax.random.fold_in(key, 11)
    first_key, second_key = jax.random.split(base_key, 2)
    cosine_part = jax.random.uniform(first_key, (SLOTS, ATOMS), jnp.float32, -1.0, 1.0)
    spread = jax.random.uniform(second_key, (SLOTS, ATOMS), jnp.float32, 0.0, 0.6)
    length = 1.0 + 1.36 * cosine_part * cosine_part + spread
    return (cosine_part, length)


def draw_cosines(key, part):
    return geometry(key)[0].astype(jnp.float32)


def draw_distances(key, part):
    return geometry(key)[1].astype(jnp.float32)


def draw_offsets(key, part):
    base_key = jax.random.fold_in(key, 23)
    keys = jax.random.split(base_key, 6)
    kind = jax.random.randint(keys[0], (SLOTS, ATOMS), 0, 3)
    signs = jax.random.randint(keys[1], (SLOTS, ATOMS), 0, 2) * 2 - 1
    near_step = 1 + jax.random.randint(keys[2], (SLOTS, ATOMS), 0, 2)
    middle_step = REACH // 2 + jax.random.randint(keys[3], (SLOTS, ATOMS), -2, 3)
    far_step = REACH - jax.random.randint(keys[4], (SLOTS, ATOMS), 0, 3)
    magnitude = jnp.where(kind == 0, near_step, jnp.where(kind == 1, middle_step, far_step))
    magnitude = jnp.clip(magnitude, 1, REACH)
    spots = jax.random.randint(keys[5], (2,), 0, ATOMS)
    shifted = magnitude * signs
    shifted = shifted.at[0, spots[0]].set(REACH)
    shifted = shifted.at[1, spots[1]].set(-REACH)
    return shifted.astype(jnp.int32)


def draw_vectors(key, part):
    base_key = jax.random.fold_in(key, 31)
    keys = jax.random.split(base_key, 3)
    position = jnp.arange(ATOMS, dtype=jnp.float32) / ATOMS
    row_scale = jnp.exp(jax.random.uniform(keys[0], (1, ATOMS), jnp.float32, math.log(0.3), math.log(3.0)))
    col_scale = jnp.exp(jax.random.uniform(keys[1], (NV, 1), jnp.float32, math.log(0.3), math.log(3.0)))
    core = jnp.clip(jax.random.normal(keys[2], (NV, ATOMS), jnp.float32), -4.0, 4.0)
    trend = 1.0 + 2.0 * position[None, :]
    result = core * row_scale * trend * col_scale / 1.5
    return result.astype(jnp.float32)


def with_ends(drawn, key, low, top_value):
    longest = drawn.shape.index(max(drawn.shape))
    spots = []
    for shift in (0, 1):
        where = [jax.random.randint(jax.random.fold_in(key, axis), (), 0, length) for axis, length in enumerate(drawn.shape)]
        where[longest] = (where[longest] + shift) % drawn.shape[longest]
        spots.append(tuple(where))
    return drawn.at[spots[0]].set(low).at[spots[1]].set(top_value)


def setup_inputs(seed: int = 0) -> dict:
    seeds = jax.random.split(jax.random.key(seed), 7)
    return {
        "vectors": draw_vectors(jax.random.fold_in(seeds[6], 71), 0),
        "offsets": draw_offsets(jax.random.fold_in(seeds[6], 71), 0),
        "counts": with_ends(jax.random.randint(seeds[2], (ATOMS,), SLOTS // 2, SLOTS + 1), jax.random.fold_in(seeds[2], 1), SLOTS // 2, SLOTS).astype(jnp.int32),
        "labels": with_ends(jax.random.randint(seeds[3], (2, ATOMS), 0, 2), jax.random.fold_in(seeds[3], 1), 0, 1).astype(jnp.int32),
        "cosines": draw_cosines(jax.random.fold_in(seeds[6], 71), 0),
        "distances": draw_distances(jax.random.fold_in(seeds[6], 71), 0),
    }


PI_BOND = -1.0
SIGMA_BOND = 0.178
DECAY_LENGTH = 0.319
LAYER_GAP = 2.36
SITE_MASS = 0.4
LAYER_BIAS = 0.25

def hop_table(cosines, distances, counts):
    square = cosines * cosines
    bond_value = PI_BOND * jnp.exp(-(distances - 1.0) / DECAY_LENGTH) * (1.0 - square)
    bond_value = bond_value + SIGMA_BOND * jnp.exp(-(distances - LAYER_GAP) / DECAY_LENGTH) * square
    slot_index = lax.broadcasted_iota(jnp.int32, cosines.shape, 0)
    return jnp.where(slot_index < counts[None, :], bond_value, jnp.zeros_like(bond_value))

def onsite_of(labels):
    sublattice = (2 * labels[0] - 1).astype(jnp.float32)
    layer_sign = (2 * labels[1] - 1).astype(jnp.float32)
    return SITE_MASS * sublattice + LAYER_BIAS * layer_sign

def hamiltonian(source, hopping, offsets, onsite):
    atom_total = source.shape[1]
    column = jnp.arange(atom_total, dtype=jnp.int32)

    def advance(slot_index, running):
        target = (column + offsets[slot_index]) % atom_total
        return running + hopping[slot_index][None, :] * jnp.take(source, target, axis=1)
    return lax.fori_loop(0, hopping.shape[0], advance, onsite[None, :] * source)

def reference(vectors, offsets, counts, labels, cosines, distances):
    hopping = hop_table(cosines, distances, counts)
    onsite = onsite_of(labels)
    applied = hamiltonian(hamiltonian(vectors, hopping, offsets, onsite), hopping, offsets, onsite)
    blocks = [applied[block_index * BLOCK:(block_index + 1) * BLOCK] for block_index in range(NV // BLOCK)]
    highest = lax.Precision.HIGHEST
    for step_index in range(STEPS):
        gram_matrix = jnp.dot(blocks[step_index], blocks[step_index].T, precision=highest) / ATOMS
        factor = jnp.linalg.cholesky(gram_matrix)
        blocks[step_index] = jax.scipy.linalg.solve_triangular(factor, blocks[step_index], lower=True)
        for following in range(step_index + 1, len(blocks)):
            coupling = jnp.dot(blocks[step_index], blocks[following].T, precision=highest) / ATOMS
            blocks[following] = blocks[following] - jnp.dot(coupling.T, blocks[step_index], precision=highest)
    return jnp.concatenate(blocks, axis=0)
```

```python
import jax
import jax.numpy as jnp
import numpy as np
from jax import lax
from jax.experimental import pallas as pl
from jax.experimental.pallas import tpu as pltpu
from jax.sharding import Mesh, PartitionSpec as P

PI_BOND = -1.0
SIGMA_BOND = 0.178
DECAY_LENGTH = 0.319
LAYER_GAP = 2.36
SITE_MASS = 0.4
LAYER_BIAS = 0.25

BLOCK = 64
STEPS = 3
HEAD = BLOCK * STEPS
SLOTS = 16
REACH = 256
NV = 512
LOCAL = 256
WIDE = LOCAL + 2 * REACH
Y_SIZE = 4
F32 = jnp.float32
BF16 = jnp.bfloat16
HIGHEST = lax.Precision.HIGHEST
VMEM = pl.BlockSpec(memory_space=pltpu.VMEM)
PARAMS = pltpu.CompilerParams(vmem_limit_bytes=48 * 1024 * 1024)


def hop_rows(table):
    cosines = table[0:16]
    distances = table[16:32]
    offsets = table[32:48]
    counts = table[48:49]
    square = cosines * cosines
    bond = PI_BOND * jnp.exp(-(distances - 1.0) / DECAY_LENGTH) * (1.0 - square)
    bond = bond + SIGMA_BOND * jnp.exp(-(distances - LAYER_GAP) / DECAY_LENGTH) * square
    slot = lax.broadcasted_iota(jnp.int32, bond.shape, 0).astype(F32)
    hopping = jnp.where(slot < counts, bond, 0.0)
    onsite = SITE_MASS * (2.0 * table[49:50] - 1.0) + LAYER_BIAS * (2.0 * table[50:51] - 1.0)
    return hopping, offsets, onsite


def build_matrix(table, high_ref, low_ref):
    hopping, offsets, onsite = hop_rows(table)
    lane = lax.broadcasted_iota(jnp.int32, (1, 128), 1).astype(F32)
    row_index = lax.broadcasted_iota(jnp.int32, (16, 128), 0).astype(F32)
    for half in range(2):
        columns = slice(128 * half, 128 * half + 128)
        empty = 640 * (1 - half)
        high_ref[empty : empty + 128, columns] = jnp.zeros((128, 128), BF16)
        low_ref[empty : empty + 128, columns] = jnp.zeros((128, 128), BF16)
        home = lane + float(REACH)
        targets = [
            jnp.broadcast_to(offsets[k : k + 1, columns] + home, (16, 128)) for k in range(SLOTS)
        ]
        values = [jnp.broadcast_to(hopping[k : k + 1, columns], (16, 128)) for k in range(SLOTS)]
        homes = jnp.broadcast_to(home, (16, 128))
        own = jnp.broadcast_to(onsite[:, columns], (16, 128))

        def chunk(step, carry):
            base = step * 16
            rows = row_index + base.astype(F32)
            total = jnp.where(homes == rows, own, 0.0)
            for k in range(SLOTS):
                total = total + jnp.where(targets[k] == rows, values[k], 0.0)
            high = total.astype(BF16)
            low = (total - high.astype(F32)).astype(BF16)
            place = pl.ds(pl.multiple_of(base + 128 * half, 16), 16)
            high_ref[place, columns] = high
            low_ref[place, columns] = low
            return carry

        lax.fori_loop(0, 40, chunk, 0)


def own_matrix_kernel(table_ref, high_ref, low_ref):
    build_matrix(table_ref[...], high_ref, low_ref)


def split(value):
    high = value.astype(BF16)
    return high, (value - high.astype(F32)).astype(BF16)


def dot3(high, low, matrix_high, matrix_low):
    def dot(left, right):
        return jnp.dot(left, right, preferred_element_type=F32)

    return dot(high, matrix_high) + (dot(high, matrix_low) + dot(low, matrix_high))


def apply_kernel(
    left2_ref, left_ref, own_ref, right_ref, right2_ref, own_high_ref, own_low_ref,
    applied_ref, gram_ref, high_ref, low_ref, once_high_ref, once_low_ref, left_high_ref,
    left_low_ref, right_high_ref, right_low_ref,
):
    build_matrix(left_ref[NV:, :], left_high_ref, left_low_ref)
    build_matrix(right_ref[NV:, :], right_high_ref, right_low_ref)
    for place, ref in enumerate((left2_ref, left_ref, own_ref, right_ref, right2_ref)):
        columns = slice(LOCAL * place, LOCAL * place + LOCAL)
        high, low = split(ref[0:NV, :])
        high_ref[:, columns] = high
        low_ref[:, columns] = low
    matrices = (
        (left_high_ref, left_low_ref),
        (own_high_ref, own_low_ref),
        (right_high_ref, right_low_ref),
    )
    for place, (matrix_high, matrix_low) in enumerate(matrices):
        window = slice(LOCAL * place, LOCAL * place + WIDE)
        columns = slice(LOCAL * place, LOCAL * place + LOCAL)
        once = dot3(high_ref[:, window], low_ref[:, window], matrix_high[...], matrix_low[...])
        high, low = split(once)
        once_high_ref[:, columns] = high
        once_low_ref[:, columns] = low
    applied = dot3(once_high_ref[...], once_low_ref[...], own_high_ref[...], own_low_ref[...])
    applied_ref[...] = applied
    gram = lax.dot_general(
        applied[0:HEAD], applied, (((1,), (1,)), ((), ())), precision=HIGHEST,
        preferred_element_type=F32,
    )
    for part in range(NV // 128):
        gram_ref[part] = gram[:, 128 * part : 128 * part + 128]


def inverse_factor(pair):
    rows = lax.broadcasted_iota(jnp.int32, (BLOCK, 1), 0)
    work = pair
    scales = jnp.zeros((BLOCK, 1), F32)
    for j in range(BLOCK):
        row = work[j : j + 1, :]
        pivot = row[:, BLOCK + j : BLOCK + j + 1]
        scales = jnp.where(rows == j, lax.rsqrt(pivot), scales)
        column = jnp.where(rows > j, work[:, BLOCK + j : BLOCK + j + 1], 0.0)
        work = work - column * (row * (1.0 / pivot))
    return (work * scales)[:, 0:BLOCK]


def dot32(left, right, dims):
    return lax.dot_general(
        left, right, (dims, ((), ())), precision=HIGHEST, preferred_element_type=F32
    )


def finish_kernel(scale, gram_ref, applied_ref, basis_ref):
    gram = [
        jnp.concatenate(
            [gram_ref[part, BLOCK * s : BLOCK * s + BLOCK, :] for part in range(NV // 128)], axis=1
        )
        * scale
        for s in range(STEPS)
    ]
    lane = lax.broadcasted_iota(jnp.int32, (BLOCK, 128), 1)
    row = lax.broadcasted_iota(jnp.int32, (BLOCK, 128), 0)
    identity = jnp.where(lane == row, 1.0, 0.0).astype(F32)
    couplings = []
    inverses = []
    for s in range(STEPS):
        part = (BLOCK * s) // 128
        tile = gram[s][:, 128 * part : 128 * part + 128]
        if (BLOCK * s) % 128 == 0:
            tile = pltpu.roll(tile, BLOCK, axis=1)
        inverse = inverse_factor(jnp.where(lane < BLOCK, identity, tile))
        coupling = dot32(inverse, gram[s], ((1,), (0,)))
        for t in range(s + 1, STEPS):
            gram[t] = gram[t] - dot32(
                coupling[:, BLOCK * t : BLOCK * t + BLOCK], coupling, ((0,), (0,))
            )
        inverses.append(inverse)
        couplings.append(coupling)
    leaders = []
    for s in range(STEPS):
        block = applied_ref[BLOCK * s : BLOCK * s + BLOCK, :]
        for t in range(s):
            block = block - dot32(
                couplings[t][:, BLOCK * s : BLOCK * s + BLOCK], leaders[t], ((0,), (0,))
            )
        leader = dot32(inverses[s], block, ((1,), (0,)))
        leaders.append(leader)
        basis_ref[BLOCK * s : BLOCK * s + BLOCK, :] = leader
    stacked = jnp.concatenate([c[:, HEAD:] for c in couplings], axis=0)
    leading = jnp.concatenate(leaders, axis=0)
    basis_ref[HEAD:, :] = applied_ref[HEAD:, :] - dot32(stacked, leading, ((0,), (0,)))


def exchange(value, axes):
    return lax.all_to_all(value, axes, split_axis=0, concat_axis=0, tiled=True)


def on_device(vectors, offsets, counts, labels, cosines, distances):
    every = ("y", "z", "cols")
    plane = ("y", "cols")
    total = lax.axis_size(every)
    planes = lax.axis_size(plane)
    depth = lax.axis_size("z")

    def shift(value, step):
        return lax.ppermute(value, every, [(i, (i + step) % total) for i in range(total)])

    table = jnp.concatenate(
        [cosines, distances, offsets.astype(F32), counts.astype(F32)[None], labels.astype(F32),
         jnp.zeros((5, LOCAL), F32)], axis=0,
    )
    payload = jnp.concatenate([vectors, table], axis=0)
    left = shift(payload, 1)
    right = shift(payload, -1)
    left2 = shift(vectors, 2)
    right2 = shift(vectors, -2)
    matrix = jax.ShapeDtypeStruct((WIDE, LOCAL), BF16)
    own_high, own_low = pl.pallas_call(
        own_matrix_kernel, out_shape=(matrix, matrix), in_specs=[VMEM], out_specs=(VMEM, VMEM),
        compiler_params=PARAMS, name="own_matrix",
    )(table)
    wide = pltpu.VMEM((WIDE, LOCAL), BF16)
    applied, gram = pl.pallas_call(
        apply_kernel,
        out_shape=(
            jax.ShapeDtypeStruct((NV, LOCAL), F32),
            jax.ShapeDtypeStruct((NV // 128, HEAD, 128), F32),
        ),
        in_specs=[VMEM] * 7,
        out_specs=(VMEM, VMEM),
        scratch_shapes=[pltpu.VMEM((NV, 5 * LOCAL), BF16)] * 2
        + [pltpu.VMEM((NV, WIDE), BF16)] * 2 + [wide] * 4,
        compiler_params=PARAMS,
        name="apply_twice",
    )(left2, left, payload, right, right2, own_high, own_low)
    piece = (NV // 128) * HEAD // planes
    gram = gram.reshape(planes, piece, 128)
    gram = exchange(gram, plane).reshape(planes, piece, 128).sum(0)
    gram = exchange(jnp.broadcast_to(gram[None], (depth, piece, 128)), "z").sum(0)
    gram = exchange(jnp.broadcast_to(gram[None], (planes, piece, 128)), plane)
    gram = gram.reshape(NV // 128, HEAD, 128)
    scale = 1.0 / (LOCAL * total)
    basis = pl.pallas_call(
        lambda *refs: finish_kernel(scale, *refs),
        out_shape=jax.ShapeDtypeStruct((NV, LOCAL), F32),
        in_specs=[VMEM] * 2, out_specs=VMEM, compiler_params=PARAMS, name="finish",
    )(gram, applied)
    return lax.all_to_all(basis, "cols", split_axis=0, concat_axis=1, tiled=True)


def solution(mesh):
    rows = mesh.shape["rows"]
    cols = mesh.shape["cols"]
    cube = Mesh(mesh.devices.reshape(Y_SIZE, rows // Y_SIZE, cols), ("y", "z", "cols"))
    every = ("y", "z", "cols")
    placed = (P(None, every), P(None, every), P(every), P(None, every), P(None, every), P(None, every))
    return jax.shard_map(
        on_device, mesh=cube, in_specs=placed, out_specs=P("cols", ("y", "z")), check_vma=False
    )
```

```python
import jax
import jax.numpy as jnp
import numpy as np
from jax import lax
from jax.experimental import pallas as pl
from jax.experimental.pallas import tpu as pltpu
from jax.sharding import Mesh, PartitionSpec as P

PI_BOND = -1.0
SIGMA_BOND = 0.178
DECAY_LENGTH = 0.319
LAYER_GAP = 2.36
SITE_MASS = 0.4
LAYER_BIAS = 0.25

BLOCK = 64
STEPS = 3
HEAD = BLOCK * STEPS
SLOTS = 16
REACH = 256
NV = 512
LOCAL = 256
WIDE = LOCAL + 2 * REACH
Y_SIZE = 4
F32 = jnp.float32
BF16 = jnp.bfloat16
HIGHEST = lax.Precision.HIGHEST
VMEM = pl.BlockSpec(memory_space=pltpu.VMEM)
PARAMS = pltpu.CompilerParams(vmem_limit_bytes=48 * 1024 * 1024)


def hop_rows(table):
    cosines = table[0:16]
    distances = table[16:32]
    offsets = table[32:48]
    counts = table[48:49]
    square = cosines * cosines
    bond = PI_BOND * jnp.exp(-(distances - 1.0) / DECAY_LENGTH) * (1.0 - square)
    bond = bond + SIGMA_BOND * jnp.exp(-(distances - LAYER_GAP) / DECAY_LENGTH) * square
    slot = lax.broadcasted_iota(jnp.int32, bond.shape, 0).astype(F32)
    hopping = jnp.where(slot < counts, bond, 0.0)
    onsite = SITE_MASS * (2.0 * table[49:50] - 1.0) + LAYER_BIAS * (2.0 * table[50:51] - 1.0)
    return hopping, offsets, onsite


def build_matrix(table, high_ref, low_ref):
    hopping, offsets, onsite = hop_rows(table)
    lane = lax.broadcasted_iota(jnp.int32, (1, 128), 1).astype(F32)
    row_index = lax.broadcasted_iota(jnp.int32, (16, 128), 0).astype(F32)
    for half in range(2):
        columns = slice(128 * half, 128 * half + 128)
        empty = 640 * (1 - half)
        high_ref[empty : empty + 128, columns] = jnp.zeros((128, 128), BF16)
        low_ref[empty : empty + 128, columns] = jnp.zeros((128, 128), BF16)
        home = lane + float(REACH)
        targets = [
            jnp.broadcast_to(offsets[k : k + 1, columns] + home, (16, 128)) for k in range(SLOTS)
        ]
        values = [jnp.broadcast_to(hopping[k : k + 1, columns], (16, 128)) for k in range(SLOTS)]
        homes = jnp.broadcast_to(home, (16, 128))
        own = jnp.broadcast_to(onsite[:, columns], (16, 128))

        def chunk(step, carry):
            base = step * 16
            rows = row_index + base.astype(F32)
            total = jnp.where(homes == rows, own, 0.0)
            for k in range(SLOTS):
                total = total + jnp.where(targets[k] == rows, values[k], 0.0)
            high = total.astype(BF16)
            low = (total - high.astype(F32)).astype(BF16)
            place = pl.ds(pl.multiple_of(base + 128 * half, 16), 16)
            high_ref[place, columns] = high
            low_ref[place, columns] = low
            return carry

        lax.fori_loop(0, 40, chunk, 0)


def own_matrix_kernel(table_ref, high_ref, low_ref):
    build_matrix(table_ref[...], high_ref, low_ref)


def split(value):
    high = value.astype(BF16)
    return high, (value - high.astype(F32)).astype(BF16)


def dot3(high, low, matrix_high, matrix_low):
    def dot(left, right):
        return jnp.dot(left, right, preferred_element_type=F32)

    return dot(high, matrix_high) + (dot(high, matrix_low) + dot(low, matrix_high))


def apply_kernel(
    left2_ref, left_ref, own_ref, right_ref, right2_ref, own_high_ref, own_low_ref,
    applied_ref, gram_ref, high_ref, low_ref, once_high_ref, once_low_ref, left_high_ref,
    left_low_ref, right_high_ref, right_low_ref,
):
    build_matrix(left_ref[NV:, :], left_high_ref, left_low_ref)
    build_matrix(right_ref[NV:, :], right_high_ref, right_low_ref)
    for place, ref in enumerate((left2_ref, left_ref, own_ref, right_ref, right2_ref)):
        columns = slice(LOCAL * place, LOCAL * place + LOCAL)
        high, low = split(ref[0:NV, :])
        high_ref[:, columns] = high
        low_ref[:, columns] = low
    matrices = (
        (left_high_ref, left_low_ref),
        (own_high_ref, own_low_ref),
        (right_high_ref, right_low_ref),
    )
    for place, (matrix_high, matrix_low) in enumerate(matrices):
        window = slice(LOCAL * place, LOCAL * place + WIDE)
        columns = slice(LOCAL * place, LOCAL * place + LOCAL)
        once = dot3(high_ref[:, window], low_ref[:, window], matrix_high[...], matrix_low[...])
        high, low = split(once)
        once_high_ref[:, columns] = high
        once_low_ref[:, columns] = low
    applied = dot3(once_high_ref[...], once_low_ref[...], own_high_ref[...], own_low_ref[...])
    applied_ref[...] = applied
    gram = lax.dot_general(
        applied[0:HEAD], applied, (((1,), (1,)), ((), ())), precision=HIGHEST,
        preferred_element_type=F32,
    )
    for part in range(NV // 128):
        gram_ref[part] = gram[:, 128 * part : 128 * part + 128]


def spread(value):
    return jnp.broadcast_to(value, (8, 128))


def inverse_factor(pair):
    rows = [pair[8 * i : 8 * i + 8] for i in range(BLOCK // 8)]
    sublane = lax.broadcasted_iota(jnp.int32, (8, 128), 0)
    for p in range(BLOCK // 8):
        start = BLOCK + 8 * p
        columns = [
            [spread(rows[i][:, start + b : start + b + 1]) for b in range(8)]
            for i in range(p, BLOCK // 8)
        ]
        for j in range(8):
            inverse = lax.rsqrt(spread(columns[0][j][j : j + 1]))
            pivot_row = spread(rows[p][j : j + 1]) * inverse
            heads = [spread(columns[0][b][j : j + 1]) * inverse for b in range(j + 1, 8)]
            for i in range(p, BLOCK // 8):
                factor = columns[i - p][j] * inverse
                if i == p:
                    factor = jnp.where(sublane > j, factor, 0.0)
                rows[i] = rows[i] - factor * pivot_row
                for b in range(j + 1, 8):
                    columns[i - p][b] = columns[i - p][b] - factor * heads[b - j - 1]
            rows[p] = jnp.where(sublane == j, pivot_row, rows[p])
    return jnp.concatenate(rows, axis=0)[:, 0:BLOCK]


def dot32(left, right, dims):
    return lax.dot_general(
        left, right, (dims, ((), ())), precision=HIGHEST, preferred_element_type=F32
    )


def finish_kernel(scale, gram_ref, applied_ref, basis_ref):
    gram = [
        jnp.concatenate(
            [gram_ref[part, BLOCK * s : BLOCK * s + BLOCK, :] for part in range(NV // 128)], axis=1
        )
        * scale
        for s in range(STEPS)
    ]
    lane = lax.broadcasted_iota(jnp.int32, (BLOCK, 128), 1)
    row = lax.broadcasted_iota(jnp.int32, (BLOCK, 128), 0)
    identity = jnp.where(lane == row, 1.0, 0.0).astype(F32)
    couplings = []
    inverses = []
    for s in range(STEPS):
        part = (BLOCK * s) // 128
        tile = gram[s][:, 128 * part : 128 * part + 128]
        if (BLOCK * s) % 128 == 0:
            tile = pltpu.roll(tile, BLOCK, axis=1)
        inverse = inverse_factor(jnp.where(lane < BLOCK, identity, tile))
        coupling = dot32(inverse, gram[s], ((1,), (0,)))
        for t in range(s + 1, STEPS):
            gram[t] = gram[t] - dot32(
                coupling[:, BLOCK * t : BLOCK * t + BLOCK], coupling, ((0,), (0,))
            )
        inverses.append(inverse)
        couplings.append(coupling)
    leaders = []
    for s in range(STEPS):
        block = applied_ref[BLOCK * s : BLOCK * s + BLOCK, :]
        for t in range(s):
            block = block - dot32(
                couplings[t][:, BLOCK * s : BLOCK * s + BLOCK], leaders[t], ((0,), (0,))
            )
        leader = dot32(inverses[s], block, ((1,), (0,)))
        leaders.append(leader)
        basis_ref[BLOCK * s : BLOCK * s + BLOCK, :] = leader
    stacked = jnp.concatenate([c[:, HEAD:] for c in couplings], axis=0)
    leading = jnp.concatenate(leaders, axis=0)
    basis_ref[HEAD:, :] = applied_ref[HEAD:, :] - dot32(stacked, leading, ((0,), (0,)))


def exchange(value, axes):
    return lax.all_to_all(value, axes, split_axis=0, concat_axis=0, tiled=True)


def on_device(vectors, offsets, counts, labels, cosines, distances):
    every = ("y", "z", "cols")
    plane = ("y", "cols")
    total = lax.axis_size(every)
    planes = lax.axis_size(plane)
    depth = lax.axis_size("z")

    def shift(value, step):
        return lax.ppermute(value, every, [(i, (i + step) % total) for i in range(total)])

    table = jnp.concatenate(
        [cosines, distances, offsets.astype(F32), counts.astype(F32)[None], labels.astype(F32),
         jnp.zeros((5, LOCAL), F32)], axis=0,
    )
    payload = jnp.concatenate([vectors, table], axis=0)
    left = shift(payload, 1)
    right = shift(payload, -1)
    left2 = shift(vectors, 2)
    right2 = shift(vectors, -2)
    matrix = jax.ShapeDtypeStruct((WIDE, LOCAL), BF16)
    own_high, own_low = pl.pallas_call(
        own_matrix_kernel, out_shape=(matrix, matrix), in_specs=[VMEM], out_specs=(VMEM, VMEM),
        compiler_params=PARAMS, name="own_matrix",
    )(table)
    wide = pltpu.VMEM((WIDE, LOCAL), BF16)
    applied, gram = pl.pallas_call(
        apply_kernel,
        out_shape=(
            jax.ShapeDtypeStruct((NV, LOCAL), F32),
            jax.ShapeDtypeStruct((NV // 128, HEAD, 128), F32),
        ),
        in_specs=[VMEM] * 7,
        out_specs=(VMEM, VMEM),
        scratch_shapes=[pltpu.VMEM((NV, 5 * LOCAL), BF16)] * 2
        + [pltpu.VMEM((NV, WIDE), BF16)] * 2 + [wide] * 4,
        compiler_params=PARAMS,
        name="apply_twice",
    )(left2, left, payload, right, right2, own_high, own_low)
    piece = (NV // 128) * HEAD // planes
    gram = gram.reshape(planes, piece, 128)
    gram = exchange(gram, plane).reshape(planes, piece, 128).sum(0)
    gram = exchange(jnp.broadcast_to(gram[None], (depth, piece, 128)), "z").sum(0)
    gram = exchange(jnp.broadcast_to(gram[None], (planes, piece, 128)), plane)
    gram = gram.reshape(NV // 128, HEAD, 128)
    scale = 1.0 / (LOCAL * total)
    basis = pl.pallas_call(
        lambda *refs: finish_kernel(scale, *refs),
        out_shape=jax.ShapeDtypeStruct((NV, LOCAL), F32),
        in_specs=[VMEM] * 2, out_specs=VMEM, compiler_params=PARAMS, name="finish",
    )(gram, applied)
    return lax.all_to_all(basis, "cols", split_axis=0, concat_axis=1, tiled=True)


def solution(mesh):
    rows = mesh.shape["rows"]
    cols = mesh.shape["cols"]
    cube = Mesh(mesh.devices.reshape(Y_SIZE, rows // Y_SIZE, cols), ("y", "z", "cols"))
    every = ("y", "z", "cols")
    placed = (P(None, every), P(None, every), P(every), P(None, every), P(None, every), P(None, every))
    return jax.shard_map(
        on_device, mesh=cube, in_specs=placed, out_specs=P("cols", ("y", "z")), check_vma=False
    )
```

```python
import jax
import jax.numpy as jnp
from jax import lax
from jax.experimental import pallas as pl
from jax.experimental.pallas import tpu as pltpu
from jax.sharding import Mesh, PartitionSpec as P

PI_BOND = -1.0
SIGMA_BOND = 0.178
DECAY_LENGTH = 0.319
LAYER_GAP = 2.36
SITE_MASS = 0.4
LAYER_BIAS = 0.25

BLOCK = 64
STEPS = 3
HEAD = BLOCK * STEPS
SLOTS = 16
REACH = 256
NV = 512
LOCAL = 256
WIDE = LOCAL + 2 * REACH
Y_SIZE = 4
CORES = 2
OWN = NV // CORES
TABLE = 40
CHIP = CORES * LOCAL
F32 = jnp.float32
BF16 = jnp.bfloat16
HIGHEST = lax.Precision.HIGHEST
VMEM = pl.BlockSpec(memory_space=pltpu.VMEM)
PARAMS = pltpu.CompilerParams(vmem_limit_bytes=48 * 1024 * 1024)


def pack_kernel(vectors_ref, cosines_ref, distances_ref, offsets_ref, counts_ref, labels_ref, out_ref):
    square = cosines_ref[...] * cosines_ref[...]
    distances = distances_ref[...]
    bond = PI_BOND * jnp.exp(-(distances - 1.0) / DECAY_LENGTH) * (1.0 - square)
    bond = bond + SIGMA_BOND * jnp.exp(-(distances - LAYER_GAP) / DECAY_LENGTH) * square
    slot = lax.broadcasted_iota(jnp.int32, bond.shape, 0)
    hopping = jnp.where(slot < counts_ref[...], bond, 0.0)
    offsets = offsets_ref[...].astype(F32)
    merged = jnp.zeros_like(hopping)
    for k in range(SLOTS):
        merged = merged + jnp.where(offsets == offsets[k : k + 1], hopping[k : k + 1], 0.0)
    labels = labels_ref[...].astype(F32)
    onsite = SITE_MASS * (2.0 * labels[0:1] - 1.0) + LAYER_BIAS * (2.0 * labels[1:2] - 1.0)
    for core in range(CORES):
        for p in range(OWN // BLOCK):
            source = BLOCK * (core + CORES * p)
            out_ref[core, BLOCK * p : BLOCK * p + BLOCK, :] = vectors_ref[source : source + BLOCK, :]
        out_ref[core, OWN : OWN + 16, :] = merged
        out_ref[core, OWN + 16 : OWN + 32, :] = offsets
        out_ref[core, OWN + 32 : OWN + 40, :] = jnp.broadcast_to(onsite, (8, LOCAL))


def build_matrix(table, high_ref, low_ref):
    hopping, offsets, onsite = table[0:16], table[16:32], table[32:33]
    lane = lax.broadcasted_iota(jnp.int32, (1, 128), 1).astype(F32)
    row_index = lax.broadcasted_iota(jnp.int32, (32, 128), 0).astype(F32)
    for half in range(2):
        columns = slice(128 * half, 128 * half + 128)
        empty = 640 * (1 - half)
        high_ref[empty : empty + 128, columns] = jnp.zeros((128, 128), BF16)
        low_ref[empty : empty + 128, columns] = jnp.zeros((128, 128), BF16)
        home = lane + float(REACH)
        targets = [
            jnp.broadcast_to(offsets[k : k + 1, columns] + home, (32, 128)) for k in range(SLOTS)
        ]
        values = [jnp.broadcast_to(hopping[k : k + 1, columns], (32, 128)) for k in range(SLOTS)]
        homes = jnp.broadcast_to(home, (32, 128))
        own = jnp.broadcast_to(onsite[:, columns], (32, 128))

        def chunk(step, carry):
            base = step * 32
            rows = row_index + base.astype(F32)
            total = jnp.where(homes == rows, own, 0.0)
            for k in range(SLOTS):
                total = jnp.where(targets[k] == rows, values[k], total)
            high = total.astype(BF16)
            low = (total - high.astype(F32)).astype(BF16)
            place = pl.ds(pl.multiple_of(base + 128 * half, 32), 32)
            high_ref[place, columns] = high
            low_ref[place, columns] = low
            return carry

        lax.fori_loop(0, 20, chunk, 0)


def own_matrix_kernel(slab_ref, *refs):
    for core in range(CORES):
        build_matrix(slab_ref[core, OWN:, :], refs[2 * core], refs[2 * core + 1])


def split(value):
    high = value.astype(BF16)
    return high, (value - high.astype(F32)).astype(BF16)


def dot3(high, low, matrix_high, matrix_low):
    def dot(left, right):
        return jnp.dot(left, right, preferred_element_type=F32)

    return dot(high, matrix_high) + (dot(high, matrix_low) + dot(low, matrix_high))


def apply_kernel(
    left_ref, own_ref, right_ref, first_high_ref, first_low_ref, second_high_ref, second_low_ref,
    applied_ref, head_ref, high_ref, low_ref, once_high_ref, once_low_ref,
    left_high_ref, left_low_ref, right_high_ref, right_low_ref,
):
    build_matrix(left_ref[1, OWN:, :], left_high_ref, left_low_ref)
    build_matrix(right_ref[0, OWN:, :], right_high_ref, right_low_ref)
    sources = [(ref, core) for ref in (left_ref, own_ref, right_ref) for core in range(CORES)]
    for place, (ref, core) in enumerate(sources):
        columns = slice(LOCAL * place, LOCAL * place + LOCAL)
        high, low = split(ref[core, 0:OWN, :])
        high_ref[:, columns] = high
        low_ref[:, columns] = low
    matrices = (
        (left_high_ref, left_low_ref),
        (first_high_ref, first_low_ref),
        (second_high_ref, second_low_ref),
        (right_high_ref, right_low_ref),
    )
    for place, (matrix_high, matrix_low) in enumerate(matrices):
        window = slice(LOCAL * place, LOCAL * place + WIDE)
        columns = slice(LOCAL * place, LOCAL * place + LOCAL)
        once = dot3(high_ref[:, window], low_ref[:, window], matrix_high[...], matrix_low[...])
        high, low = split(once)
        once_high_ref[:, columns] = high
        once_low_ref[:, columns] = low
    for place, (matrix_high, matrix_low) in enumerate(matrices[1:3]):
        window = slice(LOCAL * place, LOCAL * place + WIDE)
        columns = slice(LOCAL * place, LOCAL * place + LOCAL)
        twice = dot3(
            once_high_ref[:, window], once_low_ref[:, window], matrix_high[...], matrix_low[...]
        )
        applied_ref[:, columns] = twice
        for core in range(CORES):
            head_ref[core, :, columns] = twice[0 : 2 * BLOCK]


def head_blocks(head_ref):
    return head_ref[0, 0:BLOCK, :], head_ref[1, 0:BLOCK, :], head_ref[0, BLOCK:, :]


def gram_kernel(head_ref, applied_ref, gram_ref):
    head = jnp.concatenate(head_blocks(head_ref), axis=0)
    gram = dot32(head, applied_ref[...], ((1,), (1,)))
    for part in range(OWN // 128):
        gram_ref[part] = gram[:, 128 * part : 128 * part + 128]


def spread(value):
    return jnp.broadcast_to(value, (8, 128))


def inverse_factor(pair):
    rows = [pair[8 * i : 8 * i + 8] for i in range(BLOCK // 8)]
    sublane = lax.broadcasted_iota(jnp.int32, (8, 128), 0)
    for p in range(BLOCK // 8):
        start = BLOCK + 8 * p
        columns = [
            [spread(rows[i][:, start + b : start + b + 1]) for b in range(8)]
            for i in range(p, BLOCK // 8)
        ]
        for j in range(8):
            inverse = lax.rsqrt(spread(columns[0][j][j : j + 1]))
            pivot_row = spread(rows[p][j : j + 1]) * inverse
            heads = [spread(columns[0][b][j : j + 1]) * inverse for b in range(j + 1, 8)]
            for i in range(p, BLOCK // 8):
                factor = columns[i - p][j] * inverse
                if i == p:
                    factor = jnp.where(sublane > j, factor, 0.0)
                rows[i] = rows[i] - factor * pivot_row
                for b in range(j + 1, 8):
                    columns[i - p][b] = columns[i - p][b] - factor * heads[b - j - 1]
            rows[p] = jnp.where(sublane == j, pivot_row, rows[p])
    return jnp.concatenate(rows, axis=0)[:, 0:BLOCK]


def dot32(left, right, dims):
    return lax.dot_general(
        left, right, (dims, ((), ())), precision=HIGHEST, preferred_element_type=F32
    )


def finish_kernel(scale, core_ref, gram_ref, head_ref, applied_ref, basis_ref):
    second = core_ref[0] == 1
    tiles = gram_ref.shape[0] // 2

    def columns_of(part, core):
        return jnp.concatenate([gram_ref[part * tiles + m, core] for m in range(tiles)], axis=0)

    rest = jnp.where(second, columns_of(1, 1), columns_of(1, 0))
    full = jnp.concatenate([columns_of(0, 0), columns_of(0, 1), rest], axis=1) * scale
    gram = [full[BLOCK * s : BLOCK * s + BLOCK] for s in range(STEPS)]
    places = (0, 2 * BLOCK, BLOCK)
    lane = lax.broadcasted_iota(jnp.int32, (BLOCK, 128), 1)
    row = lax.broadcasted_iota(jnp.int32, (BLOCK, 128), 0)
    identity = jnp.where(lane == row, 1.0, 0.0).astype(F32)
    couplings = []
    inverses = []
    for s in range(STEPS):
        part = places[s] // 128
        tile = gram[s][:, 128 * part : 128 * part + 128]
        if places[s] % 128 == 0:
            tile = pltpu.roll(tile, BLOCK, axis=1)
        inverse = inverse_factor(jnp.where(lane < BLOCK, identity, tile))
        coupling = dot32(inverse, gram[s], ((1,), (0,)))
        for t in range(s + 1, STEPS):
            gram[t] = gram[t] - dot32(
                coupling[:, places[t] : places[t] + BLOCK], coupling, ((0,), (0,))
            )
        inverses.append(inverse)
        couplings.append(coupling)
    leaders = []
    heads = head_blocks(head_ref)
    for s in range(STEPS):
        block = heads[s]
        for t in range(s):
            block = block - dot32(
                couplings[t][:, places[s] : places[s] + BLOCK], leaders[t], ((0,), (0,))
            )
        leaders.append(dot32(inverses[s], block, ((1,), (0,))))
    stacked = jnp.concatenate([c[:, HEAD:] for c in couplings], axis=0)
    leading = jnp.concatenate(leaders, axis=0)
    later = applied_ref[BLOCK:, :] - dot32(stacked, leading, ((0,), (0,)))
    basis_ref[0:BLOCK, :] = jnp.where(second, leaders[1], leaders[0])
    basis_ref[BLOCK : 2 * BLOCK, :] = jnp.where(second, later[0:BLOCK], leaders[2])
    basis_ref[2 * BLOCK :, :] = later[BLOCK:]


def exchange(value, axes):
    return lax.all_to_all(value, axes, split_axis=0, concat_axis=0, tiled=True)


def call(kernel, name, out_shape, inputs, scratch=(), smem=0):
    single = not isinstance(out_shape, (tuple, list))
    return pl.pallas_call(
        kernel,
        out_shape=out_shape,
        in_specs=[pl.BlockSpec(memory_space=pltpu.SMEM)] * smem + [VMEM] * (len(inputs) - smem),
        out_specs=VMEM if single else (VMEM,) * len(out_shape),
        scratch_shapes=list(scratch),
        compiler_params=PARAMS,
        name=name,
    )(*inputs)


def on_device(vectors, offsets, counts, labels, cosines, distances):
    chips = ("y", "z", "x")
    plane = ("y", "x")
    chip_count = lax.axis_size(chips)
    planes = lax.axis_size(plane)
    depth = lax.axis_size("z")

    def shift(value, step):
        return lax.ppermute(value, chips, [(i, (i + step) % chip_count) for i in range(chip_count)])

    shape = jax.ShapeDtypeStruct
    slab = call(
        pack_kernel, "pack", shape((CORES, OWN + TABLE, LOCAL), F32),
        (vectors, cosines, distances, offsets, counts.reshape(1, LOCAL), labels),
    )
    slab = exchange(slab, "core")
    left = shift(slab, 1)
    right = shift(slab, -1)
    matrix = shape((WIDE, LOCAL), BF16)
    matrices = call(own_matrix_kernel, "own_matrix", (matrix,) * 4, (slab,))
    wide = pltpu.VMEM((WIDE, LOCAL), BF16)
    applied, head = call(
        apply_kernel,
        "apply_twice",
        (shape((OWN, CHIP), F32), shape((CORES, 2 * BLOCK, CHIP), F32)),
        (left, slab, right, *matrices),
        [pltpu.VMEM((OWN, 3 * CHIP), BF16)] * 2 + [pltpu.VMEM((OWN, 2 * CHIP), BF16)] * 2 + [wide] * 4,
    )
    head = exchange(head, "core")
    gram = call(gram_kernel, "gram", shape((OWN // 128, HEAD, 128), F32), (head, applied))
    piece = (OWN // 128) * HEAD // planes
    gram = exchange(gram.reshape(planes, piece, 128), plane).sum(0)
    gram = exchange(jnp.broadcast_to(gram[None], (depth, piece, 128)), "z").sum(0)
    everyone = planes * CORES
    gram = exchange(jnp.broadcast_to(gram[None], (everyone, piece, 128)), (*plane, "core"))
    gram = gram.reshape(planes, CORES, piece, 128)
    scale = 1.0 / (CHIP * chip_count)
    basis = call(
        lambda *refs: finish_kernel(scale, *refs), "finish", shape((OWN, CHIP), F32),
        (lax.axis_index("core").reshape(1), gram, head, applied), smem=1,
    )
    return lax.all_to_all(basis, "x", split_axis=0, concat_axis=1, tiled=True)


def solution(mesh):
    rows = mesh.shape["rows"]
    cols = mesh.shape["cols"]
    names = ("y", "z", "x", "core")
    cube = Mesh(mesh.devices.reshape(Y_SIZE, rows // Y_SIZE, cols // CORES, CORES), names)
    whole = P(None, names)
    placed = (whole, whole, P(names), whole, whole, whole)
    return jax.shard_map(
        on_device, mesh=cube, in_specs=placed, out_specs=P(("x", "core"), ("y", "z")),
        check_vma=False,
    )
```

```python
import jax
import jax.numpy as jnp
from jax import lax
from jax.experimental import pallas as pl
from jax.experimental.pallas import tpu as pltpu
from jax.sharding import Mesh, PartitionSpec as P

PI_BOND = -1.0
SIGMA_BOND = 0.178
DECAY_LENGTH = 0.319
LAYER_GAP = 2.36
SITE_MASS = 0.4
LAYER_BIAS = 0.25

BLOCK = 64
STEPS = 3
HEAD = BLOCK * STEPS
SLOTS = 16
REACH = 256
NV = 512
LOCAL = 256
WIDE = LOCAL + 2 * REACH
Y_SIZE = 4
CORES = 2
OWN = NV // CORES
TABLE = 40
CHIP = CORES * LOCAL
F32 = jnp.float32
BF16 = jnp.bfloat16
HIGHEST = lax.Precision.HIGHEST
VMEM = pl.BlockSpec(memory_space=pltpu.VMEM)
PARAMS = pltpu.CompilerParams(vmem_limit_bytes=48 * 1024 * 1024)


def pack_kernel(
    vectors_ref, cosines_ref, distances_ref, offsets_ref, counts_ref, labels_ref, out_ref,
    cosines, distances, offsets, counts, labels, table_sems, block_sems,
):
    tables = (
        (cosines_ref, cosines), (distances_ref, distances), (offsets_ref, offsets),
        (counts_ref, counts), (labels_ref, labels),
    )
    table_copies = [
        pltpu.make_async_copy(source, target, table_sems.at[i])
        for i, (source, target) in enumerate(tables)
    ]
    block_copies = [
        pltpu.make_async_copy(
            vectors_ref.at[pl.ds(BLOCK * (core + CORES * p), BLOCK)],
            out_ref.at[core, pl.ds(BLOCK * p, BLOCK)],
            block_sems.at[core + CORES * p],
        )
        for core in range(CORES)
        for p in range(OWN // BLOCK)
    ]
    for copy in table_copies + block_copies:
        copy.start()
    for copy in table_copies:
        copy.wait()
    square = cosines[...] * cosines[...]
    bond = PI_BOND * jnp.exp(-(distances[...] - 1.0) / DECAY_LENGTH) * (1.0 - square)
    bond = bond + SIGMA_BOND * jnp.exp(-(distances[...] - LAYER_GAP) / DECAY_LENGTH) * square
    slot = lax.broadcasted_iota(jnp.int32, bond.shape, 0)
    hopping = jnp.where(slot < counts[...], bond, 0.0)
    steps = offsets[...].astype(F32)
    merged = jnp.zeros_like(hopping)
    for k in range(SLOTS):
        merged = merged + jnp.where(steps == steps[k : k + 1], hopping[k : k + 1], 0.0)
    sides = labels[...].astype(F32)
    onsite = SITE_MASS * (2.0 * sides[0:1] - 1.0) + LAYER_BIAS * (2.0 * sides[1:2] - 1.0)
    for core in range(CORES):
        out_ref[core, OWN : OWN + 16, :] = merged
        out_ref[core, OWN + 16 : OWN + 32, :] = steps
        out_ref[core, OWN + 32 : OWN + 40, :] = jnp.broadcast_to(onsite, (8, LOCAL))
    for copy in block_copies:
        copy.wait()


def sum_kernel(pieces_ref, out_ref):
    total = pieces_ref[0]
    for i in range(1, pieces_ref.shape[0]):
        total = total + pieces_ref[i]
    for i in range(out_ref.shape[0]):
        out_ref[i] = total


def build_matrix(table, high_ref, low_ref):
    hopping, offsets, onsite = table[0:16], table[16:32], table[32:33]
    lane = lax.broadcasted_iota(jnp.int32, (1, 128), 1).astype(F32)
    row_index = lax.broadcasted_iota(jnp.int32, (32, 128), 0).astype(F32)
    for half in range(2):
        columns = slice(128 * half, 128 * half + 128)
        empty = 640 * (1 - half)
        high_ref[empty : empty + 128, columns] = jnp.zeros((128, 128), BF16)
        low_ref[empty : empty + 128, columns] = jnp.zeros((128, 128), BF16)
        home = lane + float(REACH)
        targets = [
            jnp.broadcast_to(offsets[k : k + 1, columns] + home, (32, 128)) for k in range(SLOTS)
        ]
        values = [jnp.broadcast_to(hopping[k : k + 1, columns], (32, 128)) for k in range(SLOTS)]
        homes = jnp.broadcast_to(home, (32, 128))
        own = jnp.broadcast_to(onsite[:, columns], (32, 128))

        def chunk(step, carry):
            base = step * 32
            rows = row_index + base.astype(F32)
            total = jnp.where(homes == rows, own, 0.0)
            for k in range(SLOTS):
                total = jnp.where(targets[k] == rows, values[k], total)
            high = total.astype(BF16)
            low = (total - high.astype(F32)).astype(BF16)
            place = pl.ds(pl.multiple_of(base + 128 * half, 32), 32)
            high_ref[place, columns] = high
            low_ref[place, columns] = low
            return carry

        lax.fori_loop(0, 20, chunk, 0)


def own_matrix_kernel(slab_ref, *refs):
    for core in range(CORES):
        build_matrix(slab_ref[core, OWN:, :], refs[2 * core], refs[2 * core + 1])


def split(value):
    high = value.astype(BF16)
    return high, (value - high.astype(F32)).astype(BF16)


def dot3(high, low, matrix_high, matrix_low):
    def dot(left, right):
        return jnp.dot(left, right, preferred_element_type=F32)

    return dot(high, matrix_high) + (dot(high, matrix_low) + dot(low, matrix_high))


def apply_kernel(
    left_ref, own_ref, right_ref, first_high_ref, first_low_ref, second_high_ref, second_low_ref,
    applied_ref, lead_ref, high_ref, low_ref, once_high_ref, once_low_ref,
    left_high_ref, left_low_ref, right_high_ref, right_low_ref,
):
    build_matrix(left_ref[1, OWN:, :], left_high_ref, left_low_ref)
    build_matrix(right_ref[0, OWN:, :], right_high_ref, right_low_ref)
    sources = [(ref, core) for ref in (left_ref, own_ref, right_ref) for core in range(CORES)]
    for place, (ref, core) in enumerate(sources):
        columns = slice(LOCAL * place, LOCAL * place + LOCAL)
        high, low = split(ref[core, 0:OWN, :])
        high_ref[:, columns] = high
        low_ref[:, columns] = low
    matrices = (
        (left_high_ref, left_low_ref),
        (first_high_ref, first_low_ref),
        (second_high_ref, second_low_ref),
        (right_high_ref, right_low_ref),
    )
    for place, (matrix_high, matrix_low) in enumerate(matrices):
        window = slice(LOCAL * place, LOCAL * place + WIDE)
        columns = slice(LOCAL * place, LOCAL * place + LOCAL)
        once = dot3(high_ref[:, window], low_ref[:, window], matrix_high[...], matrix_low[...])
        high, low = split(once)
        once_high_ref[:, columns] = high
        once_low_ref[:, columns] = low
    for place, (matrix_high, matrix_low) in enumerate(matrices[1:3]):
        window = slice(LOCAL * place, LOCAL * place + WIDE)
        columns = slice(LOCAL * place, LOCAL * place + LOCAL)
        twice = dot3(
            once_high_ref[:, window], once_low_ref[:, window], matrix_high[...], matrix_low[...]
        )
        applied_ref[:, columns] = twice
        lead_ref[:, columns] = twice[0 : 2 * BLOCK]


def gram_kernel(core_ref, lead_ref, other_ref, applied_ref, gram_ref, head_ref):
    second = core_ref[0] == 1
    for s, place, core in ((0, 0, 0), (1, 0, 1), (2, BLOCK, 0)):
        mine, theirs = lead_ref[place : place + BLOCK, :], other_ref[place : place + BLOCK, :]
        pair = (mine, theirs) if core else (theirs, mine)
        head_ref[BLOCK * s : BLOCK * s + BLOCK, :] = jnp.where(second, *pair)
    gram = dot32(head_ref[...], applied_ref[...], ((1,), (1,)))
    for part in range(OWN // 128):
        gram_ref[part] = gram[:, 128 * part : 128 * part + 128]


def spread(value):
    return jnp.broadcast_to(value, (8, 128))


def inverse_factor(pair):
    rows = [pair[8 * i : 8 * i + 8] for i in range(BLOCK // 8)]
    sublane = lax.broadcasted_iota(jnp.int32, (8, 128), 0)
    for p in range(BLOCK // 8):
        start = BLOCK + 8 * p
        columns = [
            [spread(rows[i][:, start + b : start + b + 1]) for b in range(8)]
            for i in range(p, BLOCK // 8)
        ]
        for j in range(8):
            inverse = lax.rsqrt(spread(columns[0][j][j : j + 1]))
            pivot_row = spread(rows[p][j : j + 1]) * inverse
            heads = [spread(columns[0][b][j : j + 1]) * inverse for b in range(j + 1, 8)]
            for i in range(p, BLOCK // 8):
                factor = columns[i - p][j] * inverse
                if i == p:
                    factor = jnp.where(sublane > j, factor, 0.0)
                rows[i] = rows[i] - factor * pivot_row
                for b in range(j + 1, 8):
                    columns[i - p][b] = columns[i - p][b] - factor * heads[b - j - 1]
            rows[p] = jnp.where(sublane == j, pivot_row, rows[p])
    return jnp.concatenate(rows, axis=0)[:, 0:BLOCK]


def dot32(left, right, dims):
    return lax.dot_general(
        left, right, (dims, ((), ())), precision=HIGHEST, preferred_element_type=F32
    )


def finish_kernel(scale, core_ref, gram_ref, head_ref, applied_ref, basis_ref):
    second = core_ref[0] == 1
    tiles = gram_ref.shape[0] // 2

    def columns_of(part, core):
        return jnp.concatenate([gram_ref[part * tiles + m, core] for m in range(tiles)], axis=0)

    rest = jnp.where(second, columns_of(1, 1), columns_of(1, 0))
    full = jnp.concatenate([columns_of(0, 0), columns_of(0, 1), rest], axis=1) * scale
    gram = [full[BLOCK * s : BLOCK * s + BLOCK] for s in range(STEPS)]
    places = (0, 2 * BLOCK, BLOCK)
    lane = lax.broadcasted_iota(jnp.int32, (BLOCK, 128), 1)
    row = lax.broadcasted_iota(jnp.int32, (BLOCK, 128), 0)
    identity = jnp.where(lane == row, 1.0, 0.0).astype(F32)
    couplings = []
    inverses = []
    for s in range(STEPS):
        part = places[s] // 128
        tile = gram[s][:, 128 * part : 128 * part + 128]
        if places[s] % 128 == 0:
            tile = pltpu.roll(tile, BLOCK, axis=1)
        inverse = inverse_factor(jnp.where(lane < BLOCK, identity, tile))
        coupling = dot32(inverse, gram[s], ((1,), (0,)))
        for t in range(s + 1, STEPS):
            gram[t] = gram[t] - dot32(
                coupling[:, places[t] : places[t] + BLOCK], coupling, ((0,), (0,))
            )
        inverses.append(inverse)
        couplings.append(coupling)
    leaders = []
    for s in range(STEPS):
        block = head_ref[BLOCK * s : BLOCK * s + BLOCK, :]
        for t in range(s):
            block = block - dot32(
                couplings[t][:, places[s] : places[s] + BLOCK], leaders[t], ((0,), (0,))
            )
        leaders.append(dot32(inverses[s], block, ((1,), (0,))))
    stacked = jnp.concatenate([c[:, HEAD:] for c in couplings], axis=0)
    leading = jnp.concatenate(leaders, axis=0)
    later = applied_ref[BLOCK:, :] - dot32(stacked, leading, ((0,), (0,)))
    basis_ref[0:BLOCK, :] = jnp.where(second, leaders[1], leaders[0])
    basis_ref[BLOCK : 2 * BLOCK, :] = jnp.where(second, later[0:BLOCK], leaders[2])
    basis_ref[2 * BLOCK :, :] = later[BLOCK:]


def exchange(value, axes):
    return lax.all_to_all(value, axes, split_axis=0, concat_axis=0, tiled=True)


SMEM = pl.BlockSpec(memory_space=pltpu.SMEM)
RAW = pl.BlockSpec(memory_space=pl.ANY)


def call(kernel, name, out_shape, inputs, scratch=(), specs=None):
    single = not isinstance(out_shape, (tuple, list))
    return pl.pallas_call(
        kernel,
        out_shape=out_shape,
        in_specs=specs or [VMEM] * len(inputs),
        out_specs=VMEM if single else (VMEM,) * len(out_shape),
        scratch_shapes=list(scratch),
        compiler_params=PARAMS,
        name=name,
    )(*inputs)


def on_device(vectors, offsets, counts, labels, cosines, distances):
    chips = ("y", "z", "x")
    plane = ("y", "x")
    chip_count = lax.axis_size(chips)
    planes = lax.axis_size(plane)
    depth = lax.axis_size("z")

    def shift(value, step):
        return lax.ppermute(value, chips, [(i, (i + step) % chip_count) for i in range(chip_count)])

    shape = jax.ShapeDtypeStruct
    tables = (cosines, distances, offsets, counts.reshape(1, LOCAL), labels)
    slab = call(
        pack_kernel, "pack", shape((CORES, OWN + TABLE, LOCAL), F32), (vectors, *tables),
        [pltpu.VMEM(t.shape, t.dtype) for t in tables]
        + [pltpu.SemaphoreType.DMA((len(tables),)), pltpu.SemaphoreType.DMA((NV // BLOCK,))],
        [RAW] * 6,
    )
    slab = exchange(slab, "core")
    left = shift(slab, 1)
    right = shift(slab, -1)
    matrix = shape((WIDE, LOCAL), BF16)
    matrices = call(own_matrix_kernel, "own_matrix", (matrix,) * 4, (slab,))
    wide = pltpu.VMEM((WIDE, LOCAL), BF16)
    applied, lead = call(
        apply_kernel,
        "apply_twice",
        (shape((OWN, CHIP), F32), shape((2 * BLOCK, CHIP), F32)),
        (left, slab, right, *matrices),
        [pltpu.VMEM((OWN, 3 * CHIP), BF16)] * 2 + [pltpu.VMEM((OWN, 2 * CHIP), BF16)] * 2 + [wide] * 4,
    )
    other = lax.ppermute(lead, "core", [(0, 1), (1, 0)])
    core = lax.axis_index("core").reshape(1)
    gram, head = call(
        gram_kernel, "gram", (shape((OWN // 128, HEAD, 128), F32), shape((HEAD, CHIP), F32)),
        (core, lead, other, applied), (), [SMEM] + [VMEM] * 3,
    )
    piece = (OWN // 128) * HEAD // planes
    everyone = planes * CORES
    gram = exchange(gram.reshape(planes, piece, 128), plane)
    gram = exchange(call(sum_kernel, "sum_plane", shape((depth, piece, 128), F32), (gram,)), "z")
    gram = call(sum_kernel, "sum_depth", shape((everyone, piece, 128), F32), (gram,))
    gram = exchange(gram, (*plane, "core"))
    gram = gram.reshape(planes, CORES, piece, 128)
    scale = 1.0 / (CHIP * chip_count)
    basis = call(
        lambda *refs: finish_kernel(scale, *refs), "finish", shape((OWN, CHIP), F32),
        (core, gram, head, applied), (), [SMEM] + [VMEM] * 3,
    )
    return lax.all_to_all(basis, "x", split_axis=0, concat_axis=1, tiled=True)


def solution(mesh):
    rows = mesh.shape["rows"]
    cols = mesh.shape["cols"]
    names = ("y", "z", "x", "core")
    cube = Mesh(mesh.devices.reshape(Y_SIZE, rows // Y_SIZE, cols // CORES, CORES), names)
    whole = P(None, names)
    placed = (whole, whole, P(names), whole, whole, whole)
    return jax.shard_map(
        on_device, mesh=cube, in_specs=placed, out_specs=P(("x", "core"), ("y", "z")),
        check_vma=False,
    )
```

```python
import jax
import jax.numpy as jnp
from jax import lax
from jax.experimental import pallas as pl
from jax.experimental.pallas import tpu as pltpu
from jax.sharding import Mesh, PartitionSpec as P

PI_BOND = -1.0
SIGMA_BOND = 0.178
DECAY_LENGTH = 0.319
LAYER_GAP = 2.36
SITE_MASS = 0.4
LAYER_BIAS = 0.25

BLOCK = 64
STEPS = 3
HEAD = BLOCK * STEPS
SLOTS = 16
REACH = 256
NV = 512
LOCAL = 256
WIDE = LOCAL + 2 * REACH
Y_SIZE = 4
CORES = 2
OWN = NV // CORES
TABLE = 40
SHARED = HEAD + OWN - BLOCK
CHIP = CORES * LOCAL
F32 = jnp.float32
BF16 = jnp.bfloat16
HIGHEST = lax.Precision.HIGHEST
VMEM = pl.BlockSpec(memory_space=pltpu.VMEM)
PARAMS = pltpu.CompilerParams(vmem_limit_bytes=48 * 1024 * 1024)


def pack_kernel(
    vectors_ref, cosines_ref, distances_ref, offsets_ref, counts_ref, labels_ref, out_ref,
    cosines, distances, offsets, counts, labels, table_sems, block_sems,
):
    tables = (
        (cosines_ref, cosines), (distances_ref, distances), (offsets_ref, offsets),
        (counts_ref, counts), (labels_ref, labels),
    )
    table_copies = [
        pltpu.make_async_copy(source, target, table_sems.at[i])
        for i, (source, target) in enumerate(tables)
    ]
    block_copies = [
        pltpu.make_async_copy(
            vectors_ref.at[pl.ds(BLOCK * (core + CORES * p), BLOCK)],
            out_ref.at[core, pl.ds(BLOCK * p, BLOCK)],
            block_sems.at[core + CORES * p],
        )
        for core in range(CORES)
        for p in range(OWN // BLOCK)
    ]
    for copy in table_copies + block_copies:
        copy.start()
    for copy in table_copies:
        copy.wait()
    square = cosines[...] * cosines[...]
    bond = PI_BOND * jnp.exp(-(distances[...] - 1.0) / DECAY_LENGTH) * (1.0 - square)
    bond = bond + SIGMA_BOND * jnp.exp(-(distances[...] - LAYER_GAP) / DECAY_LENGTH) * square
    slot = lax.broadcasted_iota(jnp.int32, bond.shape, 0)
    hopping = jnp.where(slot < counts[...], bond, 0.0)
    steps = offsets[...].astype(F32)
    merged = jnp.zeros_like(hopping)
    for k in range(SLOTS):
        merged = merged + jnp.where(steps == steps[k : k + 1], hopping[k : k + 1], 0.0)
    sides = labels[...].astype(F32)
    onsite = SITE_MASS * (2.0 * sides[0:1] - 1.0) + LAYER_BIAS * (2.0 * sides[1:2] - 1.0)
    for core in range(CORES):
        out_ref[core, OWN : OWN + 16, :] = merged
        out_ref[core, OWN + 16 : OWN + 32, :] = steps
        out_ref[core, OWN + 32 : OWN + 40, :] = jnp.broadcast_to(onsite, (8, LOCAL))
    for copy in block_copies:
        copy.wait()


def sum_kernel(pieces_ref, out_ref):
    total = pieces_ref[0]
    for i in range(1, pieces_ref.shape[0]):
        total = total + pieces_ref[i]
    for i in range(out_ref.shape[0]):
        out_ref[i] = total


def build_matrix(table, high_ref, low_ref):
    hopping, offsets, onsite = table[0:16], table[16:32], table[32:33]
    lane = lax.broadcasted_iota(jnp.int32, (1, 128), 1).astype(F32)
    row_index = lax.broadcasted_iota(jnp.int32, (32, 128), 0).astype(F32)
    for half in range(2):
        columns = slice(128 * half, 128 * half + 128)
        empty = 640 * (1 - half)
        high_ref[empty : empty + 128, columns] = jnp.zeros((128, 128), BF16)
        low_ref[empty : empty + 128, columns] = jnp.zeros((128, 128), BF16)
        home = lane + float(REACH)
        targets = [
            jnp.broadcast_to(offsets[k : k + 1, columns] + home, (32, 128)) for k in range(SLOTS)
        ]
        values = [jnp.broadcast_to(hopping[k : k + 1, columns], (32, 128)) for k in range(SLOTS)]
        homes = jnp.broadcast_to(home, (32, 128))
        own = jnp.broadcast_to(onsite[:, columns], (32, 128))

        def chunk(step, carry):
            base = step * 32
            rows = row_index + base.astype(F32)
            total = jnp.where(homes == rows, own, 0.0)
            for k in range(SLOTS):
                total = jnp.where(targets[k] == rows, values[k], total)
            high = total.astype(BF16)
            low = (total - high.astype(F32)).astype(BF16)
            place = pl.ds(pl.multiple_of(base + 128 * half, 32), 32)
            high_ref[place, columns] = high
            low_ref[place, columns] = low
            return carry

        lax.fori_loop(0, 20, chunk, 0)


def own_matrix_kernel(slab_ref, *refs):
    for core in range(CORES):
        build_matrix(slab_ref[core, OWN:, :], refs[2 * core], refs[2 * core + 1])


def split(value):
    high = value.astype(BF16)
    return high, (value - high.astype(F32)).astype(BF16)


def dot3(high, low, matrix_high, matrix_low):
    def dot(left, right):
        return jnp.dot(left, right, preferred_element_type=F32)

    return dot(high, matrix_high) + (dot(high, matrix_low) + dot(low, matrix_high))


def apply_kernel(
    left_ref, own_ref, right_ref, first_high_ref, first_low_ref, second_high_ref, second_low_ref,
    applied_ref, lead_ref, high_ref, low_ref, once_high_ref, once_low_ref,
    left_high_ref, left_low_ref, right_high_ref, right_low_ref,
):
    build_matrix(left_ref[1, OWN:, :], left_high_ref, left_low_ref)
    build_matrix(right_ref[0, OWN:, :], right_high_ref, right_low_ref)
    sources = [(ref, core) for ref in (left_ref, own_ref, right_ref) for core in range(CORES)]
    for place, (ref, core) in enumerate(sources):
        columns = slice(LOCAL * place, LOCAL * place + LOCAL)
        high, low = split(ref[core, 0:OWN, :])
        high_ref[:, columns] = high
        low_ref[:, columns] = low
    matrices = (
        (left_high_ref, left_low_ref),
        (first_high_ref, first_low_ref),
        (second_high_ref, second_low_ref),
        (right_high_ref, right_low_ref),
    )
    for place, (matrix_high, matrix_low) in enumerate(matrices):
        window = slice(LOCAL * place, LOCAL * place + WIDE)
        columns = slice(LOCAL * place, LOCAL * place + LOCAL)
        once = dot3(high_ref[:, window], low_ref[:, window], matrix_high[...], matrix_low[...])
        high, low = split(once)
        once_high_ref[:, columns] = high
        once_low_ref[:, columns] = low
    for place, (matrix_high, matrix_low) in enumerate(matrices[1:3]):
        window = slice(LOCAL * place, LOCAL * place + WIDE)
        columns = slice(LOCAL * place, LOCAL * place + LOCAL)
        twice = dot3(
            once_high_ref[:, window], once_low_ref[:, window], matrix_high[...], matrix_low[...]
        )
        applied_ref[:, columns] = twice
        lead_ref[:, columns] = twice[0 : 2 * BLOCK]


def gram_kernel(core_ref, lead_ref, other_ref, applied_ref, gram_ref, shared_ref):
    second = core_ref[0] == 1
    for s, place, core in ((0, 0, 0), (1, 0, 1), (2, BLOCK, 0)):
        mine, theirs = lead_ref[place : place + BLOCK, :], other_ref[place : place + BLOCK, :]
        pair = (mine, theirs) if core else (theirs, mine)
        shared_ref[BLOCK * s : BLOCK * s + BLOCK, :] = jnp.where(second, *pair)
    shared_ref[HEAD:, :] = applied_ref[BLOCK:, :]
    gram = dot32(shared_ref[0:HEAD, :], applied_ref[...], ((1,), (1,)))
    for part in range(OWN // 128):
        gram_ref[part] = gram[:, 128 * part : 128 * part + 128]


def spread(value):
    return jnp.broadcast_to(value, (8, 128))


def inverse_factor(pair):
    rows = [pair[8 * i : 8 * i + 8] for i in range(BLOCK // 8)]
    sublane = lax.broadcasted_iota(jnp.int32, (8, 128), 0)
    for p in range(BLOCK // 8):
        start = BLOCK + 8 * p
        columns = [
            [spread(rows[i][:, start + b : start + b + 1]) for b in range(8)]
            for i in range(p, BLOCK // 8)
        ]
        for j in range(8):
            inverse = lax.rsqrt(spread(columns[0][j][j : j + 1]))
            pivot_row = spread(rows[p][j : j + 1]) * inverse
            heads = [spread(columns[0][b][j : j + 1]) * inverse for b in range(j + 1, 8)]
            for i in range(p, BLOCK // 8):
                factor = columns[i - p][j] * inverse
                if i == p:
                    factor = jnp.where(sublane > j, factor, 0.0)
                rows[i] = rows[i] - factor * pivot_row
                for b in range(j + 1, 8):
                    columns[i - p][b] = columns[i - p][b] - factor * heads[b - j - 1]
            rows[p] = jnp.where(sublane == j, pivot_row, rows[p])
    return jnp.concatenate(rows, axis=0)[:, 0:BLOCK]


def dot32(left, right, dims):
    return lax.dot_general(
        left, right, (dims, ((), ())), precision=HIGHEST, preferred_element_type=F32
    )


def finish_kernel(scale, place_ref, gram_ref, shared_ref, basis_ref, heads, later, results, sems):
    chip, core = place_ref[0], place_ref[1]
    second = core == 1
    column = CORES * chip + core
    count = shared_ref.shape[0]
    start = pl.multiple_of(HEAD + BLOCK * jnp.maximum(chip - 1, 0), BLOCK)
    copies = []
    for q in range(count):
        copies.append(
            pltpu.make_async_copy(
                shared_ref.at[q, pl.ds(0, HEAD)], heads.at[:, pl.ds(CHIP * q, CHIP)], sems.at[q]
            )
        )
        copies.append(
            pltpu.make_async_copy(
                shared_ref.at[q, pl.ds(start, BLOCK)],
                later.at[:, pl.ds(CHIP * q, CHIP)],
                sems.at[count + q],
            )
        )
    for copy in copies:
        copy.start()
    tiles = gram_ref.shape[0] // 2

    def columns_of(part, core):
        return jnp.concatenate([gram_ref[part * tiles + m, core] for m in range(tiles)], axis=0)

    first_pair, second_pair = columns_of(0, 0), columns_of(0, 1)
    low = jnp.where(second, second_pair, first_pair)
    high = jnp.where(second, columns_of(1, 1), columns_of(1, 0))
    mine = jnp.where(chip >= 2, high, low)
    mine = jnp.where(chip % 2 == 1, pltpu.roll(mine, BLOCK, axis=1), mine)
    full = jnp.concatenate([first_pair, second_pair, mine], axis=1) * scale
    gram = [full[BLOCK * s : BLOCK * s + BLOCK] for s in range(STEPS)]
    places = (0, 2 * BLOCK, BLOCK)
    lane = lax.broadcasted_iota(jnp.int32, (BLOCK, 128), 1)
    row = lax.broadcasted_iota(jnp.int32, (BLOCK, 128), 0)
    identity = jnp.where(lane == row, 1.0, 0.0).astype(F32)
    couplings = []
    inverses = []
    for s in range(STEPS):
        part = places[s] // 128
        tile = gram[s][:, 128 * part : 128 * part + 128]
        if places[s] % 128 == 0:
            tile = pltpu.roll(tile, BLOCK, axis=1)
        inverse = inverse_factor(jnp.where(lane < BLOCK, identity, tile))
        coupling = dot32(inverse, gram[s], ((1,), (0,)))
        for t in range(s + 1, STEPS):
            gram[t] = gram[t] - dot32(
                coupling[:, places[t] : places[t] + BLOCK], coupling, ((0,), (0,))
            )
        inverses.append(inverse)
        couplings.append(coupling)
    follows = column >= STEPS
    weights = [None] * STEPS
    for s in reversed(range(STEPS)):
        leads = jnp.where(column == s, identity[:, 0:BLOCK], 0.0)
        weight = jnp.where(follows, -couplings[s][:, 4 * BLOCK : 5 * BLOCK], leads)
        for t in range(s + 1, STEPS):
            weight = weight - dot32(
                couplings[s][:, places[t] : places[t] + BLOCK], weights[t], ((1,), (0,))
            )
        weights[s] = dot32(inverses[s], weight, ((0,), (0,)))
    weight_high, weight_low = split(jnp.concatenate(weights, axis=0).T)
    outs = []
    for q in range(count):
        columns = slice(CHIP * q, CHIP * q + CHIP)
        copies[2 * q].wait()
        copies[2 * q + 1].wait()
        head_high, head_low = split(heads[:, columns])
        result = jnp.where(follows, later[:, columns], 0.0)
        results[:, columns] = result + dot3(weight_high, weight_low, head_high, head_low)
        out = pltpu.make_async_copy(
            results.at[:, pl.ds(CHIP * q, CHIP)],
            basis_ref.at[:, pl.ds(CHIP * q, CHIP)],
            sems.at[2 * count + q],
        )
        out.start()
        outs.append(out)
    for out in outs:
        out.wait()


def exchange(value, axes):
    return lax.all_to_all(value, axes, split_axis=0, concat_axis=0, tiled=True)


SMEM = pl.BlockSpec(memory_space=pltpu.SMEM)
RAW = pl.BlockSpec(memory_space=pltpu.HBM)


def call(kernel, name, out_shape, inputs, scratch=(), specs=None, out_specs=None):
    single = not isinstance(out_shape, (tuple, list))
    if specs:
        inputs = [
            pltpu.with_memory_space_constraint(value, pltpu.HBM) if spec is RAW else value
            for value, spec in zip(inputs, specs)
        ]
    return pl.pallas_call(
        kernel,
        out_shape=out_shape,
        in_specs=specs or [VMEM] * len(inputs),
        out_specs=out_specs or VMEM if single else (VMEM,) * len(out_shape),
        scratch_shapes=list(scratch),
        compiler_params=PARAMS,
        name=name,
    )(*inputs)


def on_device(vectors, offsets, counts, labels, cosines, distances):
    chips = ("y", "z", "x")
    plane = ("y", "x")
    chip_count = lax.axis_size(chips)
    planes = lax.axis_size(plane)
    depth = lax.axis_size("z")

    def shift(value, step):
        return lax.ppermute(value, chips, [(i, (i + step) % chip_count) for i in range(chip_count)])

    shape = jax.ShapeDtypeStruct
    tables = (cosines, distances, offsets, counts.reshape(1, LOCAL), labels)
    slab = call(
        pack_kernel, "pack", shape((CORES, OWN + TABLE, LOCAL), F32), (vectors, *tables),
        [pltpu.VMEM(t.shape, t.dtype) for t in tables]
        + [pltpu.SemaphoreType.DMA((len(tables),)), pltpu.SemaphoreType.DMA((NV // BLOCK,))],
        [RAW] * 6,
    )
    slab = exchange(slab, "core")
    left = shift(slab, 1)
    right = shift(slab, -1)
    matrix = shape((WIDE, LOCAL), BF16)
    matrices = call(own_matrix_kernel, "own_matrix", (matrix,) * 4, (slab,))
    wide = pltpu.VMEM((WIDE, LOCAL), BF16)
    applied, lead = call(
        apply_kernel,
        "apply_twice",
        (shape((OWN, CHIP), F32), shape((2 * BLOCK, CHIP), F32)),
        (left, slab, right, *matrices),
        [pltpu.VMEM((OWN, 3 * CHIP), BF16)] * 2 + [pltpu.VMEM((OWN, 2 * CHIP), BF16)] * 2 + [wide] * 4,
    )
    other = lax.ppermute(lead, "core", [(0, 1), (1, 0)])
    core = lax.axis_index("core").reshape(1)
    gram, shared = call(
        gram_kernel, "gram", (shape((OWN // 128, HEAD, 128), F32), shape((SHARED, CHIP), F32)),
        (core, lead, other, applied), (), [SMEM] + [VMEM] * 3,
    )
    shared = lax.all_gather(shared, "x")
    piece = (OWN // 128) * HEAD // planes
    everyone = planes * CORES
    gram = exchange(gram.reshape(planes, piece, 128), plane)
    gram = exchange(call(sum_kernel, "sum_plane", shape((depth, piece, 128), F32), (gram,)), "z")
    gram = call(sum_kernel, "sum_depth", shape((everyone, piece, 128), F32), (gram,))
    gram = exchange(gram, (*plane, "core"))
    gram = gram.reshape(planes, CORES, piece, 128)
    scale = 1.0 / (CHIP * chip_count)
    count = lax.axis_size("x")
    slab_width = CHIP * count
    place = jnp.stack([lax.axis_index("x"), lax.axis_index("core")])
    return call(
        lambda *refs: finish_kernel(scale, *refs), "finish", shape((BLOCK, slab_width), F32),
        (place, gram, shared),
        [pltpu.VMEM((HEAD, slab_width), F32)] + [pltpu.VMEM((BLOCK, slab_width), F32)] * 2
        + [pltpu.SemaphoreType.DMA((3 * count,))],
        [SMEM, VMEM, RAW], RAW,
    )


def solution(mesh):
    rows = mesh.shape["rows"]
    cols = mesh.shape["cols"]
    names = ("y", "z", "x", "core")
    cube = Mesh(mesh.devices.reshape(Y_SIZE, rows // Y_SIZE, cols // CORES, CORES), names)
    whole = P(None, names)
    placed = (whole, whole, P(names), whole, whole, whole)
    return jax.shard_map(
        on_device, mesh=cube, in_specs=placed, out_specs=P(("x", "core"), ("y", "z")),
        check_vma=False,
    )
```

```python
import jax
import jax.numpy as jnp
from jax import lax
from jax.experimental import pallas as pl
from jax.experimental.pallas import tpu as pltpu
from jax.sharding import Mesh, PartitionSpec as P

PI_BOND = -1.0
SIGMA_BOND = 0.178
DECAY_LENGTH = 0.319
LAYER_GAP = 2.36
SITE_MASS = 0.4
LAYER_BIAS = 0.25

BLOCK = 64
STEPS = 3
HEAD = BLOCK * STEPS
SLOTS = 16
REACH = 256
NV = 512
LOCAL = 256
WIDE = LOCAL + 2 * REACH
Y_SIZE = 4
CORES = 2
OWN = NV // CORES
TABLE = 40
SHARED = HEAD + BLOCK
CHIP = CORES * LOCAL
F32 = jnp.float32
BF16 = jnp.bfloat16
HIGHEST = lax.Precision.HIGHEST
VMEM = pl.BlockSpec(memory_space=pltpu.VMEM)
PARAMS = pltpu.CompilerParams(vmem_limit_bytes=48 * 1024 * 1024)


def pack_kernel(
    vectors_ref, cosines_ref, distances_ref, offsets_ref, counts_ref, labels_ref, out_ref,
    cosines, distances, offsets, counts, labels, table_sems, block_sems,
):
    tables = (
        (cosines_ref, cosines), (distances_ref, distances), (offsets_ref, offsets),
        (counts_ref, counts), (labels_ref, labels),
    )
    table_copies = [
        pltpu.make_async_copy(source, target, table_sems.at[i])
        for i, (source, target) in enumerate(tables)
    ]
    block_copies = [
        pltpu.make_async_copy(
            vectors_ref.at[pl.ds(BLOCK * (core + CORES * p), BLOCK)],
            out_ref.at[core, pl.ds(BLOCK * p, BLOCK)],
            block_sems.at[core + CORES * p],
        )
        for core in range(CORES)
        for p in range(OWN // BLOCK)
    ]
    for copy in table_copies + block_copies:
        copy.start()
    for copy in table_copies:
        copy.wait()
    square = cosines[...] * cosines[...]
    bond = PI_BOND * jnp.exp(-(distances[...] - 1.0) / DECAY_LENGTH) * (1.0 - square)
    bond = bond + SIGMA_BOND * jnp.exp(-(distances[...] - LAYER_GAP) / DECAY_LENGTH) * square
    slot = lax.broadcasted_iota(jnp.int32, bond.shape, 0)
    hopping = jnp.where(slot < counts[...], bond, 0.0)
    steps = offsets[...].astype(F32)
    merged = jnp.zeros_like(hopping)
    for k in range(SLOTS):
        merged = merged + jnp.where(steps == steps[k : k + 1], hopping[k : k + 1], 0.0)
    sides = labels[...].astype(F32)
    onsite = SITE_MASS * (2.0 * sides[0:1] - 1.0) + LAYER_BIAS * (2.0 * sides[1:2] - 1.0)
    for core in range(CORES):
        out_ref[core, OWN : OWN + 16, :] = merged
        out_ref[core, OWN + 16 : OWN + 32, :] = steps
        out_ref[core, OWN + 32 : OWN + 40, :] = jnp.broadcast_to(onsite, (8, LOCAL))
    for copy in block_copies:
        copy.wait()


def sum_kernel(pieces_ref, out_ref):
    total = pieces_ref[0]
    for i in range(1, pieces_ref.shape[0]):
        total = total + pieces_ref[i]
    for i in range(out_ref.shape[0]):
        out_ref[i] = total


def build_matrix(table, high_ref, low_ref):
    hopping, offsets, onsite = table[0:16], table[16:32], table[32:33]
    lane = lax.broadcasted_iota(jnp.int32, (1, 128), 1).astype(F32)
    row_index = lax.broadcasted_iota(jnp.int32, (32, 128), 0).astype(F32)
    for half in range(2):
        columns = slice(128 * half, 128 * half + 128)
        empty = 640 * (1 - half)
        high_ref[empty : empty + 128, columns] = jnp.zeros((128, 128), BF16)
        low_ref[empty : empty + 128, columns] = jnp.zeros((128, 128), BF16)
        home = lane + float(REACH)
        targets = [
            jnp.broadcast_to(offsets[k : k + 1, columns] + home, (32, 128)) for k in range(SLOTS)
        ]
        values = [jnp.broadcast_to(hopping[k : k + 1, columns], (32, 128)) for k in range(SLOTS)]
        homes = jnp.broadcast_to(home, (32, 128))
        own = jnp.broadcast_to(onsite[:, columns], (32, 128))

        def chunk(step, carry):
            base = step * 32
            rows = row_index + base.astype(F32)
            total = jnp.where(homes == rows, own, 0.0)
            for k in range(SLOTS):
                total = jnp.where(targets[k] == rows, values[k], total)
            high = total.astype(BF16)
            low = (total - high.astype(F32)).astype(BF16)
            place = pl.ds(pl.multiple_of(base + 128 * half, 32), 32)
            high_ref[place, columns] = high
            low_ref[place, columns] = low
            return carry

        lax.fori_loop(0, 20, chunk, 0)


def own_matrix_kernel(slab_ref, *refs):
    for core in range(CORES):
        build_matrix(slab_ref[core, OWN:, :], refs[2 * core], refs[2 * core + 1])


def split(value):
    high = value.astype(BF16)
    return high, (value - high.astype(F32)).astype(BF16)


def dot3(high, low, matrix_high, matrix_low):
    def dot(left, right):
        return jnp.dot(left, right, preferred_element_type=F32)

    return dot(high, matrix_high) + (dot(high, matrix_low) + dot(low, matrix_high))


def apply_kernel(
    left_ref, own_ref, right_ref, first_high_ref, first_low_ref, second_high_ref, second_low_ref,
    applied_ref, lead_ref, high_ref, low_ref, once_high_ref, once_low_ref,
    left_high_ref, left_low_ref, right_high_ref, right_low_ref,
):
    build_matrix(left_ref[1, OWN:, :], left_high_ref, left_low_ref)
    build_matrix(right_ref[0, OWN:, :], right_high_ref, right_low_ref)
    sources = [(ref, core) for ref in (left_ref, own_ref, right_ref) for core in range(CORES)]
    for place, (ref, core) in enumerate(sources):
        columns = slice(LOCAL * place, LOCAL * place + LOCAL)
        high, low = split(ref[core, 0:OWN, :])
        high_ref[:, columns] = high
        low_ref[:, columns] = low
    matrices = (
        (left_high_ref, left_low_ref),
        (first_high_ref, first_low_ref),
        (second_high_ref, second_low_ref),
        (right_high_ref, right_low_ref),
    )
    for place, (matrix_high, matrix_low) in enumerate(matrices):
        window = slice(LOCAL * place, LOCAL * place + WIDE)
        columns = slice(LOCAL * place, LOCAL * place + LOCAL)
        once = dot3(high_ref[:, window], low_ref[:, window], matrix_high[...], matrix_low[...])
        high, low = split(once)
        once_high_ref[:, columns] = high
        once_low_ref[:, columns] = low
    for place, (matrix_high, matrix_low) in enumerate(matrices[1:3]):
        window = slice(LOCAL * place, LOCAL * place + WIDE)
        columns = slice(LOCAL * place, LOCAL * place + LOCAL)
        twice = dot3(
            once_high_ref[:, window], once_low_ref[:, window], matrix_high[...], matrix_low[...]
        )
        applied_ref[:, columns] = twice
        lead_ref[:, columns] = twice[0 : 2 * BLOCK]


def gram_kernel(core_ref, lead_ref, other_ref, applied_ref, gram_ref, shared_ref):
    second = core_ref[0] == 1
    count = shared_ref.shape[0]
    for s, place, core in ((0, 0, 0), (1, 0, 1), (2, BLOCK, 0)):
        mine, theirs = lead_ref[place : place + BLOCK, :], other_ref[place : place + BLOCK, :]
        pair = (mine, theirs) if core else (theirs, mine)
        block = jnp.where(second, *pair)
        for q in range(count):
            shared_ref[q, BLOCK * s : BLOCK * s + BLOCK, :] = block
    for q in range(count):
        shared_ref[q, HEAD:, :] = applied_ref[BLOCK * q : BLOCK * q + BLOCK, :]
    gram = dot32(shared_ref[0, 0:HEAD, :], applied_ref[...], ((1,), (1,)))
    for part in range(OWN // 128):
        gram_ref[part] = gram[:, 128 * part : 128 * part + 128]


def spread(value):
    return jnp.broadcast_to(value, (8, 128))


def inverse_factor(pair):
    rows = [pair[8 * i : 8 * i + 8] for i in range(BLOCK // 8)]
    sublane = lax.broadcasted_iota(jnp.int32, (8, 128), 0)
    for p in range(BLOCK // 8):
        start = BLOCK + 8 * p
        columns = [
            [spread(rows[i][:, start + b : start + b + 1]) for b in range(8)]
            for i in range(p, BLOCK // 8)
        ]
        for j in range(8):
            inverse = lax.rsqrt(spread(columns[0][j][j : j + 1]))
            pivot_row = spread(rows[p][j : j + 1]) * inverse
            heads = [spread(columns[0][b][j : j + 1]) * inverse for b in range(j + 1, 8)]
            for i in range(p, BLOCK // 8):
                factor = columns[i - p][j] * inverse
                if i == p:
                    factor = jnp.where(sublane > j, factor, 0.0)
                rows[i] = rows[i] - factor * pivot_row
                for b in range(j + 1, 8):
                    columns[i - p][b] = columns[i - p][b] - factor * heads[b - j - 1]
            rows[p] = jnp.where(sublane == j, pivot_row, rows[p])
    return jnp.concatenate(rows, axis=0)[:, 0:BLOCK]


def dot32(left, right, dims):
    return lax.dot_general(
        left, right, (dims, ((), ())), precision=HIGHEST, preferred_element_type=F32
    )


def finish_kernel(scale, place_ref, gram_ref, shared_ref, basis_ref, results, sems):
    chip, core = place_ref[0], place_ref[1]
    second = core == 1
    column = CORES * chip + core
    count = shared_ref.shape[0]
    tiles = gram_ref.shape[0] // 2

    def columns_of(part, core):
        return jnp.concatenate([gram_ref[part * tiles + m, core] for m in range(tiles)], axis=0)

    first_pair, second_pair = columns_of(0, 0), columns_of(0, 1)
    low = jnp.where(second, second_pair, first_pair)
    high = jnp.where(second, columns_of(1, 1), columns_of(1, 0))
    mine = jnp.where(chip >= 2, high, low)
    mine = jnp.where(chip % 2 == 1, pltpu.roll(mine, BLOCK, axis=1), mine)
    full = jnp.concatenate([first_pair, second_pair, mine], axis=1) * scale
    gram = [full[BLOCK * s : BLOCK * s + BLOCK] for s in range(STEPS)]
    places = (0, 2 * BLOCK, BLOCK)
    lane = lax.broadcasted_iota(jnp.int32, (BLOCK, 128), 1)
    row = lax.broadcasted_iota(jnp.int32, (BLOCK, 128), 0)
    identity = jnp.where(lane == row, 1.0, 0.0).astype(F32)
    couplings = []
    inverses = []
    for s in range(STEPS):
        part = places[s] // 128
        tile = gram[s][:, 128 * part : 128 * part + 128]
        if places[s] % 128 == 0:
            tile = pltpu.roll(tile, BLOCK, axis=1)
        inverse = inverse_factor(jnp.where(lane < BLOCK, identity, tile))
        coupling = dot32(inverse, gram[s], ((1,), (0,)))
        for t in range(s + 1, STEPS):
            gram[t] = gram[t] - dot32(
                coupling[:, places[t] : places[t] + BLOCK], coupling, ((0,), (0,))
            )
        inverses.append(inverse)
        couplings.append(coupling)
    follows = column >= STEPS
    weights = [None] * STEPS
    for s in reversed(range(STEPS)):
        leads = jnp.where(column == s, identity[:, 0:BLOCK], 0.0)
        weight = jnp.where(follows, -couplings[s][:, 4 * BLOCK : 5 * BLOCK], leads)
        for t in range(s + 1, STEPS):
            weight = weight - dot32(
                couplings[s][:, places[t] : places[t] + BLOCK], weights[t], ((1,), (0,))
            )
        weights[s] = dot32(inverses[s], weight, ((0,), (0,)))
    weight_high, weight_low = split(jnp.concatenate(weights, axis=0).T)
    outs = []
    for q in range(count):
        columns = slice(CHIP * q, CHIP * q + CHIP)
        head_high, head_low = split(shared_ref[q, 0:HEAD, :])
        result = jnp.where(follows, shared_ref[q, HEAD:, :], 0.0)
        results[:, columns] = result + dot3(weight_high, weight_low, head_high, head_low)
        out = pltpu.make_async_copy(
            results.at[:, pl.ds(CHIP * q, CHIP)],
            basis_ref.at[:, pl.ds(CHIP * q, CHIP)],
            sems.at[q],
        )
        out.start()
        outs.append(out)
    for out in outs:
        out.wait()


def exchange(value, axes):
    return lax.all_to_all(value, axes, split_axis=0, concat_axis=0, tiled=True)


SMEM = pl.BlockSpec(memory_space=pltpu.SMEM)
RAW = pl.BlockSpec(memory_space=pltpu.HBM)


def call(kernel, name, out_shape, inputs, scratch=(), specs=None, out_specs=None):
    single = not isinstance(out_shape, (tuple, list))
    if specs:
        inputs = [
            pltpu.with_memory_space_constraint(value, pltpu.HBM) if spec is RAW else value
            for value, spec in zip(inputs, specs)
        ]
    return pl.pallas_call(
        kernel,
        out_shape=out_shape,
        in_specs=specs or [VMEM] * len(inputs),
        out_specs=out_specs or VMEM if single else (VMEM,) * len(out_shape),
        scratch_shapes=list(scratch),
        compiler_params=PARAMS,
        name=name,
    )(*inputs)


def on_device(vectors, offsets, counts, labels, cosines, distances):
    chips = ("y", "z", "x")
    plane = ("y", "x")
    chip_count = lax.axis_size(chips)
    planes = lax.axis_size(plane)
    depth = lax.axis_size("z")
    count = lax.axis_size("x")

    def shift(value, step):
        return lax.ppermute(value, chips, [(i, (i + step) % chip_count) for i in range(chip_count)])

    shape = jax.ShapeDtypeStruct
    tables = (cosines, distances, offsets, counts.reshape(1, LOCAL), labels)
    slab = call(
        pack_kernel, "pack", shape((CORES, OWN + TABLE, LOCAL), F32), (vectors, *tables),
        [pltpu.VMEM(t.shape, t.dtype) for t in tables]
        + [pltpu.SemaphoreType.DMA((len(tables),)), pltpu.SemaphoreType.DMA((NV // BLOCK,))],
        [RAW] * 6,
    )
    slab = exchange(slab, "core")
    left = shift(slab, 1)
    right = shift(slab, -1)
    matrix = shape((WIDE, LOCAL), BF16)
    matrices = call(own_matrix_kernel, "own_matrix", (matrix,) * 4, (slab,))
    wide = pltpu.VMEM((WIDE, LOCAL), BF16)
    applied, lead = call(
        apply_kernel,
        "apply_twice",
        (shape((OWN, CHIP), F32), shape((2 * BLOCK, CHIP), F32)),
        (left, slab, right, *matrices),
        [pltpu.VMEM((OWN, 3 * CHIP), BF16)] * 2 + [pltpu.VMEM((OWN, 2 * CHIP), BF16)] * 2 + [wide] * 4,
    )
    other = lax.ppermute(lead, "core", [(0, 1), (1, 0)])
    core = lax.axis_index("core").reshape(1)
    gram, shared = call(
        gram_kernel, "gram", (shape((OWN // 128, HEAD, 128), F32), shape((count, SHARED, CHIP), F32)),
        (core, lead, other, applied), (), [SMEM] + [VMEM] * 3,
    )
    piece = (OWN // 128) * HEAD // planes
    everyone = planes * CORES
    gram = exchange(gram.reshape(planes, piece, 128), plane)
    gram = call(sum_kernel, "sum_plane", shape((depth, piece, 128), F32), (gram,))
    gram, shared = lax.optimization_barrier((gram, shared))
    shared = exchange(shared, "x")
    gram = exchange(gram, "z")
    gram = call(sum_kernel, "sum_depth", shape((everyone, piece, 128), F32), (gram,))
    gram = exchange(gram, (*plane, "core"))
    gram = gram.reshape(planes, CORES, piece, 128)
    scale = 1.0 / (CHIP * chip_count)
    slab_width = CHIP * count
    place = jnp.stack([lax.axis_index("x"), lax.axis_index("core")])
    return call(
        lambda *refs: finish_kernel(scale, *refs), "finish", shape((BLOCK, slab_width), F32),
        (place, gram, shared),
        [pltpu.VMEM((BLOCK, slab_width), F32), pltpu.SemaphoreType.DMA((count,))],
        [SMEM, VMEM, VMEM], RAW,
    )


def solution(mesh):
    rows = mesh.shape["rows"]
    cols = mesh.shape["cols"]
    names = ("y", "z", "x", "core")
    cube = Mesh(mesh.devices.reshape(Y_SIZE, rows // Y_SIZE, cols // CORES, CORES), names)
    whole = P(None, names)
    placed = (whole, whole, P(names), whole, whole, whole)
    return jax.shard_map(
        on_device, mesh=cube, in_specs=placed, out_specs=P(("x", "core"), ("y", "z")),
        check_vma=False,
    )
```

```python
import jax
import jax.numpy as jnp
from jax import lax
from jax.experimental import pallas as pl
from jax.experimental.pallas import tpu as pltpu
from jax.sharding import Mesh, PartitionSpec as P

PI_BOND = -1.0
SIGMA_BOND = 0.178
DECAY_LENGTH = 0.319
LAYER_GAP = 2.36
SITE_MASS = 0.4
LAYER_BIAS = 0.25

BLOCK = 64
STEPS = 3
HEAD = BLOCK * STEPS
SLOTS = 16
REACH = 256
NV = 512
LOCAL = 256
WIDE = LOCAL + 2 * REACH
Y_SIZE = 4
CORES = 2
OWN = NV // CORES
TABLE = 40
SHARED = HEAD + BLOCK
CHIP = CORES * LOCAL
F32 = jnp.float32
BF16 = jnp.bfloat16
HIGHEST = lax.Precision.HIGHEST
VMEM = pl.BlockSpec(memory_space=pltpu.VMEM)
PARAMS = pltpu.CompilerParams(vmem_limit_bytes=48 * 1024 * 1024)


def pack_kernel(
    vectors_ref, cosines_ref, distances_ref, offsets_ref, counts_ref, labels_ref, out_ref,
    cosines, distances, offsets, counts, labels, table_sems, block_sems,
):
    tables = (
        (cosines_ref, cosines), (distances_ref, distances), (offsets_ref, offsets),
        (counts_ref, counts), (labels_ref, labels),
    )
    table_copies = [
        pltpu.make_async_copy(source, target, table_sems.at[i])
        for i, (source, target) in enumerate(tables)
    ]
    block_copies = [
        pltpu.make_async_copy(
            vectors_ref.at[pl.ds(BLOCK * (core + CORES * p), BLOCK)],
            out_ref.at[core, pl.ds(BLOCK * p, BLOCK)],
            block_sems.at[core + CORES * p],
        )
        for core in range(CORES)
        for p in range(OWN // BLOCK)
    ]
    for copy in table_copies + block_copies:
        copy.start()
    for copy in table_copies:
        copy.wait()
    square = cosines[...] * cosines[...]
    bond = PI_BOND * jnp.exp(-(distances[...] - 1.0) / DECAY_LENGTH) * (1.0 - square)
    bond = bond + SIGMA_BOND * jnp.exp(-(distances[...] - LAYER_GAP) / DECAY_LENGTH) * square
    slot = lax.broadcasted_iota(jnp.int32, bond.shape, 0)
    hopping = jnp.where(slot < counts[...], bond, 0.0)
    steps = offsets[...].astype(F32)
    merged = jnp.zeros_like(hopping)
    for k in range(SLOTS):
        merged = merged + jnp.where(steps == steps[k : k + 1], hopping[k : k + 1], 0.0)
    sides = labels[...].astype(F32)
    onsite = SITE_MASS * (2.0 * sides[0:1] - 1.0) + LAYER_BIAS * (2.0 * sides[1:2] - 1.0)
    for core in range(CORES):
        out_ref[core, OWN : OWN + 16, :] = merged
        out_ref[core, OWN + 16 : OWN + 32, :] = steps
        out_ref[core, OWN + 32 : OWN + 40, :] = jnp.broadcast_to(onsite, (8, LOCAL))
    for copy in block_copies:
        copy.wait()


def sum_kernel(pieces_ref, out_ref):
    total = pieces_ref[0]
    for i in range(1, pieces_ref.shape[0]):
        total = total + pieces_ref[i]
    for i in range(out_ref.shape[0]):
        out_ref[i] = total


def build_matrix(table, high_ref, low_ref):
    hopping, offsets, onsite = table[0:16], table[16:32], table[32:33]
    lane = lax.broadcasted_iota(jnp.int32, (1, 128), 1).astype(F32)
    row_index = lax.broadcasted_iota(jnp.int32, (32, 128), 0).astype(F32)
    for half in range(2):
        columns = slice(128 * half, 128 * half + 128)
        empty = 640 * (1 - half)
        high_ref[empty : empty + 128, columns] = jnp.zeros((128, 128), BF16)
        low_ref[empty : empty + 128, columns] = jnp.zeros((128, 128), BF16)
        home = lane + float(REACH)
        targets = [
            jnp.broadcast_to(offsets[k : k + 1, columns] + home, (32, 128)) for k in range(SLOTS)
        ]
        values = [jnp.broadcast_to(hopping[k : k + 1, columns], (32, 128)) for k in range(SLOTS)]
        homes = jnp.broadcast_to(home, (32, 128))
        own = jnp.broadcast_to(onsite[:, columns], (32, 128))

        def chunk(step, carry):
            base = step * 32
            rows = row_index + base.astype(F32)
            total = jnp.where(homes == rows, own, 0.0)
            for k in range(SLOTS):
                total = jnp.where(targets[k] == rows, values[k], total)
            high = total.astype(BF16)
            low = (total - high.astype(F32)).astype(BF16)
            place = pl.ds(pl.multiple_of(base + 128 * half, 32), 32)
            high_ref[place, columns] = high
            low_ref[place, columns] = low
            return carry

        lax.fori_loop(0, 20, chunk, 0)


def own_matrix_kernel(slab_ref, *refs):
    for core in range(CORES):
        build_matrix(slab_ref[core, OWN:, :], refs[2 * core], refs[2 * core + 1])


def split(value):
    high = value.astype(BF16)
    return high, (value - high.astype(F32)).astype(BF16)


def dot3(high, low, matrix_high, matrix_low):
    def dot(left, right):
        return jnp.dot(left, right, preferred_element_type=F32)

    return dot(high, matrix_high) + (dot(high, matrix_low) + dot(low, matrix_high))


def apply_kernel(
    left_ref, own_ref, right_ref, first_high_ref, first_low_ref, second_high_ref, second_low_ref,
    applied_ref, lead_ref, high_ref, low_ref, once_high_ref, once_low_ref,
    left_high_ref, left_low_ref, right_high_ref, right_low_ref,
):
    build_matrix(left_ref[1, OWN:, :], left_high_ref, left_low_ref)
    build_matrix(right_ref[0, OWN:, :], right_high_ref, right_low_ref)
    sources = [(ref, core) for ref in (left_ref, own_ref, right_ref) for core in range(CORES)]
    for place, (ref, core) in enumerate(sources):
        columns = slice(LOCAL * place, LOCAL * place + LOCAL)
        high, low = split(ref[core, 0:OWN, :])
        high_ref[:, columns] = high
        low_ref[:, columns] = low
    matrices = (
        (left_high_ref, left_low_ref),
        (first_high_ref, first_low_ref),
        (second_high_ref, second_low_ref),
        (right_high_ref, right_low_ref),
    )
    for place, (matrix_high, matrix_low) in enumerate(matrices):
        window = slice(LOCAL * place, LOCAL * place + WIDE)
        columns = slice(LOCAL * place, LOCAL * place + LOCAL)
        once = dot3(high_ref[:, window], low_ref[:, window], matrix_high[...], matrix_low[...])
        high, low = split(once)
        once_high_ref[:, columns] = high
        once_low_ref[:, columns] = low
    for place, (matrix_high, matrix_low) in enumerate(matrices[1:3]):
        window = slice(LOCAL * place, LOCAL * place + WIDE)
        columns = slice(LOCAL * place, LOCAL * place + LOCAL)
        twice = dot3(
            once_high_ref[:, window], once_low_ref[:, window], matrix_high[...], matrix_low[...]
        )
        applied_ref[:, columns] = twice
        lead_ref[:, columns] = twice[0 : 2 * BLOCK]


def gram_kernel(place_ref, lead_ref, other_ref, applied_ref, gram_ref, *shared_refs):
    chip, second = place_ref[0], place_ref[1] == 1
    count = len(shared_refs)
    for s, place, core in ((0, 0, 0), (1, 0, 1), (2, BLOCK, 0)):
        mine, theirs = lead_ref[place : place + BLOCK, :], other_ref[place : place + BLOCK, :]
        pair = (mine, theirs) if core else (theirs, mine)
        block = jnp.where(second, *pair)
        for ref in shared_refs:
            ref[BLOCK * s : BLOCK * s + BLOCK, :] = block
    for step, ref in enumerate(shared_refs):
        start = pl.multiple_of(lax.rem(chip + step, count) * BLOCK, BLOCK)
        ref[HEAD:, :] = applied_ref[pl.ds(start, BLOCK), :]
    gram = dot32(shared_refs[0][0:HEAD, :], applied_ref[...], ((1,), (1,)))
    for part in range(OWN // 128):
        gram_ref[part] = gram[:, 128 * part : 128 * part + 128]


def spread(value):
    return jnp.broadcast_to(value, (8, 128))


def inverse_factor(pair):
    rows = [pair[8 * i : 8 * i + 8] for i in range(BLOCK // 8)]
    sublane = lax.broadcasted_iota(jnp.int32, (8, 128), 0)
    for p in range(BLOCK // 8):
        start = BLOCK + 8 * p
        columns = [
            [spread(rows[i][:, start + b : start + b + 1]) for b in range(8)]
            for i in range(p, BLOCK // 8)
        ]
        for j in range(8):
            inverse = lax.rsqrt(spread(columns[0][j][j : j + 1]))
            pivot_row = spread(rows[p][j : j + 1]) * inverse
            heads = [spread(columns[0][b][j : j + 1]) * inverse for b in range(j + 1, 8)]
            for i in range(p, BLOCK // 8):
                factor = columns[i - p][j] * inverse
                if i == p:
                    factor = jnp.where(sublane > j, factor, 0.0)
                rows[i] = rows[i] - factor * pivot_row
                for b in range(j + 1, 8):
                    columns[i - p][b] = columns[i - p][b] - factor * heads[b - j - 1]
            rows[p] = jnp.where(sublane == j, pivot_row, rows[p])
    return jnp.concatenate(rows, axis=0)[:, 0:BLOCK]


def dot32(left, right, dims):
    return lax.dot_general(
        left, right, (dims, ((), ())), precision=HIGHEST, preferred_element_type=F32
    )


def finish_kernel(scale, place_ref, gram_ref, *refs):
    *shared_refs, basis_ref, results, sems = refs
    chip, core = place_ref[0], place_ref[1]
    second = core == 1
    column = CORES * chip + core
    count = len(shared_refs)
    tiles = gram_ref.shape[0] // 2

    def columns_of(part, core):
        return jnp.concatenate([gram_ref[part * tiles + m, core] for m in range(tiles)], axis=0)

    first_pair, second_pair = columns_of(0, 0), columns_of(0, 1)
    low = jnp.where(second, second_pair, first_pair)
    high = jnp.where(second, columns_of(1, 1), columns_of(1, 0))
    mine = jnp.where(chip >= 2, high, low)
    mine = jnp.where(chip % 2 == 1, pltpu.roll(mine, BLOCK, axis=1), mine)
    full = jnp.concatenate([first_pair, second_pair, mine], axis=1) * scale
    gram = [full[BLOCK * s : BLOCK * s + BLOCK] for s in range(STEPS)]
    places = (0, 2 * BLOCK, BLOCK)
    lane = lax.broadcasted_iota(jnp.int32, (BLOCK, 128), 1)
    row = lax.broadcasted_iota(jnp.int32, (BLOCK, 128), 0)
    identity = jnp.where(lane == row, 1.0, 0.0).astype(F32)
    couplings = []
    inverses = []
    for s in range(STEPS):
        part = places[s] // 128
        tile = gram[s][:, 128 * part : 128 * part + 128]
        if places[s] % 128 == 0:
            tile = pltpu.roll(tile, BLOCK, axis=1)
        inverse = inverse_factor(jnp.where(lane < BLOCK, identity, tile))
        coupling = dot32(inverse, gram[s], ((1,), (0,)))
        for t in range(s + 1, STEPS):
            gram[t] = gram[t] - dot32(
                coupling[:, places[t] : places[t] + BLOCK], coupling, ((0,), (0,))
            )
        inverses.append(inverse)
        couplings.append(coupling)
    follows = column >= STEPS
    weights = [None] * STEPS
    for s in reversed(range(STEPS)):
        leads = jnp.where(column == s, identity[:, 0:BLOCK], 0.0)
        weight = jnp.where(follows, -couplings[s][:, 4 * BLOCK : 5 * BLOCK], leads)
        for t in range(s + 1, STEPS):
            weight = weight - dot32(
                couplings[s][:, places[t] : places[t] + BLOCK], weights[t], ((1,), (0,))
            )
        weights[s] = dot32(inverses[s], weight, ((0,), (0,)))
    weight_high, weight_low = split(jnp.concatenate(weights, axis=0).T)
    outs = []
    for step, ref in enumerate(shared_refs):
        head_high, head_low = split(ref[0:HEAD, :])
        result = jnp.where(follows, ref[HEAD:, :], 0.0)
        results[step] = result + dot3(weight_high, weight_low, head_high, head_low)
        source = lax.rem(chip + count - step, count)
        columns = pl.ds(pl.multiple_of(source * CHIP, CHIP), CHIP)
        out = pltpu.make_async_copy(results.at[step], basis_ref.at[:, columns], sems.at[step])
        out.start()
        outs.append(out)
    for out in outs:
        out.wait()


def exchange(value, axes):
    return lax.all_to_all(value, axes, split_axis=0, concat_axis=0, tiled=True)


SMEM = pl.BlockSpec(memory_space=pltpu.SMEM)
RAW = pl.BlockSpec(memory_space=pltpu.HBM)


def call(kernel, name, out_shape, inputs, scratch=(), specs=None, out_specs=None):
    single = not isinstance(out_shape, (tuple, list))
    if specs:
        inputs = [
            pltpu.with_memory_space_constraint(value, pltpu.HBM) if spec is RAW else value
            for value, spec in zip(inputs, specs)
        ]
    return pl.pallas_call(
        kernel,
        out_shape=out_shape,
        in_specs=specs or [VMEM] * len(inputs),
        out_specs=out_specs or VMEM if single else (VMEM,) * len(out_shape),
        scratch_shapes=list(scratch),
        compiler_params=PARAMS,
        name=name,
    )(*inputs)


def on_device(vectors, offsets, counts, labels, cosines, distances):
    chips = ("y", "z", "x")
    plane = ("y", "x")
    chip_count = lax.axis_size(chips)
    planes = lax.axis_size(plane)
    depth = lax.axis_size("z")
    count = lax.axis_size("x")

    def shift(value, step):
        return lax.ppermute(value, chips, [(i, (i + step) % chip_count) for i in range(chip_count)])

    shape = jax.ShapeDtypeStruct
    tables = (cosines, distances, offsets, counts.reshape(1, LOCAL), labels)
    slab = call(
        pack_kernel, "pack", shape((CORES, OWN + TABLE, LOCAL), F32), (vectors, *tables),
        [pltpu.VMEM(t.shape, t.dtype) for t in tables]
        + [pltpu.SemaphoreType.DMA((len(tables),)), pltpu.SemaphoreType.DMA((NV // BLOCK,))],
        [RAW] * 6,
    )
    slab = exchange(slab, "core")
    left = shift(slab, 1)
    right = shift(slab, -1)
    matrix = shape((WIDE, LOCAL), BF16)
    matrices = call(own_matrix_kernel, "own_matrix", (matrix,) * 4, (slab,))
    wide = pltpu.VMEM((WIDE, LOCAL), BF16)
    applied, lead = call(
        apply_kernel,
        "apply_twice",
        (shape((OWN, CHIP), F32), shape((2 * BLOCK, CHIP), F32)),
        (left, slab, right, *matrices),
        [pltpu.VMEM((OWN, 3 * CHIP), BF16)] * 2 + [pltpu.VMEM((OWN, 2 * CHIP), BF16)] * 2 + [wide] * 4,
    )
    other = lax.ppermute(lead, "core", [(0, 1), (1, 0)])
    place = jnp.stack([lax.axis_index("x"), lax.axis_index("core")])
    gram, *shared = call(
        gram_kernel, "gram",
        (shape((OWN // 128, HEAD, 128), F32),) + (shape((SHARED, CHIP), F32),) * count,
        (place, lead, other, applied), (), [SMEM] + [VMEM] * 3,
    )
    piece = (OWN // 128) * HEAD // planes
    everyone = planes * CORES
    gram = exchange(gram.reshape(planes, piece, 128), plane)
    gram = call(sum_kernel, "sum_plane", shape((depth, piece, 128), F32), (gram,))
    gram, *shared = lax.optimization_barrier((gram, *shared))
    shared = [shared[0]] + [
        lax.ppermute(shared[step], "x", [(i, (i + step) % count) for i in range(count)])
        for step in range(1, count)
    ]
    gram = exchange(gram, "z")
    gram = call(sum_kernel, "sum_depth", shape((everyone, piece, 128), F32), (gram,))
    gram = exchange(gram, (*plane, "core"))
    gram = gram.reshape(planes, CORES, piece, 128)
    scale = 1.0 / (CHIP * chip_count)
    slab_width = CHIP * count
    return call(
        lambda *refs: finish_kernel(scale, *refs), "finish", shape((BLOCK, slab_width), F32),
        (place, gram, *shared),
        [pltpu.VMEM((count, BLOCK, CHIP), F32), pltpu.SemaphoreType.DMA((count,))],
        [SMEM] + [VMEM] * (1 + count), RAW,
    )


def solution(mesh):
    rows = mesh.shape["rows"]
    cols = mesh.shape["cols"]
    names = ("y", "z", "x", "core")
    cube = Mesh(mesh.devices.reshape(Y_SIZE, rows // Y_SIZE, cols // CORES, CORES), names)
    whole = P(None, names)
    placed = (whole, whole, P(names), whole, whole, whole)
    return jax.shard_map(
        on_device, mesh=cube, in_specs=placed, out_specs=P(("x", "core"), ("y", "z")),
        check_vma=False,
    )
```

```python
import jax
import jax.numpy as jnp
from jax import lax
from jax.experimental import pallas as pl
from jax.experimental.pallas import tpu as pltpu
from jax.sharding import Mesh, PartitionSpec as P

PI_BOND = -1.0
SIGMA_BOND = 0.178
DECAY_LENGTH = 0.319
LAYER_GAP = 2.36
SITE_MASS = 0.4
LAYER_BIAS = 0.25

BLOCK = 64
STEPS = 3
HEAD = BLOCK * STEPS
SLOTS = 16
REACH = 256
NV = 512
LOCAL = 256
WIDE = LOCAL + 2 * REACH
Y_SIZE = 4
CORES = 2
OWN = NV // CORES
TABLE = 40
SHARED = HEAD + BLOCK
CHIP = CORES * LOCAL
F32 = jnp.float32
BF16 = jnp.bfloat16
HIGHEST = lax.Precision.HIGHEST
VMEM = pl.BlockSpec(memory_space=pltpu.VMEM)
PARAMS = pltpu.CompilerParams(vmem_limit_bytes=48 * 1024 * 1024)


def pack_kernel(
    core_ref, vectors_ref, cosines_ref, distances_ref, offsets_ref, counts_ref, labels_ref,
    own_ref, send_ref, cosines, distances, offsets, counts, labels, table_sems, block_sems,
):
    tables = (
        (cosines_ref, cosines), (distances_ref, distances), (offsets_ref, offsets),
        (counts_ref, counts), (labels_ref, labels),
    )
    table_copies = [
        pltpu.make_async_copy(source, target, table_sems.at[i])
        for i, (source, target) in enumerate(tables)
    ]
    block_copies = []
    for owner, ref in ((core_ref[0], own_ref), (1 - core_ref[0], send_ref)):
        for p in range(OWN // BLOCK):
            start = pl.multiple_of((owner + CORES * p) * BLOCK, BLOCK)
            block_copies.append(
                pltpu.make_async_copy(
                    vectors_ref.at[pl.ds(start, BLOCK)],
                    ref.at[pl.ds(BLOCK * p, BLOCK)],
                    block_sems.at[len(block_copies)],
                )
            )
    for copy in table_copies + block_copies:
        copy.start()
    for copy in table_copies:
        copy.wait()
    square = cosines[...] * cosines[...]
    bond = PI_BOND * jnp.exp(-(distances[...] - 1.0) / DECAY_LENGTH) * (1.0 - square)
    bond = bond + SIGMA_BOND * jnp.exp(-(distances[...] - LAYER_GAP) / DECAY_LENGTH) * square
    slot = lax.broadcasted_iota(jnp.int32, bond.shape, 0)
    hopping = jnp.where(slot < counts[...], bond, 0.0)
    steps = offsets[...].astype(F32)
    merged = jnp.zeros_like(hopping)
    for k in range(SLOTS):
        merged = merged + jnp.where(steps == steps[k : k + 1], hopping[k : k + 1], 0.0)
    sides = labels[...].astype(F32)
    onsite = SITE_MASS * (2.0 * sides[0:1] - 1.0) + LAYER_BIAS * (2.0 * sides[1:2] - 1.0)
    for ref in (own_ref, send_ref):
        ref[OWN : OWN + 16, :] = merged
        ref[OWN + 16 : OWN + 32, :] = steps
        ref[OWN + 32 : OWN + 40, :] = jnp.broadcast_to(onsite, (8, LOCAL))
    for copy in block_copies:
        copy.wait()


def sum_kernel(pieces_ref, out_ref):
    total = pieces_ref[0]
    for i in range(1, pieces_ref.shape[0]):
        total = total + pieces_ref[i]
    for i in range(out_ref.shape[0]):
        out_ref[i] = total


def build_matrix(table, high_ref, low_ref):
    hopping, offsets, onsite = table[0:16], table[16:32], table[32:33]
    lane = lax.broadcasted_iota(jnp.int32, (1, 128), 1).astype(F32)
    row_index = lax.broadcasted_iota(jnp.int32, (32, 128), 0).astype(F32)
    for half in range(2):
        columns = slice(128 * half, 128 * half + 128)
        empty = 640 * (1 - half)
        high_ref[empty : empty + 128, columns] = jnp.zeros((128, 128), BF16)
        low_ref[empty : empty + 128, columns] = jnp.zeros((128, 128), BF16)
        home = lane + float(REACH)
        targets = [
            jnp.broadcast_to(offsets[k : k + 1, columns] + home, (32, 128)) for k in range(SLOTS)
        ]
        values = [jnp.broadcast_to(hopping[k : k + 1, columns], (32, 128)) for k in range(SLOTS)]
        homes = jnp.broadcast_to(home, (32, 128))
        own = jnp.broadcast_to(onsite[:, columns], (32, 128))

        def chunk(step, carry):
            base = step * 32
            rows = row_index + base.astype(F32)
            total = jnp.where(homes == rows, own, 0.0)
            for k in range(SLOTS):
                total = jnp.where(targets[k] == rows, values[k], total)
            high = total.astype(BF16)
            low = (total - high.astype(F32)).astype(BF16)
            place = pl.ds(pl.multiple_of(base + 128 * half, 32), 32)
            high_ref[place, columns] = high
            low_ref[place, columns] = low
            return carry

        lax.fori_loop(0, 20, chunk, 0)


def own_matrix_kernel(core_ref, own_ref, mate_ref, *refs):
    second = core_ref[0] == 1
    own, mate = own_ref[OWN:, :], mate_ref[OWN:, :]
    build_matrix(jnp.where(second, mate, own), refs[0], refs[1])
    build_matrix(jnp.where(second, own, mate), refs[2], refs[3])


def split(value):
    high = value.astype(BF16)
    return high, (value - high.astype(F32)).astype(BF16)


def dot3(high, low, matrix_high, matrix_low):
    def dot(left, right):
        return jnp.dot(left, right, preferred_element_type=F32)

    return dot(high, matrix_high) + (dot(high, matrix_low) + dot(low, matrix_high))


def apply_kernel(
    core_ref, left_ref, left_mate_ref, own_ref, mate_ref, right_ref, right_mate_ref,
    first_high_ref, first_low_ref, second_high_ref, second_low_ref,
    applied_ref, lead_ref, high_ref, low_ref, once_high_ref, once_low_ref,
    left_high_ref, left_low_ref, right_high_ref, right_low_ref,
):
    core = core_ref[0]
    second = core == 1
    left_table = jnp.where(second, left_ref[OWN:, :], left_mate_ref[OWN:, :])
    right_table = jnp.where(second, right_mate_ref[OWN:, :], right_ref[OWN:, :])
    build_matrix(left_table, left_high_ref, left_low_ref)
    build_matrix(right_table, right_high_ref, right_low_ref)
    pairs = ((left_ref, left_mate_ref), (own_ref, mate_ref), (right_ref, right_mate_ref))
    for chip, pair in enumerate(pairs):
        for place, ref in zip((core, 1 - core), pair):
            start = pl.multiple_of((CORES * chip + place) * LOCAL, LOCAL)
            high, low = split(ref[0:OWN, :])
            high_ref[:, pl.ds(start, LOCAL)] = high
            low_ref[:, pl.ds(start, LOCAL)] = low
    matrices = (
        (left_high_ref, left_low_ref),
        (first_high_ref, first_low_ref),
        (second_high_ref, second_low_ref),
        (right_high_ref, right_low_ref),
    )
    for place, (matrix_high, matrix_low) in enumerate(matrices):
        window = slice(LOCAL * place, LOCAL * place + WIDE)
        columns = slice(LOCAL * place, LOCAL * place + LOCAL)
        once = dot3(high_ref[:, window], low_ref[:, window], matrix_high[...], matrix_low[...])
        high, low = split(once)
        once_high_ref[:, columns] = high
        once_low_ref[:, columns] = low
    for place, (matrix_high, matrix_low) in enumerate(matrices[1:3]):
        window = slice(LOCAL * place, LOCAL * place + WIDE)
        columns = slice(LOCAL * place, LOCAL * place + LOCAL)
        twice = dot3(
            once_high_ref[:, window], once_low_ref[:, window], matrix_high[...], matrix_low[...]
        )
        applied_ref[:, columns] = twice
        lead_ref[:, columns] = twice[0 : 2 * BLOCK]


def head_block(s, core_ref, lead_ref, other_ref):
    place, core = ((0, 0), (0, 1), (BLOCK, 0))[s]
    mine, theirs = lead_ref[place : place + BLOCK, :], other_ref[place : place + BLOCK, :]
    return jnp.where(core_ref[0] == core, mine, theirs)


def gram_kernel(core_ref, lead_ref, other_ref, applied_ref, gram_ref):
    blocks = [head_block(s, core_ref, lead_ref, other_ref) for s in range(STEPS)]
    gram = dot32(jnp.concatenate(blocks, axis=0), applied_ref[...], ((1,), (1,)))
    for part in range(OWN // 128):
        gram_ref[part] = gram[:, 128 * part : 128 * part + 128]


def share_kernel(core_ref, chip_ref, lead_ref, other_ref, applied_ref, *shared_refs):
    count = len(shared_refs)
    for s in range(STEPS):
        block = head_block(s, core_ref, lead_ref, other_ref)
        for ref in shared_refs:
            ref[BLOCK * s : BLOCK * s + BLOCK, :] = block
    for step, ref in enumerate(shared_refs):
        start = pl.multiple_of(lax.rem(chip_ref[0] + step, count) * BLOCK, BLOCK)
        ref[HEAD:, :] = applied_ref[pl.ds(start, BLOCK), :]


def spread(value):
    return jnp.broadcast_to(value, (8, 128))


def inverse_factor(pair):
    rows = [pair[8 * i : 8 * i + 8] for i in range(BLOCK // 8)]
    sublane = lax.broadcasted_iota(jnp.int32, (8, 128), 0)
    for p in range(BLOCK // 8):
        start = BLOCK + 8 * p
        columns = [
            [spread(rows[i][:, start + b : start + b + 1]) for b in range(8)]
            for i in range(p, BLOCK // 8)
        ]
        for j in range(8):
            inverse = lax.rsqrt(spread(columns[0][j][j : j + 1]))
            pivot_row = spread(rows[p][j : j + 1]) * inverse
            heads = [spread(columns[0][b][j : j + 1]) * inverse for b in range(j + 1, 8)]
            for i in range(p, BLOCK // 8):
                factor = columns[i - p][j] * inverse
                if i == p:
                    factor = jnp.where(sublane > j, factor, 0.0)
                rows[i] = rows[i] - factor * pivot_row
                for b in range(j + 1, 8):
                    columns[i - p][b] = columns[i - p][b] - factor * heads[b - j - 1]
            rows[p] = jnp.where(sublane == j, pivot_row, rows[p])
    return jnp.concatenate(rows, axis=0)[:, 0:BLOCK]


def dot32(left, right, dims):
    return lax.dot_general(
        left, right, (dims, ((), ())), precision=HIGHEST, preferred_element_type=F32
    )


def finish_kernel(scale, core_ref, chip_ref, gram_ref, *refs):
    *shared_refs, basis_ref, results, sems = refs
    chip, core = chip_ref[0], core_ref[0]
    second = core == 1
    column = CORES * chip + core
    count = len(shared_refs)
    tiles = gram_ref.shape[0] // 2

    def columns_of(part, core):
        return jnp.concatenate([gram_ref[part * tiles + m, core] for m in range(tiles)], axis=0)

    first_pair, second_pair = columns_of(0, 0), columns_of(0, 1)
    low = jnp.where(second, second_pair, first_pair)
    high = jnp.where(second, columns_of(1, 1), columns_of(1, 0))
    mine = jnp.where(chip >= 2, high, low)
    mine = jnp.where(chip % 2 == 1, pltpu.roll(mine, BLOCK, axis=1), mine)
    full = jnp.concatenate([first_pair, second_pair, mine], axis=1) * scale
    gram = [full[BLOCK * s : BLOCK * s + BLOCK] for s in range(STEPS)]
    places = (0, 2 * BLOCK, BLOCK)
    lane = lax.broadcasted_iota(jnp.int32, (BLOCK, 128), 1)
    row = lax.broadcasted_iota(jnp.int32, (BLOCK, 128), 0)
    identity = jnp.where(lane == row, 1.0, 0.0).astype(F32)
    couplings = []
    inverses = []
    for s in range(STEPS):
        part = places[s] // 128
        tile = gram[s][:, 128 * part : 128 * part + 128]
        if places[s] % 128 == 0:
            tile = pltpu.roll(tile, BLOCK, axis=1)
        inverse = inverse_factor(jnp.where(lane < BLOCK, identity, tile))
        coupling = dot32(inverse, gram[s], ((1,), (0,)))
        for t in range(s + 1, STEPS):
            gram[t] = gram[t] - dot32(
                coupling[:, places[t] : places[t] + BLOCK], coupling, ((0,), (0,))
            )
        inverses.append(inverse)
        couplings.append(coupling)
    follows = column >= STEPS
    weights = [None] * STEPS
    for s in reversed(range(STEPS)):
        leads = jnp.where(column == s, identity[:, 0:BLOCK], 0.0)
        weight = jnp.where(follows, -couplings[s][:, 4 * BLOCK : 5 * BLOCK], leads)
        for t in range(s + 1, STEPS):
            weight = weight - dot32(
                couplings[s][:, places[t] : places[t] + BLOCK], weights[t], ((1,), (0,))
            )
        weights[s] = dot32(inverses[s], weight, ((0,), (0,)))
    weight_high, weight_low = split(jnp.concatenate(weights, axis=0).T)
    outs = []
    for step, ref in enumerate(shared_refs):
        head_high, head_low = split(ref[0:HEAD, :])
        result = jnp.where(follows, ref[HEAD:, :], 0.0)
        results[step] = result + dot3(weight_high, weight_low, head_high, head_low)
        source = lax.rem(chip + count - step, count)
        columns = pl.ds(pl.multiple_of(source * CHIP, CHIP), CHIP)
        out = pltpu.make_async_copy(results.at[step], basis_ref.at[:, columns], sems.at[step])
        out.start()
        outs.append(out)
    for out in outs:
        out.wait()


def exchange(value, axes):
    return lax.all_to_all(value, axes, split_axis=0, concat_axis=0, tiled=True)


SMEM = pl.BlockSpec(memory_space=pltpu.SMEM)
RAW = pl.BlockSpec(memory_space=pltpu.HBM)


def call(kernel, name, out_shape, inputs, scratch=(), specs=None, out_specs=None):
    single = not isinstance(out_shape, (tuple, list))
    if specs:
        inputs = [
            pltpu.with_memory_space_constraint(value, pltpu.HBM) if spec is RAW else value
            for value, spec in zip(inputs, specs)
        ]
    return pl.pallas_call(
        kernel,
        out_shape=out_shape,
        in_specs=specs or [VMEM] * len(inputs),
        out_specs=out_specs or VMEM if single else (VMEM,) * len(out_shape),
        scratch_shapes=list(scratch),
        compiler_params=PARAMS,
        name=name,
    )(*inputs)


def on_device(vectors, offsets, counts, labels, cosines, distances):
    chips = ("y", "z", "x")
    plane = ("y", "x")
    chip_count = lax.axis_size(chips)
    planes = lax.axis_size(plane)
    depth = lax.axis_size("z")
    count = lax.axis_size("x")

    def shift(value, step):
        return lax.ppermute(value, chips, [(i, (i + step) % chip_count) for i in range(chip_count)])

    shape = jax.ShapeDtypeStruct
    core = lax.axis_index("core").reshape(1)
    chip = lax.axis_index("x").reshape(1)
    tables = (cosines, distances, offsets, counts.reshape(1, LOCAL), labels)
    part = shape((OWN + TABLE, LOCAL), F32)
    own, send = call(
        pack_kernel, "pack", (part, part), (core, vectors, *tables),
        [pltpu.VMEM(t.shape, t.dtype) for t in tables]
        + [pltpu.SemaphoreType.DMA((len(tables),)), pltpu.SemaphoreType.DMA((NV // BLOCK,))],
        [SMEM] + [RAW] * 6,
    )
    left = shift(own, 1)
    right = shift(own, -1)
    mate = lax.ppermute(send, "core", [(0, 1), (1, 0)])
    left_mate = shift(mate, 1)
    right_mate = shift(mate, -1)
    matrix = shape((WIDE, LOCAL), BF16)
    matrices = call(
        own_matrix_kernel, "own_matrix", (matrix,) * 4, (core, own, mate), (), [SMEM] + [VMEM] * 2
    )
    wide = pltpu.VMEM((WIDE, LOCAL), BF16)
    applied, lead = call(
        apply_kernel,
        "apply_twice",
        (shape((OWN, CHIP), F32), shape((2 * BLOCK, CHIP), F32)),
        (core, left, left_mate, own, mate, right, right_mate, *matrices),
        [pltpu.VMEM((OWN, 3 * CHIP), BF16)] * 2 + [pltpu.VMEM((OWN, 2 * CHIP), BF16)] * 2 + [wide] * 4,
        [SMEM] + [VMEM] * 10,
    )
    other = lax.ppermute(lead, "core", [(0, 1), (1, 0)])
    gram = call(
        gram_kernel, "gram", shape((OWN // 128, HEAD, 128), F32),
        (core, lead, other, applied), (), [SMEM] + [VMEM] * 3,
    )
    shared = call(
        share_kernel, "share", (shape((SHARED, CHIP), F32),) * count,
        (core, chip, lead, other, applied), (), [SMEM] * 2 + [VMEM] * 3,
    )
    piece = (OWN // 128) * HEAD // planes
    everyone = planes * CORES
    gram = exchange(gram.reshape(planes, piece, 128), plane)
    gram = call(sum_kernel, "sum_plane", shape((depth, piece, 128), F32), (gram,))
    shared = [shared[0]] + [
        lax.ppermute(shared[step], "x", [(i, (i + step) % count) for i in range(count)])
        for step in range(1, count)
    ]
    gram = exchange(gram, "z")
    gram = call(sum_kernel, "sum_depth", shape((everyone, piece, 128), F32), (gram,))
    gram = exchange(gram, (*plane, "core"))
    gram = gram.reshape(planes, CORES, piece, 128)
    scale = 1.0 / (CHIP * chip_count)
    slab_width = CHIP * count
    return call(
        lambda *refs: finish_kernel(scale, *refs), "finish", shape((BLOCK, slab_width), F32),
        (core, chip, gram, *shared),
        [pltpu.VMEM((count, BLOCK, CHIP), F32), pltpu.SemaphoreType.DMA((count,))],
        [SMEM] * 2 + [VMEM] * (1 + count), RAW,
    )


def solution(mesh):
    rows = mesh.shape["rows"]
    cols = mesh.shape["cols"]
    names = ("y", "z", "x", "core")
    cube = Mesh(mesh.devices.reshape(Y_SIZE, rows // Y_SIZE, cols // CORES, CORES), names)
    whole = P(None, names)
    placed = (whole, whole, P(names), whole, whole, whole)
    return jax.shard_map(
        on_device, mesh=cube, in_specs=placed, out_specs=P(("x", "core"), ("y", "z")),
        check_vma=False,
    )
```

```python
import jax
import jax.numpy as jnp
from jax import lax
from jax.experimental import pallas as pl
from jax.experimental.pallas import tpu as pltpu
from jax.sharding import Mesh, PartitionSpec as P

PI_BOND = -1.0
SIGMA_BOND = 0.178
DECAY_LENGTH = 0.319
LAYER_GAP = 2.36
SITE_MASS = 0.4
LAYER_BIAS = 0.25

BLOCK = 64
STEPS = 3
HEAD = BLOCK * STEPS
SLOTS = 16
REACH = 256
NV = 512
LOCAL = 256
WIDE = LOCAL + 2 * REACH
Y_SIZE = 4
CORES = 2
OWN = NV // CORES
TABLE = 40
SHARED = HEAD + BLOCK
CHIP = CORES * LOCAL
F32 = jnp.float32
BF16 = jnp.bfloat16
HIGHEST = lax.Precision.HIGHEST
VMEM = pl.BlockSpec(memory_space=pltpu.VMEM)
PARAMS = pltpu.CompilerParams(vmem_limit_bytes=48 * 1024 * 1024)


def pack_kernel(
    vectors_ref, cosines_ref, distances_ref, offsets_ref, counts_ref, labels_ref, out_ref,
    cosines, distances, offsets, counts, labels, table_sems, block_sems,
):
    tables = (
        (cosines_ref, cosines), (distances_ref, distances), (offsets_ref, offsets),
        (counts_ref, counts), (labels_ref, labels),
    )
    table_copies = [
        pltpu.make_async_copy(source, target, table_sems.at[i])
        for i, (source, target) in enumerate(tables)
    ]
    block_copies = [
        pltpu.make_async_copy(
            vectors_ref.at[pl.ds(BLOCK * (core + CORES * p), BLOCK)],
            out_ref.at[core, pl.ds(BLOCK * p, BLOCK)],
            block_sems.at[core + CORES * p],
        )
        for core in range(CORES)
        for p in range(OWN // BLOCK)
    ]
    for copy in table_copies + block_copies:
        copy.start()
    for copy in table_copies:
        copy.wait()
    square = cosines[...] * cosines[...]
    bond = PI_BOND * jnp.exp(-(distances[...] - 1.0) / DECAY_LENGTH) * (1.0 - square)
    bond = bond + SIGMA_BOND * jnp.exp(-(distances[...] - LAYER_GAP) / DECAY_LENGTH) * square
    slot = lax.broadcasted_iota(jnp.int32, bond.shape, 0)
    hopping = jnp.where(slot < counts[...], bond, 0.0)
    steps = offsets[...].astype(F32)
    merged = jnp.zeros_like(hopping)
    for k in range(SLOTS):
        merged = merged + jnp.where(steps == steps[k : k + 1], hopping[k : k + 1], 0.0)
    sides = labels[...].astype(F32)
    onsite = SITE_MASS * (2.0 * sides[0:1] - 1.0) + LAYER_BIAS * (2.0 * sides[1:2] - 1.0)
    for core in range(CORES):
        out_ref[core, OWN : OWN + 16, :] = merged
        out_ref[core, OWN + 16 : OWN + 32, :] = steps
        out_ref[core, OWN + 32 : OWN + 40, :] = jnp.broadcast_to(onsite, (8, LOCAL))
    for copy in block_copies:
        copy.wait()


def sum_kernel(pieces_ref, out_ref):
    total = pieces_ref[0]
    for i in range(1, pieces_ref.shape[0]):
        total = total + pieces_ref[i]
    for i in range(out_ref.shape[0]):
        out_ref[i] = total


def build_matrix(table, high_ref, low_ref):
    hopping, offsets, onsite = table[0:16], table[16:32], table[32:33]
    lane = lax.broadcasted_iota(jnp.int32, (1, 128), 1).astype(F32)
    row_index = lax.broadcasted_iota(jnp.int32, (32, 128), 0).astype(F32)
    for half in range(2):
        columns = slice(128 * half, 128 * half + 128)
        empty = 640 * (1 - half)
        high_ref[empty : empty + 128, columns] = jnp.zeros((128, 128), BF16)
        low_ref[empty : empty + 128, columns] = jnp.zeros((128, 128), BF16)
        home = lane + float(REACH)
        targets = [
            jnp.broadcast_to(offsets[k : k + 1, columns] + home, (32, 128)) for k in range(SLOTS)
        ]
        values = [jnp.broadcast_to(hopping[k : k + 1, columns], (32, 128)) for k in range(SLOTS)]
        homes = jnp.broadcast_to(home, (32, 128))
        own = jnp.broadcast_to(onsite[:, columns], (32, 128))

        def chunk(step, carry):
            base = step * 32
            rows = row_index + base.astype(F32)
            total = jnp.where(homes == rows, own, 0.0)
            for k in range(SLOTS):
                total = jnp.where(targets[k] == rows, values[k], total)
            high = total.astype(BF16)
            low = (total - high.astype(F32)).astype(BF16)
            place = pl.ds(pl.multiple_of(base + 128 * half, 32), 32)
            high_ref[place, columns] = high
            low_ref[place, columns] = low
            return carry

        lax.fori_loop(0, 20, chunk, 0)


def own_matrix_kernel(slab_ref, *refs):
    for core in range(CORES):
        build_matrix(slab_ref[core, OWN:, :], refs[2 * core], refs[2 * core + 1])


def split(value):
    high = value.astype(BF16)
    return high, (value - high.astype(F32)).astype(BF16)


def dot3(high, low, matrix_high, matrix_low):
    def dot(left, right):
        return jnp.dot(left, right, preferred_element_type=F32)

    return dot(high, matrix_high) + (dot(high, matrix_low) + dot(low, matrix_high))


def apply_kernel(
    left_ref, own_ref, right_ref, first_high_ref, first_low_ref, second_high_ref, second_low_ref,
    applied_ref, lead_ref, high_ref, low_ref, once_high_ref, once_low_ref,
    left_high_ref, left_low_ref, right_high_ref, right_low_ref,
):
    build_matrix(left_ref[1, OWN:, :], left_high_ref, left_low_ref)
    build_matrix(right_ref[0, OWN:, :], right_high_ref, right_low_ref)
    sources = [(ref, core) for ref in (left_ref, own_ref, right_ref) for core in range(CORES)]
    for place, (ref, core) in enumerate(sources):
        columns = slice(LOCAL * place, LOCAL * place + LOCAL)
        high, low = split(ref[core, 0:OWN, :])
        high_ref[:, columns] = high
        low_ref[:, columns] = low
    matrices = (
        (left_high_ref, left_low_ref),
        (first_high_ref, first_low_ref),
        (second_high_ref, second_low_ref),
        (right_high_ref, right_low_ref),
    )
    for place, (matrix_high, matrix_low) in enumerate(matrices):
        window = slice(LOCAL * place, LOCAL * place + WIDE)
        columns = slice(LOCAL * place, LOCAL * place + LOCAL)
        once = dot3(high_ref[:, window], low_ref[:, window], matrix_high[...], matrix_low[...])
        high, low = split(once)
        once_high_ref[:, columns] = high
        once_low_ref[:, columns] = low
    for place, (matrix_high, matrix_low) in enumerate(matrices[1:3]):
        window = slice(LOCAL * place, LOCAL * place + WIDE)
        columns = slice(LOCAL * place, LOCAL * place + LOCAL)
        twice = dot3(
            once_high_ref[:, window], once_low_ref[:, window], matrix_high[...], matrix_low[...]
        )
        applied_ref[:, columns] = twice
        lead_ref[:, columns] = twice[0 : 2 * BLOCK]


def head_block(s, core_ref, lead_ref, other_ref):
    place, core = ((0, 0), (0, 1), (BLOCK, 0))[s]
    mine, theirs = lead_ref[place : place + BLOCK, :], other_ref[place : place + BLOCK, :]
    return jnp.where(core_ref[0] == core, mine, theirs)


def gram_kernel(core_ref, lead_ref, other_ref, applied_ref, gram_ref):
    blocks = [head_block(s, core_ref, lead_ref, other_ref) for s in range(STEPS)]
    gram = dot32(jnp.concatenate(blocks, axis=0), applied_ref[...], ((1,), (1,)))
    for part in range(OWN // 128):
        gram_ref[part] = gram[:, 128 * part : 128 * part + 128]


def share_kernel(core_ref, chip_ref, lead_ref, other_ref, applied_ref, *shared_refs):
    count = len(shared_refs)
    for s in range(STEPS):
        block = head_block(s, core_ref, lead_ref, other_ref)
        for ref in shared_refs:
            ref[BLOCK * s : BLOCK * s + BLOCK, :] = block
    for step, ref in enumerate(shared_refs):
        start = pl.multiple_of(lax.rem(chip_ref[0] + step, count) * BLOCK, BLOCK)
        ref[HEAD:, :] = applied_ref[pl.ds(start, BLOCK), :]


def spread(value):
    return jnp.broadcast_to(value, (8, 128))


def inverse_factor(pair):
    rows = [pair[8 * i : 8 * i + 8] for i in range(BLOCK // 8)]
    sublane = lax.broadcasted_iota(jnp.int32, (8, 128), 0)
    for p in range(BLOCK // 8):
        start = BLOCK + 8 * p
        columns = [
            [spread(rows[i][:, start + b : start + b + 1]) for b in range(8)]
            for i in range(p, BLOCK // 8)
        ]
        for j in range(8):
            inverse = lax.rsqrt(spread(columns[0][j][j : j + 1]))
            pivot_row = spread(rows[p][j : j + 1]) * inverse
            heads = [spread(columns[0][b][j : j + 1]) * inverse for b in range(j + 1, 8)]
            for i in range(p, BLOCK // 8):
                factor = columns[i - p][j] * inverse
                if i == p:
                    factor = jnp.where(sublane > j, factor, 0.0)
                rows[i] = rows[i] - factor * pivot_row
                for b in range(j + 1, 8):
                    columns[i - p][b] = columns[i - p][b] - factor * heads[b - j - 1]
            rows[p] = jnp.where(sublane == j, pivot_row, rows[p])
    return jnp.concatenate(rows, axis=0)[:, 0:BLOCK]


def dot32(left, right, dims):
    return lax.dot_general(
        left, right, (dims, ((), ())), precision=HIGHEST, preferred_element_type=F32
    )


def finish_kernel(scale, core_ref, chip_ref, gram_ref, *refs):
    *shared_refs, basis_ref, results, sems = refs
    chip, core = chip_ref[0], core_ref[0]
    second = core == 1
    column = CORES * chip + core
    count = len(shared_refs)
    tiles = gram_ref.shape[0] // 2

    def columns_of(part, core):
        return jnp.concatenate([gram_ref[part * tiles + m, core] for m in range(tiles)], axis=0)

    first_pair, second_pair = columns_of(0, 0), columns_of(0, 1)
    low = jnp.where(second, second_pair, first_pair)
    high = jnp.where(second, columns_of(1, 1), columns_of(1, 0))
    mine = jnp.where(chip >= 2, high, low)
    mine = jnp.where(chip % 2 == 1, pltpu.roll(mine, BLOCK, axis=1), mine)
    full = jnp.concatenate([first_pair, second_pair, mine], axis=1) * scale
    gram = [full[BLOCK * s : BLOCK * s + BLOCK] for s in range(STEPS)]
    places = (0, 2 * BLOCK, BLOCK)
    lane = lax.broadcasted_iota(jnp.int32, (BLOCK, 128), 1)
    row = lax.broadcasted_iota(jnp.int32, (BLOCK, 128), 0)
    identity = jnp.where(lane == row, 1.0, 0.0).astype(F32)
    couplings = []
    inverses = []
    for s in range(STEPS):
        part = places[s] // 128
        tile = gram[s][:, 128 * part : 128 * part + 128]
        if places[s] % 128 == 0:
            tile = pltpu.roll(tile, BLOCK, axis=1)
        inverse = inverse_factor(jnp.where(lane < BLOCK, identity, tile))
        coupling = dot32(inverse, gram[s], ((1,), (0,)))
        for t in range(s + 1, STEPS):
            gram[t] = gram[t] - dot32(
                coupling[:, places[t] : places[t] + BLOCK], coupling, ((0,), (0,))
            )
        inverses.append(inverse)
        couplings.append(coupling)
    follows = column >= STEPS
    weights = [None] * STEPS
    for s in reversed(range(STEPS)):
        leads = jnp.where(column == s, identity[:, 0:BLOCK], 0.0)
        weight = jnp.where(follows, -couplings[s][:, 4 * BLOCK : 5 * BLOCK], leads)
        for t in range(s + 1, STEPS):
            weight = weight - dot32(
                couplings[s][:, places[t] : places[t] + BLOCK], weights[t], ((1,), (0,))
            )
        weights[s] = dot32(inverses[s], weight, ((0,), (0,)))
    weight_high, weight_low = split(jnp.concatenate(weights, axis=0).T)
    outs = []
    for step, ref in enumerate(shared_refs):
        head_high, head_low = split(ref[0:HEAD, :])
        result = jnp.where(follows, ref[HEAD:, :], 0.0)
        results[step] = result + dot3(weight_high, weight_low, head_high, head_low)
        source = lax.rem(chip + count - step, count)
        columns = pl.ds(pl.multiple_of(source * CHIP, CHIP), CHIP)
        out = pltpu.make_async_copy(results.at[step], basis_ref.at[:, columns], sems.at[step])
        out.start()
        outs.append(out)
    for out in outs:
        out.wait()


def exchange(value, axes):
    return lax.all_to_all(value, axes, split_axis=0, concat_axis=0, tiled=True)


SMEM = pl.BlockSpec(memory_space=pltpu.SMEM)
RAW = pl.BlockSpec(memory_space=pltpu.HBM)


def call(kernel, name, out_shape, inputs, scratch=(), specs=None, out_specs=None):
    single = not isinstance(out_shape, (tuple, list))
    if specs:
        inputs = [
            pltpu.with_memory_space_constraint(value, pltpu.HBM) if spec is RAW else value
            for value, spec in zip(inputs, specs)
        ]
    return pl.pallas_call(
        kernel,
        out_shape=out_shape,
        in_specs=specs or [VMEM] * len(inputs),
        out_specs=out_specs or VMEM if single else (VMEM,) * len(out_shape),
        scratch_shapes=list(scratch),
        compiler_params=PARAMS,
        name=name,
    )(*inputs)


def on_device(vectors, offsets, counts, labels, cosines, distances):
    chips = ("y", "z", "x")
    plane = ("y", "x")
    chip_count = lax.axis_size(chips)
    planes = lax.axis_size(plane)
    depth = lax.axis_size("z")
    count = lax.axis_size("x")

    def shift(value, step):
        return lax.ppermute(value, chips, [(i, (i + step) % chip_count) for i in range(chip_count)])

    shape = jax.ShapeDtypeStruct
    tables = (cosines, distances, offsets, counts.reshape(1, LOCAL), labels)
    slab = call(
        pack_kernel, "pack", shape((CORES, OWN + TABLE, LOCAL), F32), (vectors, *tables),
        [pltpu.VMEM(t.shape, t.dtype) for t in tables]
        + [pltpu.SemaphoreType.DMA((len(tables),)), pltpu.SemaphoreType.DMA((NV // BLOCK,))],
        [RAW] * 6,
    )
    slab = exchange(slab, "core")
    left = shift(slab, 1)
    right = shift(slab, -1)
    matrix = shape((WIDE, LOCAL), BF16)
    matrices = call(own_matrix_kernel, "own_matrix", (matrix,) * 4, (slab,))
    wide = pltpu.VMEM((WIDE, LOCAL), BF16)
    applied, lead = call(
        apply_kernel,
        "apply_twice",
        (shape((OWN, CHIP), F32), shape((2 * BLOCK, CHIP), F32)),
        (left, slab, right, *matrices),
        [pltpu.VMEM((OWN, 3 * CHIP), BF16)] * 2 + [pltpu.VMEM((OWN, 2 * CHIP), BF16)] * 2 + [wide] * 4,
    )
    other = lax.ppermute(lead, "core", [(0, 1), (1, 0)])
    core = lax.axis_index("core").reshape(1)
    chip = lax.axis_index("x").reshape(1)
    gram = call(
        gram_kernel, "gram", shape((OWN // 128, HEAD, 128), F32),
        (core, lead, other, applied), (), [SMEM] + [VMEM] * 3,
    )
    shared = call(
        share_kernel, "share", (shape((SHARED, CHIP), F32),) * count,
        (core, chip, lead, other, applied), (), [SMEM] * 2 + [VMEM] * 3,
    )
    piece = (OWN // 128) * HEAD // planes
    everyone = planes * CORES
    gram = exchange(gram.reshape(planes, piece, 128), plane)
    gram = call(sum_kernel, "sum_plane", shape((depth, piece, 128), F32), (gram,))
    shared = [shared[0]] + [
        lax.ppermute(shared[step], "x", [(i, (i + step) % count) for i in range(count)])
        for step in range(1, count)
    ]
    gram = exchange(gram, "z")
    gram = call(sum_kernel, "sum_depth", shape((everyone, piece, 128), F32), (gram,))
    gram = exchange(gram, (*plane, "core"))
    gram = gram.reshape(planes, CORES, piece, 128)
    scale = 1.0 / (CHIP * chip_count)
    slab_width = CHIP * count
    return call(
        lambda *refs: finish_kernel(scale, *refs), "finish", shape((BLOCK, slab_width), F32),
        (core, chip, gram, *shared),
        [pltpu.VMEM((count, BLOCK, CHIP), F32), pltpu.SemaphoreType.DMA((count,))],
        [SMEM] * 2 + [VMEM] * (1 + count), RAW,
    )


def solution(mesh):
    rows = mesh.shape["rows"]
    cols = mesh.shape["cols"]
    names = ("y", "z", "x", "core")
    cube = Mesh(mesh.devices.reshape(Y_SIZE, rows // Y_SIZE, cols // CORES, CORES), names)
    whole = P(None, names)
    placed = (whole, whole, P(names), whole, whole, whole)
    return jax.shard_map(
        on_device, mesh=cube, in_specs=placed, out_specs=P(("x", "core"), ("y", "z")),
        check_vma=False,
    )
```

```python
import jax
import jax.numpy as jnp
from jax import lax
from jax.experimental import pallas as pl
from jax.experimental.pallas import tpu as pltpu
from jax.sharding import Mesh, PartitionSpec as P

PI_BOND = -1.0
SIGMA_BOND = 0.178
DECAY_LENGTH = 0.319
LAYER_GAP = 2.36
SITE_MASS = 0.4
LAYER_BIAS = 0.25

BLOCK = 64
STEPS = 3
HEAD = BLOCK * STEPS
SLOTS = 16
REACH = 256
NV = 512
LOCAL = 256
WIDE = LOCAL + 2 * REACH
Y_SIZE = 4
CORES = 2
OWN = NV // CORES
TABLE = 40
HALF = HEAD // CORES
CHIP = CORES * LOCAL
F32 = jnp.float32
BF16 = jnp.bfloat16
HIGHEST = lax.Precision.HIGHEST
VMEM = pl.BlockSpec(memory_space=pltpu.VMEM)
PARAMS = pltpu.CompilerParams(vmem_limit_bytes=48 * 1024 * 1024)


def pack_kernel(
    vectors_ref, cosines_ref, distances_ref, offsets_ref, counts_ref, labels_ref, out_ref,
    cosines, distances, offsets, counts, labels, table_sems, block_sems,
):
    tables = (
        (cosines_ref, cosines), (distances_ref, distances), (offsets_ref, offsets),
        (counts_ref, counts), (labels_ref, labels),
    )
    table_copies = [
        pltpu.make_async_copy(source, target, table_sems.at[i])
        for i, (source, target) in enumerate(tables)
    ]
    block_copies = [
        pltpu.make_async_copy(
            vectors_ref.at[pl.ds(BLOCK * (core + CORES * p), BLOCK)],
            out_ref.at[core, pl.ds(BLOCK * p, BLOCK)],
            block_sems.at[core + CORES * p],
        )
        for core in range(CORES)
        for p in range(OWN // BLOCK)
    ]
    for copy in table_copies + block_copies:
        copy.start()
    for copy in table_copies:
        copy.wait()
    square = cosines[...] * cosines[...]
    bond = PI_BOND * jnp.exp(-(distances[...] - 1.0) / DECAY_LENGTH) * (1.0 - square)
    bond = bond + SIGMA_BOND * jnp.exp(-(distances[...] - LAYER_GAP) / DECAY_LENGTH) * square
    slot = lax.broadcasted_iota(jnp.int32, bond.shape, 0)
    hopping = jnp.where(slot < counts[...], bond, 0.0)
    steps = offsets[...].astype(F32)
    merged = jnp.zeros_like(hopping)
    for k in range(SLOTS):
        merged = merged + jnp.where(steps == steps[k : k + 1], hopping[k : k + 1], 0.0)
    sides = labels[...].astype(F32)
    onsite = SITE_MASS * (2.0 * sides[0:1] - 1.0) + LAYER_BIAS * (2.0 * sides[1:2] - 1.0)
    for core in range(CORES):
        out_ref[core, OWN : OWN + 16, :] = merged
        out_ref[core, OWN + 16 : OWN + 32, :] = steps
        out_ref[core, OWN + 32 : OWN + 40, :] = jnp.broadcast_to(onsite, (8, LOCAL))
    for copy in block_copies:
        copy.wait()


def sum_kernel(pieces_ref, out_ref):
    total = pieces_ref[0]
    for i in range(1, pieces_ref.shape[0]):
        total = total + pieces_ref[i]
    for i in range(out_ref.shape[0]):
        out_ref[i] = total


def build_matrix(table, high_ref, low_ref):
    hopping, offsets, onsite = table[0:16], table[16:32], table[32:33]
    lane = lax.broadcasted_iota(jnp.int32, (1, 128), 1).astype(F32)
    row_index = lax.broadcasted_iota(jnp.int32, (32, 128), 0).astype(F32)
    for half in range(2):
        columns = slice(128 * half, 128 * half + 128)
        empty = 640 * (1 - half)
        high_ref[empty : empty + 128, columns] = jnp.zeros((128, 128), BF16)
        low_ref[empty : empty + 128, columns] = jnp.zeros((128, 128), BF16)
        home = lane + float(REACH)
        targets = [
            jnp.broadcast_to(offsets[k : k + 1, columns] + home, (32, 128)) for k in range(SLOTS)
        ]
        values = [jnp.broadcast_to(hopping[k : k + 1, columns], (32, 128)) for k in range(SLOTS)]
        homes = jnp.broadcast_to(home, (32, 128))
        own = jnp.broadcast_to(onsite[:, columns], (32, 128))

        def chunk(step, carry):
            base = step * 32
            rows = row_index + base.astype(F32)
            total = jnp.where(homes == rows, own, 0.0)
            for k in range(SLOTS):
                total = jnp.where(targets[k] == rows, values[k], total)
            high = total.astype(BF16)
            low = (total - high.astype(F32)).astype(BF16)
            place = pl.ds(pl.multiple_of(base + 128 * half, 32), 32)
            high_ref[place, columns] = high
            low_ref[place, columns] = low
            return carry

        lax.fori_loop(0, 20, chunk, 0)


def own_matrix_kernel(slab_ref, *refs):
    for core in range(CORES):
        build_matrix(slab_ref[core, OWN:, :], refs[2 * core], refs[2 * core + 1])


def split(value):
    high = value.astype(BF16)
    return high, (value - high.astype(F32)).astype(BF16)


def dot3(high, low, matrix_high, matrix_low):
    def dot(left, right):
        return jnp.dot(left, right, preferred_element_type=F32)

    return dot(high, matrix_high) + (dot(high, matrix_low) + dot(low, matrix_high))


def apply_kernel(
    left_ref, own_ref, right_ref, first_high_ref, first_low_ref, second_high_ref, second_low_ref,
    applied_ref, lead_ref, high_ref, low_ref, once_high_ref, once_low_ref,
    left_high_ref, left_low_ref, right_high_ref, right_low_ref,
):
    build_matrix(left_ref[1, OWN:, :], left_high_ref, left_low_ref)
    build_matrix(right_ref[0, OWN:, :], right_high_ref, right_low_ref)
    sources = [(ref, core) for ref in (left_ref, own_ref, right_ref) for core in range(CORES)]
    for place, (ref, core) in enumerate(sources):
        columns = slice(LOCAL * place, LOCAL * place + LOCAL)
        high, low = split(ref[core, 0:OWN, :])
        high_ref[:, columns] = high
        low_ref[:, columns] = low
    matrices = (
        (left_high_ref, left_low_ref),
        (first_high_ref, first_low_ref),
        (second_high_ref, second_low_ref),
        (right_high_ref, right_low_ref),
    )
    for place, (matrix_high, matrix_low) in enumerate(matrices):
        window = slice(LOCAL * place, LOCAL * place + WIDE)
        columns = slice(LOCAL * place, LOCAL * place + LOCAL)
        once = dot3(high_ref[:, window], low_ref[:, window], matrix_high[...], matrix_low[...])
        high, low = split(once)
        once_high_ref[:, columns] = high
        once_low_ref[:, columns] = low
    for place, (matrix_high, matrix_low) in enumerate(matrices[1:3]):
        window = slice(LOCAL * place, LOCAL * place + WIDE)
        columns = slice(LOCAL * place, LOCAL * place + LOCAL)
        twice = dot3(
            once_high_ref[:, window], once_low_ref[:, window], matrix_high[...], matrix_low[...]
        )
        applied_ref[:, columns] = twice
        lead_ref[:, columns] = twice[0 : 2 * BLOCK]


def head_block(s, core_ref, lead_ref, other_ref):
    place, core = ((0, 0), (0, 1), (BLOCK, 0))[s]
    mine, theirs = lead_ref[place : place + BLOCK, :], other_ref[place : place + BLOCK, :]
    return jnp.where(core_ref[0] == core, mine, theirs)


def gram_kernel(core_ref, lead_ref, other_ref, applied_ref, gram_ref):
    blocks = [head_block(s, core_ref, lead_ref, other_ref) for s in range(STEPS)]
    gram = dot32(jnp.concatenate(blocks, axis=0), applied_ref[...], ((1,), (1,)))
    for part in range(OWN // 128):
        gram_ref[part] = gram[:, 128 * part : 128 * part + 128]


def share_kernel(core_ref, chip_ref, lead_ref, other_ref, applied_ref, home_ref, *sent_refs):
    count = 1 + len(sent_refs)
    second = core_ref[0] == 1
    head = [head_block(s, core_ref, lead_ref, other_ref) for s in range(STEPS)]
    for s in range(STEPS):
        home_ref[BLOCK * s : BLOCK * s + BLOCK, :] = head[s]
    middle = HALF - BLOCK
    half = (
        jnp.where(second, head[1][middle:], head[0][0 : BLOCK - middle]),
        jnp.where(second, head[2][0:BLOCK], jnp.concatenate(
            [head[0][BLOCK - middle :], head[1][0:middle]], axis=0)),
    )
    for ref in sent_refs:
        ref[0 : BLOCK - middle, :] = half[0]
        ref[BLOCK - middle : HALF, :] = half[1]
    for step, ref in enumerate((home_ref, *sent_refs)):
        start = pl.multiple_of(lax.rem(chip_ref[0] + step, count) * BLOCK, BLOCK)
        ref[ref.shape[0] - BLOCK :, :] = applied_ref[pl.ds(start, BLOCK), :]


def spread(value):
    return jnp.broadcast_to(value, (8, 128))


def inverse_factor(pair):
    rows = [pair[8 * i : 8 * i + 8] for i in range(BLOCK // 8)]
    sublane = lax.broadcasted_iota(jnp.int32, (8, 128), 0)
    for p in range(BLOCK // 8):
        start = BLOCK + 8 * p
        columns = [
            [spread(rows[i][:, start + b : start + b + 1]) for b in range(8)]
            for i in range(p, BLOCK // 8)
        ]
        for j in range(8):
            inverse = lax.rsqrt(spread(columns[0][j][j : j + 1]))
            pivot_row = spread(rows[p][j : j + 1]) * inverse
            heads = [spread(columns[0][b][j : j + 1]) * inverse for b in range(j + 1, 8)]
            for i in range(p, BLOCK // 8):
                factor = columns[i - p][j] * inverse
                if i == p:
                    factor = jnp.where(sublane > j, factor, 0.0)
                rows[i] = rows[i] - factor * pivot_row
                for b in range(j + 1, 8):
                    columns[i - p][b] = columns[i - p][b] - factor * heads[b - j - 1]
            rows[p] = jnp.where(sublane == j, pivot_row, rows[p])
    return jnp.concatenate(rows, axis=0)[:, 0:BLOCK]


def dot32(left, right, dims):
    return lax.dot_general(
        left, right, (dims, ((), ())), precision=HIGHEST, preferred_element_type=F32
    )


def finish_kernel(scale, core_ref, chip_ref, gram_ref, *refs):
    home_ref, *others, basis_ref, results, sems = refs
    count = 1 + len(others) // 2
    got_refs, mate_refs = others[: count - 1], others[count - 1 :]
    chip, core = chip_ref[0], core_ref[0]
    second = core == 1
    column = CORES * chip + core
    tiles = gram_ref.shape[0] // 2

    def columns_of(part, core):
        return jnp.concatenate([gram_ref[part * tiles + m, core] for m in range(tiles)], axis=0)

    first_pair, second_pair = columns_of(0, 0), columns_of(0, 1)
    low = jnp.where(second, second_pair, first_pair)
    high = jnp.where(second, columns_of(1, 1), columns_of(1, 0))
    mine = jnp.where(chip >= 2, high, low)
    mine = jnp.where(chip % 2 == 1, pltpu.roll(mine, BLOCK, axis=1), mine)
    full = jnp.concatenate([first_pair, second_pair, mine], axis=1) * scale
    gram = [full[BLOCK * s : BLOCK * s + BLOCK] for s in range(STEPS)]
    places = (0, 2 * BLOCK, BLOCK)
    lane = lax.broadcasted_iota(jnp.int32, (BLOCK, 128), 1)
    row = lax.broadcasted_iota(jnp.int32, (BLOCK, 128), 0)
    identity = jnp.where(lane == row, 1.0, 0.0).astype(F32)
    couplings = []
    inverses = []
    for s in range(STEPS):
        part = places[s] // 128
        tile = gram[s][:, 128 * part : 128 * part + 128]
        if places[s] % 128 == 0:
            tile = pltpu.roll(tile, BLOCK, axis=1)
        inverse = inverse_factor(jnp.where(lane < BLOCK, identity, tile))
        coupling = dot32(inverse, gram[s], ((1,), (0,)))
        for t in range(s + 1, STEPS):
            gram[t] = gram[t] - dot32(
                coupling[:, places[t] : places[t] + BLOCK], coupling, ((0,), (0,))
            )
        inverses.append(inverse)
        couplings.append(coupling)
    follows = column >= STEPS
    weights = [None] * STEPS
    for s in reversed(range(STEPS)):
        leads = jnp.where(column == s, identity[:, 0:BLOCK], 0.0)
        weight = jnp.where(follows, -couplings[s][:, 4 * BLOCK : 5 * BLOCK], leads)
        for t in range(s + 1, STEPS):
            weight = weight - dot32(
                couplings[s][:, places[t] : places[t] + BLOCK], weights[t], ((1,), (0,))
            )
        weights[s] = dot32(inverses[s], weight, ((0,), (0,)))
    weights = jnp.concatenate(weights, axis=0)
    swapped = jnp.concatenate([weights[HALF:], weights[0:HALF]], axis=0)
    home_weights = split(weights.T)
    other_weights = split(jnp.where(second, swapped, weights).T)
    outs = []
    for step in range(count):
        if step == 0:
            head, block, parts = home_ref[0:HEAD, :], home_ref[HEAD:, :], home_weights
        else:
            got = got_refs[step - 1]
            head = jnp.concatenate([got[0:HALF, :], mate_refs[step - 1][0:HALF, :]], axis=0)
            block, parts = got[HALF:, :], other_weights
        head_high, head_low = split(head)
        results[step] = jnp.where(follows, block, 0.0) + dot3(*parts, head_high, head_low)
        source = lax.rem(chip + count - step, count)
        columns = pl.ds(pl.multiple_of(source * CHIP, CHIP), CHIP)
        out = pltpu.make_async_copy(results.at[step], basis_ref.at[:, columns], sems.at[step])
        out.start()
        outs.append(out)
    for out in outs:
        out.wait()


def exchange(value, axes):
    return lax.all_to_all(value, axes, split_axis=0, concat_axis=0, tiled=True)


SMEM = pl.BlockSpec(memory_space=pltpu.SMEM)
RAW = pl.BlockSpec(memory_space=pltpu.HBM)


def call(kernel, name, out_shape, inputs, scratch=(), specs=None, out_specs=None):
    single = not isinstance(out_shape, (tuple, list))
    if specs:
        inputs = [
            pltpu.with_memory_space_constraint(value, pltpu.HBM) if spec is RAW else value
            for value, spec in zip(inputs, specs)
        ]
    return pl.pallas_call(
        kernel,
        out_shape=out_shape,
        in_specs=specs or [VMEM] * len(inputs),
        out_specs=out_specs or VMEM if single else (VMEM,) * len(out_shape),
        scratch_shapes=list(scratch),
        compiler_params=PARAMS,
        name=name,
    )(*inputs)


def on_device(vectors, offsets, counts, labels, cosines, distances):
    chips = ("y", "z", "x")
    plane = ("y", "x")
    chip_count = lax.axis_size(chips)
    planes = lax.axis_size(plane)
    depth = lax.axis_size("z")
    count = lax.axis_size("x")

    def shift(value, step):
        return lax.ppermute(value, chips, [(i, (i + step) % chip_count) for i in range(chip_count)])

    shape = jax.ShapeDtypeStruct
    tables = (cosines, distances, offsets, counts.reshape(1, LOCAL), labels)
    slab = call(
        pack_kernel, "pack", shape((CORES, OWN + TABLE, LOCAL), F32), (vectors, *tables),
        [pltpu.VMEM(t.shape, t.dtype) for t in tables]
        + [pltpu.SemaphoreType.DMA((len(tables),)), pltpu.SemaphoreType.DMA((NV // BLOCK,))],
        [RAW] * 6,
    )
    slab = exchange(slab, "core")
    left = shift(slab, 1)
    right = shift(slab, -1)
    matrix = shape((WIDE, LOCAL), BF16)
    matrices = call(own_matrix_kernel, "own_matrix", (matrix,) * 4, (slab,))
    wide = pltpu.VMEM((WIDE, LOCAL), BF16)
    applied, lead = call(
        apply_kernel,
        "apply_twice",
        (shape((OWN, CHIP), F32), shape((2 * BLOCK, CHIP), F32)),
        (left, slab, right, *matrices),
        [pltpu.VMEM((OWN, 3 * CHIP), BF16)] * 2 + [pltpu.VMEM((OWN, 2 * CHIP), BF16)] * 2 + [wide] * 4,
    )
    other = lax.ppermute(lead, "core", [(0, 1), (1, 0)])
    core = lax.axis_index("core").reshape(1)
    chip = lax.axis_index("x").reshape(1)
    gram = call(
        gram_kernel, "gram", shape((OWN // 128, HEAD, 128), F32),
        (core, lead, other, applied), (), [SMEM] + [VMEM] * 3,
    )
    home, *sent = call(
        share_kernel, "share",
        (shape((HEAD + BLOCK, CHIP), F32),) + (shape((HALF + BLOCK, CHIP), F32),) * (count - 1),
        (core, chip, lead, other, applied), (), [SMEM] * 2 + [VMEM] * 3,
    )
    got = [
        lax.ppermute(value, "x", [(i, (i + step + 1) % count) for i in range(count)])
        for step, value in enumerate(sent)
    ]
    theirs = [lax.ppermute(value, "core", [(0, 1), (1, 0)]) for value in got]
    piece = (OWN // 128) * HEAD // planes
    everyone = planes * CORES
    gram = exchange(gram.reshape(planes, piece, 128), plane)
    gram = call(sum_kernel, "sum_plane", shape((depth, piece, 128), F32), (gram,))
    gram = exchange(gram, "z")
    gram = call(sum_kernel, "sum_depth", shape((everyone, piece, 128), F32), (gram,))
    gram = exchange(gram, (*plane, "core"))
    gram = gram.reshape(planes, CORES, piece, 128)
    scale = 1.0 / (CHIP * chip_count)
    slab_width = CHIP * count
    return call(
        lambda *refs: finish_kernel(scale, *refs), "finish", shape((BLOCK, slab_width), F32),
        (core, chip, gram, home, *got, *theirs),
        [pltpu.VMEM((count, BLOCK, CHIP), F32), pltpu.SemaphoreType.DMA((count,))],
        [SMEM] * 2 + [VMEM] * (2 * count), RAW,
    )


def solution(mesh):
    rows = mesh.shape["rows"]
    cols = mesh.shape["cols"]
    names = ("y", "z", "x", "core")
    cube = Mesh(mesh.devices.reshape(Y_SIZE, rows // Y_SIZE, cols // CORES, CORES), names)
    whole = P(None, names)
    placed = (whole, whole, P(names), whole, whole, whole)
    return jax.shard_map(
        on_device, mesh=cube, in_specs=placed, out_specs=P(("x", "core"), ("y", "z")),
        check_vma=False,
    )
```

```python
import jax
import jax.numpy as jnp
from jax import lax
from jax.experimental import pallas as pl
from jax.experimental.pallas import tpu as pltpu
from jax.sharding import Mesh, PartitionSpec as P

PI_BOND = -1.0
SIGMA_BOND = 0.178
DECAY_LENGTH = 0.319
LAYER_GAP = 2.36
SITE_MASS = 0.4
LAYER_BIAS = 0.25

BLOCK = 64
STEPS = 3
HEAD = BLOCK * STEPS
SLOTS = 16
REACH = 256
NV = 512
LOCAL = 256
WIDE = LOCAL + 2 * REACH
CHUNK = 128
Y_SIZE = 4
CORES = 2
OWN = NV // CORES
TABLE = 40
HALF = HEAD // CORES
CHIP = CORES * LOCAL
F32 = jnp.float32
BF16 = jnp.bfloat16
HIGHEST = lax.Precision.HIGHEST
VMEM = pl.BlockSpec(memory_space=pltpu.VMEM)
PARAMS = pltpu.CompilerParams(vmem_limit_bytes=48 * 1024 * 1024)


def pack_kernel(
    vectors_ref, cosines_ref, distances_ref, offsets_ref, counts_ref, labels_ref, out_ref,
    cosines, distances, offsets, counts, labels, table_sems, block_sems,
):
    tables = (
        (cosines_ref, cosines), (distances_ref, distances), (offsets_ref, offsets),
        (counts_ref, counts), (labels_ref, labels),
    )
    table_copies = [
        pltpu.make_async_copy(source, target, table_sems.at[i])
        for i, (source, target) in enumerate(tables)
    ]
    block_copies = [
        pltpu.make_async_copy(
            vectors_ref.at[pl.ds(BLOCK * (core + CORES * p), BLOCK)],
            out_ref.at[core, pl.ds(BLOCK * p, BLOCK)],
            block_sems.at[core + CORES * p],
        )
        for core in range(CORES)
        for p in range(OWN // BLOCK)
    ]
    for copy in table_copies + block_copies:
        copy.start()
    for copy in table_copies:
        copy.wait()
    square = cosines[...] * cosines[...]
    bond = PI_BOND * jnp.exp(-(distances[...] - 1.0) / DECAY_LENGTH) * (1.0 - square)
    bond = bond + SIGMA_BOND * jnp.exp(-(distances[...] - LAYER_GAP) / DECAY_LENGTH) * square
    slot = lax.broadcasted_iota(jnp.int32, bond.shape, 0)
    hopping = jnp.where(slot < counts[...], bond, 0.0)
    steps = offsets[...].astype(F32)
    merged = jnp.zeros_like(hopping)
    for k in range(SLOTS):
        merged = merged + jnp.where(steps == steps[k : k + 1], hopping[k : k + 1], 0.0)
    sides = labels[...].astype(F32)
    onsite = SITE_MASS * (2.0 * sides[0:1] - 1.0) + LAYER_BIAS * (2.0 * sides[1:2] - 1.0)
    for core in range(CORES):
        out_ref[core, OWN : OWN + 16, :] = merged
        out_ref[core, OWN + 16 : OWN + 32, :] = steps
        out_ref[core, OWN + 32 : OWN + 40, :] = jnp.broadcast_to(onsite, (8, LOCAL))
    for copy in block_copies:
        copy.wait()


def sum_kernel(pieces_ref, out_ref):
    total = pieces_ref[0]
    for i in range(1, pieces_ref.shape[0]):
        total = total + pieces_ref[i]
    for i in range(out_ref.shape[0]):
        out_ref[i] = total


def build_matrix(table, high_ref, low_ref):
    hopping, offsets, onsite = table[0:16], table[16:32], table[32:33]
    lane = lax.broadcasted_iota(jnp.int32, (1, 128), 1).astype(F32)
    row_index = lax.broadcasted_iota(jnp.int32, (CHUNK, 128), 0).astype(F32)
    for half in range(2):
        columns = slice(128 * half, 128 * half + 128)
        empty = 640 * (1 - half)
        high_ref[empty : empty + 128, columns] = jnp.zeros((128, 128), BF16)
        low_ref[empty : empty + 128, columns] = jnp.zeros((128, 128), BF16)
        home = lane + float(REACH)
        targets = [
            jnp.broadcast_to(offsets[k : k + 1, columns] + home, (CHUNK, 128)) for k in range(SLOTS)
        ]
        values = [jnp.broadcast_to(hopping[k : k + 1, columns], (CHUNK, 128)) for k in range(SLOTS)]
        homes = jnp.broadcast_to(home, (CHUNK, 128))
        own = jnp.broadcast_to(onsite[:, columns], (CHUNK, 128))

        def chunk(step, carry):
            base = step * CHUNK
            rows = row_index + base.astype(F32)
            total = jnp.where(homes == rows, own, 0.0)
            for k in range(SLOTS):
                total = jnp.where(targets[k] == rows, values[k], total)
            high = total.astype(BF16)
            low = (total - high.astype(F32)).astype(BF16)
            place = pl.ds(pl.multiple_of(base + 128 * half, 128), CHUNK)
            high_ref[place, columns] = high
            low_ref[place, columns] = low
            return carry

        lax.fori_loop(0, (WIDE - 128) // CHUNK, chunk, 0)


def own_matrix_kernel(slab_ref, *refs):
    for core in range(CORES):
        build_matrix(slab_ref[core, OWN:, :], refs[2 * core], refs[2 * core + 1])


def split(value):
    high = value.astype(BF16)
    return high, (value - high.astype(F32)).astype(BF16)


def dot3(high, low, matrix_high, matrix_low):
    def dot(left, right):
        return jnp.dot(left, right, preferred_element_type=F32)

    return dot(high, matrix_high) + (dot(high, matrix_low) + dot(low, matrix_high))


def apply_kernel(
    left_ref, own_ref, right_ref, first_high_ref, first_low_ref, second_high_ref, second_low_ref,
    applied_ref, lead_ref, high_ref, low_ref, once_high_ref, once_low_ref,
    left_high_ref, left_low_ref, right_high_ref, right_low_ref,
):
    build_matrix(left_ref[1, OWN:, :], left_high_ref, left_low_ref)
    build_matrix(right_ref[0, OWN:, :], right_high_ref, right_low_ref)
    sources = [(ref, core) for ref in (left_ref, own_ref, right_ref) for core in range(CORES)]
    for place, (ref, core) in enumerate(sources):
        columns = slice(LOCAL * place, LOCAL * place + LOCAL)
        high, low = split(ref[core, 0:OWN, :])
        high_ref[:, columns] = high
        low_ref[:, columns] = low
    matrices = (
        (left_high_ref, left_low_ref),
        (first_high_ref, first_low_ref),
        (second_high_ref, second_low_ref),
        (right_high_ref, right_low_ref),
    )
    for place, (matrix_high, matrix_low) in enumerate(matrices):
        window = slice(LOCAL * place, LOCAL * place + WIDE)
        columns = slice(LOCAL * place, LOCAL * place + LOCAL)
        once = dot3(high_ref[:, window], low_ref[:, window], matrix_high[...], matrix_low[...])
        high, low = split(once)
        once_high_ref[:, columns] = high
        once_low_ref[:, columns] = low
    for place, (matrix_high, matrix_low) in enumerate(matrices[1:3]):
        window = slice(LOCAL * place, LOCAL * place + WIDE)
        columns = slice(LOCAL * place, LOCAL * place + LOCAL)
        twice = dot3(
            once_high_ref[:, window], once_low_ref[:, window], matrix_high[...], matrix_low[...]
        )
        applied_ref[:, columns] = twice
        lead_ref[:, columns] = twice[0 : 2 * BLOCK]


def head_block(s, core_ref, lead_ref, other_ref):
    place, core = ((0, 0), (0, 1), (BLOCK, 0))[s]
    mine, theirs = lead_ref[place : place + BLOCK, :], other_ref[place : place + BLOCK, :]
    return jnp.where(core_ref[0] == core, mine, theirs)


def gram_kernel(core_ref, lead_ref, other_ref, applied_ref, gram_ref):
    blocks = [head_block(s, core_ref, lead_ref, other_ref) for s in range(STEPS)]
    gram = dot32(jnp.concatenate(blocks, axis=0), applied_ref[...], ((1,), (1,)))
    for part in range(OWN // 128):
        gram_ref[part] = gram[:, 128 * part : 128 * part + 128]


def share_kernel(core_ref, chip_ref, lead_ref, other_ref, applied_ref, home_ref, *sent_refs):
    count = 1 + len(sent_refs)
    second = core_ref[0] == 1
    head = [head_block(s, core_ref, lead_ref, other_ref) for s in range(STEPS)]
    for s in range(STEPS):
        home_ref[BLOCK * s : BLOCK * s + BLOCK, :] = head[s]
    middle = HALF - BLOCK
    half = (
        jnp.where(second, head[1][middle:], head[0][0 : BLOCK - middle]),
        jnp.where(second, head[2][0:BLOCK], jnp.concatenate(
            [head[0][BLOCK - middle :], head[1][0:middle]], axis=0)),
    )
    for ref in sent_refs:
        ref[0 : BLOCK - middle, :] = half[0]
        ref[BLOCK - middle : HALF, :] = half[1]
    for step, ref in enumerate((home_ref, *sent_refs)):
        start = pl.multiple_of(lax.rem(chip_ref[0] + step, count) * BLOCK, BLOCK)
        ref[ref.shape[0] - BLOCK :, :] = applied_ref[pl.ds(start, BLOCK), :]


def spread(value):
    return jnp.broadcast_to(value, (8, 128))


def inverse_factor(pair):
    rows = [pair[8 * i : 8 * i + 8] for i in range(BLOCK // 8)]
    sublane = lax.broadcasted_iota(jnp.int32, (8, 128), 0)
    for p in range(BLOCK // 8):
        start = BLOCK + 8 * p
        columns = [
            [spread(rows[i][:, start + b : start + b + 1]) for b in range(8)]
            for i in range(p, BLOCK // 8)
        ]
        for j in range(8):
            inverse = lax.rsqrt(spread(columns[0][j][j : j + 1]))
            pivot_row = spread(rows[p][j : j + 1]) * inverse
            heads = [spread(columns[0][b][j : j + 1]) * inverse for b in range(j + 1, 8)]
            for i in range(p, BLOCK // 8):
                factor = columns[i - p][j] * inverse
                if i == p:
                    factor = jnp.where(sublane > j, factor, 0.0)
                rows[i] = rows[i] - factor * pivot_row
                for b in range(j + 1, 8):
                    columns[i - p][b] = columns[i - p][b] - factor * heads[b - j - 1]
            rows[p] = jnp.where(sublane == j, pivot_row, rows[p])
    return jnp.concatenate(rows, axis=0)[:, 0:BLOCK]


def dot32(left, right, dims):
    return lax.dot_general(
        left, right, (dims, ((), ())), precision=HIGHEST, preferred_element_type=F32
    )


def finish_kernel(scale, core_ref, chip_ref, gram_ref, *refs):
    home_ref, *others, basis_ref, results, sems = refs
    count = 1 + len(others) // 2
    got_refs, mate_refs = others[: count - 1], others[count - 1 :]
    chip, core = chip_ref[0], core_ref[0]
    second = core == 1
    column = CORES * chip + core
    tiles = gram_ref.shape[0] // 2

    def columns_of(part, core):
        return jnp.concatenate([gram_ref[part * tiles + m, core] for m in range(tiles)], axis=0)

    first_pair, second_pair = columns_of(0, 0), columns_of(0, 1)
    low = jnp.where(second, second_pair, first_pair)
    high = jnp.where(second, columns_of(1, 1), columns_of(1, 0))
    mine = jnp.where(chip >= 2, high, low)
    mine = jnp.where(chip % 2 == 1, pltpu.roll(mine, BLOCK, axis=1), mine)
    full = jnp.concatenate([first_pair, second_pair, mine], axis=1) * scale
    gram = [full[BLOCK * s : BLOCK * s + BLOCK] for s in range(STEPS)]
    places = (0, 2 * BLOCK, BLOCK)
    lane = lax.broadcasted_iota(jnp.int32, (BLOCK, 128), 1)
    row = lax.broadcasted_iota(jnp.int32, (BLOCK, 128), 0)
    identity = jnp.where(lane == row, 1.0, 0.0).astype(F32)
    zero = jnp.zeros((BLOCK, BLOCK), F32)
    for s in range(STEPS):
        unit = [identity[:, 0:BLOCK] if t == s else zero for t in range(STEPS)]
        gram[s] = jnp.concatenate([gram[s], *unit], axis=1)
    couplings = []
    for s in range(STEPS):
        part = places[s] // 128
        tile = gram[s][:, 128 * part : 128 * part + 128]
        if places[s] % 128 == 0:
            tile = pltpu.roll(tile, BLOCK, axis=1)
        inverse = inverse_factor(jnp.where(lane < BLOCK, identity, tile))
        coupling = dot32(inverse, gram[s], ((1,), (0,)))
        for t in range(s + 1, STEPS):
            gram[t] = gram[t] - dot32(
                coupling[:, places[t] : places[t] + BLOCK], coupling, ((0,), (0,))
            )
        couplings.append(coupling)
    follows = column >= STEPS
    units = 6 * BLOCK
    mine = jnp.concatenate([c[:, 4 * BLOCK : 5 * BLOCK] for c in couplings], axis=0)
    inverse = jnp.concatenate([c[:, units:] for c in couplings], axis=0)
    weight = -dot32(mine, inverse, ((0,), (0,)))
    for s in range(STEPS):
        weight = jnp.where(column == s, couplings[s][:, units:], weight)
    parts = split(weight)
    outs = []
    for step in range(count):
        if step == 0:
            head, block = home_ref[0:HEAD, :], home_ref[HEAD:, :]
        else:
            got, mate = got_refs[step - 1], mate_refs[step - 1]
            first, last = got[0:HALF, :], mate[0:HALF, :]
            head = jnp.where(
                second,
                jnp.concatenate([last, first], axis=0),
                jnp.concatenate([first, last], axis=0),
            )
            block = got[HALF:, :]
        head_high, head_low = split(head)
        results[step] = jnp.where(follows, block, 0.0) + dot3(*parts, head_high, head_low)
        source = lax.rem(chip + count - step, count)
        columns = pl.ds(pl.multiple_of(source * CHIP, CHIP), CHIP)
        out = pltpu.make_async_copy(results.at[step], basis_ref.at[:, columns], sems.at[step])
        out.start()
        outs.append(out)
    for out in outs:
        out.wait()


def exchange(value, axes):
    return lax.all_to_all(value, axes, split_axis=0, concat_axis=0, tiled=True)


SMEM = pl.BlockSpec(memory_space=pltpu.SMEM)
RAW = pl.BlockSpec(memory_space=pltpu.HBM)


def call(kernel, name, out_shape, inputs, scratch=(), specs=None, out_specs=None):
    single = not isinstance(out_shape, (tuple, list))
    if specs:
        inputs = [
            pltpu.with_memory_space_constraint(value, pltpu.HBM) if spec is RAW else value
            for value, spec in zip(inputs, specs)
        ]
    return pl.pallas_call(
        kernel,
        out_shape=out_shape,
        in_specs=specs or [VMEM] * len(inputs),
        out_specs=out_specs or VMEM if single else (VMEM,) * len(out_shape),
        scratch_shapes=list(scratch),
        compiler_params=PARAMS,
        name=name,
    )(*inputs)


def on_device(vectors, offsets, counts, labels, cosines, distances):
    chips = ("y", "z", "x")
    plane = ("y", "x")
    chip_count = lax.axis_size(chips)
    planes = lax.axis_size(plane)
    depth = lax.axis_size("z")
    count = lax.axis_size("x")

    def shift(value, step):
        return lax.ppermute(value, chips, [(i, (i + step) % chip_count) for i in range(chip_count)])

    shape = jax.ShapeDtypeStruct
    tables = (cosines, distances, offsets, counts.reshape(1, LOCAL), labels)
    slab = call(
        pack_kernel, "pack", shape((CORES, OWN + TABLE, LOCAL), F32), (vectors, *tables),
        [pltpu.VMEM(t.shape, t.dtype) for t in tables]
        + [pltpu.SemaphoreType.DMA((len(tables),)), pltpu.SemaphoreType.DMA((NV // BLOCK,))],
        [RAW] * 6,
    )
    slab = exchange(slab, "core")
    left = shift(slab, 1)
    right = shift(slab, -1)
    matrix = shape((WIDE, LOCAL), BF16)
    matrices = call(own_matrix_kernel, "own_matrix", (matrix,) * 4, (slab,))
    wide = pltpu.VMEM((WIDE, LOCAL), BF16)
    applied, lead = call(
        apply_kernel,
        "apply_twice",
        (shape((OWN, CHIP), F32), shape((2 * BLOCK, CHIP), F32)),
        (left, slab, right, *matrices),
        [pltpu.VMEM((OWN, 3 * CHIP), BF16)] * 2 + [pltpu.VMEM((OWN, 2 * CHIP), BF16)] * 2 + [wide] * 4,
    )
    other = lax.ppermute(lead, "core", [(0, 1), (1, 0)])
    core = lax.axis_index("core").reshape(1)
    chip = lax.axis_index("x").reshape(1)
    gram = call(
        gram_kernel, "gram", shape((OWN // 128, HEAD, 128), F32),
        (core, lead, other, applied), (), [SMEM] + [VMEM] * 3,
    )
    home, *sent = call(
        share_kernel, "share",
        (shape((HEAD + BLOCK, CHIP), F32),) + (shape((HALF + BLOCK, CHIP), F32),) * (count - 1),
        (core, chip, lead, other, applied), (), [SMEM] * 2 + [VMEM] * 3,
    )
    piece = (OWN // 128) * HEAD // planes
    everyone = planes * CORES
    gram = exchange(gram.reshape(planes, piece, 128), plane)
    gram, home, *sent = lax.optimization_barrier((gram, home, *sent))
    gram = call(sum_kernel, "sum_plane", shape((depth, piece, 128), F32), (gram,))
    got = [
        lax.ppermute(value, "x", [(i, (i + step + 1) % count) for i in range(count)])
        for step, value in enumerate(sent)
    ]
    theirs = [lax.ppermute(value, "core", [(0, 1), (1, 0)]) for value in got]
    gram = exchange(gram, "z")
    gram = call(sum_kernel, "sum_depth", shape((everyone, piece, 128), F32), (gram,))
    gram = exchange(gram, (*plane, "core"))
    gram = gram.reshape(planes, CORES, piece, 128)
    scale = 1.0 / (CHIP * chip_count)
    slab_width = CHIP * count
    return call(
        lambda *refs: finish_kernel(scale, *refs), "finish", shape((BLOCK, slab_width), F32),
        (core, chip, gram, home, *got, *theirs),
        [pltpu.VMEM((count, BLOCK, CHIP), F32), pltpu.SemaphoreType.DMA((count,))],
        [SMEM] * 2 + [VMEM] * (2 * count), RAW,
    )


def solution(mesh):
    rows = mesh.shape["rows"]
    cols = mesh.shape["cols"]
    names = ("y", "z", "x", "core")
    cube = Mesh(mesh.devices.reshape(Y_SIZE, rows // Y_SIZE, cols // CORES, CORES), names)
    whole = P(None, names)
    placed = (whole, whole, P(names), whole, whole, whole)
    return jax.shard_map(
        on_device, mesh=cube, in_specs=placed, out_specs=P(("x", "core"), ("y", "z")),
        check_vma=False,
    )
```

```python
import jax
import jax.numpy as jnp
from jax import lax
from jax.experimental import pallas as pl
from jax.experimental.pallas import tpu as pltpu
from jax.sharding import Mesh, PartitionSpec as P

PI_BOND = -1.0
SIGMA_BOND = 0.178
DECAY_LENGTH = 0.319
LAYER_GAP = 2.36
SITE_MASS = 0.4
LAYER_BIAS = 0.25

BLOCK = 64
STEPS = 3
HEAD = BLOCK * STEPS
SLOTS = 16
REACH = 256
NV = 512
LOCAL = 256
WIDE = LOCAL + 2 * REACH
CHUNK = 128
Y_SIZE = 4
CORES = 2
OWN = NV // CORES
TABLE = 40
HALF = HEAD // CORES
CHIP = CORES * LOCAL
F32 = jnp.float32
BF16 = jnp.bfloat16
HIGHEST = lax.Precision.HIGHEST
VMEM = pl.BlockSpec(memory_space=pltpu.VMEM)
PARAMS = pltpu.CompilerParams(vmem_limit_bytes=48 * 1024 * 1024)


def pack_kernel(
    vectors_ref, cosines_ref, distances_ref, offsets_ref, counts_ref, labels_ref, out_ref,
    cosines, distances, offsets, counts, labels, table_sems, block_sems,
):
    tables = (
        (cosines_ref, cosines), (distances_ref, distances), (offsets_ref, offsets),
        (counts_ref, counts), (labels_ref, labels),
    )
    table_copies = [
        pltpu.make_async_copy(source, target, table_sems.at[i])
        for i, (source, target) in enumerate(tables)
    ]
    block_copies = [
        pltpu.make_async_copy(
            vectors_ref.at[pl.ds(BLOCK * (core + CORES * p), BLOCK)],
            out_ref.at[core, pl.ds(BLOCK * p, BLOCK)],
            block_sems.at[core + CORES * p],
        )
        for core in range(CORES)
        for p in range(OWN // BLOCK)
    ]
    for copy in table_copies + block_copies:
        copy.start()
    for copy in table_copies:
        copy.wait()
    square = cosines[...] * cosines[...]
    bond = PI_BOND * jnp.exp(-(distances[...] - 1.0) / DECAY_LENGTH) * (1.0 - square)
    bond = bond + SIGMA_BOND * jnp.exp(-(distances[...] - LAYER_GAP) / DECAY_LENGTH) * square
    slot = lax.broadcasted_iota(jnp.int32, bond.shape, 0)
    hopping = jnp.where(slot < counts[...], bond, 0.0)
    steps = offsets[...].astype(F32)
    merged = jnp.zeros_like(hopping)
    for k in range(SLOTS):
        merged = merged + jnp.where(steps == steps[k : k + 1], hopping[k : k + 1], 0.0)
    sides = labels[...].astype(F32)
    onsite = SITE_MASS * (2.0 * sides[0:1] - 1.0) + LAYER_BIAS * (2.0 * sides[1:2] - 1.0)
    for core in range(CORES):
        out_ref[core, OWN : OWN + 16, :] = merged
        out_ref[core, OWN + 16 : OWN + 32, :] = steps
        out_ref[core, OWN + 32 : OWN + 40, :] = jnp.broadcast_to(onsite, (8, LOCAL))
    for copy in block_copies:
        copy.wait()


def sum_kernel(pieces_ref, out_ref):
    total = pieces_ref[0]
    for i in range(1, pieces_ref.shape[0]):
        total = total + pieces_ref[i]
    for i in range(out_ref.shape[0]):
        out_ref[i] = total


def build_matrix(table, high_ref, low_ref):
    hopping, offsets, onsite = table[0:16], table[16:32], table[32:33]
    lane = lax.broadcasted_iota(jnp.int32, (1, 128), 1).astype(F32)
    row_index = lax.broadcasted_iota(jnp.int32, (CHUNK, 128), 0).astype(F32)
    for half in range(2):
        columns = slice(128 * half, 128 * half + 128)
        empty = 640 * (1 - half)
        high_ref[empty : empty + 128, columns] = jnp.zeros((128, 128), BF16)
        low_ref[empty : empty + 128, columns] = jnp.zeros((128, 128), BF16)
        home = lane + float(REACH)
        targets = [
            jnp.broadcast_to(offsets[k : k + 1, columns] + home, (CHUNK, 128)) for k in range(SLOTS)
        ]
        values = [jnp.broadcast_to(hopping[k : k + 1, columns], (CHUNK, 128)) for k in range(SLOTS)]
        homes = jnp.broadcast_to(home, (CHUNK, 128))
        own = jnp.broadcast_to(onsite[:, columns], (CHUNK, 128))

        def chunk(step, carry):
            base = step * CHUNK
            rows = row_index + base.astype(F32)
            total = jnp.where(homes == rows, own, 0.0)
            for k in range(SLOTS):
                total = jnp.where(targets[k] == rows, values[k], total)
            high = total.astype(BF16)
            low = (total - high.astype(F32)).astype(BF16)
            place = pl.ds(pl.multiple_of(base + 128 * half, 128), CHUNK)
            high_ref[place, columns] = high
            low_ref[place, columns] = low
            return carry

        lax.fori_loop(0, (WIDE - 128) // CHUNK, chunk, 0)


def own_matrix_kernel(slab_ref, *refs):
    for core in range(CORES):
        build_matrix(slab_ref[core, OWN:, :], refs[2 * core], refs[2 * core + 1])


def split(value):
    high = value.astype(BF16)
    return high, (value - high.astype(F32)).astype(BF16)


def dot3(high, low, matrix_high, matrix_low):
    def dot(left, right):
        return jnp.dot(left, right, preferred_element_type=F32)

    return dot(high, matrix_high) + (dot(high, matrix_low) + dot(low, matrix_high))


def apply_kernel(
    left_ref, own_ref, right_ref, first_high_ref, first_low_ref, second_high_ref, second_low_ref,
    applied_ref, lead_ref, high_ref, low_ref, once_high_ref, once_low_ref,
    left_high_ref, left_low_ref, right_high_ref, right_low_ref,
):
    build_matrix(left_ref[1, OWN:, :], left_high_ref, left_low_ref)
    build_matrix(right_ref[0, OWN:, :], right_high_ref, right_low_ref)
    sources = [(ref, core) for ref in (left_ref, own_ref, right_ref) for core in range(CORES)]
    for place, (ref, core) in enumerate(sources):
        columns = slice(LOCAL * place, LOCAL * place + LOCAL)
        high, low = split(ref[core, 0:OWN, :])
        high_ref[:, columns] = high
        low_ref[:, columns] = low
    matrices = (
        (left_high_ref, left_low_ref),
        (first_high_ref, first_low_ref),
        (second_high_ref, second_low_ref),
        (right_high_ref, right_low_ref),
    )
    for place, (matrix_high, matrix_low) in enumerate(matrices):
        window = slice(LOCAL * place, LOCAL * place + WIDE)
        columns = slice(LOCAL * place, LOCAL * place + LOCAL)
        once = dot3(high_ref[:, window], low_ref[:, window], matrix_high[...], matrix_low[...])
        high, low = split(once)
        once_high_ref[:, columns] = high
        once_low_ref[:, columns] = low
    for place, (matrix_high, matrix_low) in enumerate(matrices[1:3]):
        window = slice(LOCAL * place, LOCAL * place + WIDE)
        columns = slice(LOCAL * place, LOCAL * place + LOCAL)
        twice = dot3(
            once_high_ref[:, window], once_low_ref[:, window], matrix_high[...], matrix_low[...]
        )
        applied_ref[:, columns] = twice
        lead_ref[:, columns] = twice[0 : 2 * BLOCK]


def head_block(s, core_ref, lead_ref, other_ref):
    place, core = ((0, 0), (0, 1), (BLOCK, 0))[s]
    mine, theirs = lead_ref[place : place + BLOCK, :], other_ref[place : place + BLOCK, :]
    return jnp.where(core_ref[0] == core, mine, theirs)


def gram_kernel(core_ref, lead_ref, other_ref, applied_ref, gram_ref):
    blocks = [head_block(s, core_ref, lead_ref, other_ref) for s in range(STEPS)]
    gram = dot32(jnp.concatenate(blocks, axis=0), applied_ref[...], ((1,), (1,)))
    for part in range(OWN // 128):
        gram_ref[part] = gram[:, 128 * part : 128 * part + 128]


def share_kernel(core_ref, chip_ref, lead_ref, other_ref, applied_ref, *sent_refs):
    count = 1 + len(sent_refs)
    second = core_ref[0] == 1
    head = [head_block(s, core_ref, lead_ref, other_ref) for s in range(STEPS)]
    middle = HALF - BLOCK
    rest = BLOCK - middle
    top = jnp.where(second, head[1][middle:], head[0][0:rest])
    bottom = jnp.where(
        second, head[2], jnp.concatenate([head[0][rest:], head[1][0:middle]], axis=0)
    )
    for step, ref in enumerate(sent_refs):
        ref[0:rest, :] = top
        ref[rest:HALF, :] = bottom
        start = pl.multiple_of(lax.rem(chip_ref[0] + step + 1, count) * BLOCK, BLOCK)
        ref[HALF:, :] = applied_ref[pl.ds(start, BLOCK), :]


def stack_kernel(*refs):
    *got_refs, out_ref = refs
    for step, ref in enumerate(got_refs):
        out_ref[HALF * step : HALF * step + HALF, :] = ref[0:HALF, :]


def spread(value):
    return jnp.broadcast_to(value, (8, 128))


def inverse_factor(pair):
    rows = [pair[8 * i : 8 * i + 8] for i in range(BLOCK // 8)]
    sublane = lax.broadcasted_iota(jnp.int32, (8, 128), 0)
    for p in range(BLOCK // 8):
        start = BLOCK + 8 * p
        columns = [
            [spread(rows[i][:, start + b : start + b + 1]) for b in range(8)]
            for i in range(p, BLOCK // 8)
        ]
        for j in range(8):
            inverse = lax.rsqrt(spread(columns[0][j][j : j + 1]))
            pivot_row = spread(rows[p][j : j + 1]) * inverse
            heads = [spread(columns[0][b][j : j + 1]) * inverse for b in range(j + 1, 8)]
            for i in range(p, BLOCK // 8):
                factor = columns[i - p][j] * inverse
                if i == p:
                    factor = jnp.where(sublane > j, factor, 0.0)
                rows[i] = rows[i] - factor * pivot_row
                for b in range(j + 1, 8):
                    columns[i - p][b] = columns[i - p][b] - factor * heads[b - j - 1]
            rows[p] = jnp.where(sublane == j, pivot_row, rows[p])
    return jnp.concatenate(rows, axis=0)[:, 0:BLOCK]


def dot32(left, right, dims):
    return lax.dot_general(
        left, right, (dims, ((), ())), precision=HIGHEST, preferred_element_type=F32
    )


def finish_kernel(scale, core_ref, chip_ref, gram_ref, *refs):
    lead_ref, other_ref, applied_ref, mate_ref, *got_refs, basis_ref, results, sems = refs
    count = 1 + len(got_refs)
    chip, core = chip_ref[0], core_ref[0]
    second = core == 1
    column = CORES * chip + core
    tiles = gram_ref.shape[0] // 2

    def columns_of(part, core):
        return jnp.concatenate([gram_ref[part * tiles + m, core] for m in range(tiles)], axis=0)

    first_pair, second_pair = columns_of(0, 0), columns_of(0, 1)
    low = jnp.where(second, second_pair, first_pair)
    high = jnp.where(second, columns_of(1, 1), columns_of(1, 0))
    mine = jnp.where(chip >= 2, high, low)
    mine = jnp.where(chip % 2 == 1, pltpu.roll(mine, BLOCK, axis=1), mine)
    full = jnp.concatenate([first_pair, second_pair, mine], axis=1) * scale
    gram = [full[BLOCK * s : BLOCK * s + BLOCK] for s in range(STEPS)]
    places = (0, 2 * BLOCK, BLOCK)
    lane = lax.broadcasted_iota(jnp.int32, (BLOCK, 128), 1)
    row = lax.broadcasted_iota(jnp.int32, (BLOCK, 128), 0)
    identity = jnp.where(lane == row, 1.0, 0.0).astype(F32)
    zero = jnp.zeros((BLOCK, BLOCK), F32)
    for s in range(STEPS):
        unit = [identity[:, 0:BLOCK] if t == s else zero for t in range(STEPS)]
        gram[s] = jnp.concatenate([gram[s], *unit], axis=1)
    couplings = []
    for s in range(STEPS):
        part = places[s] // 128
        tile = gram[s][:, 128 * part : 128 * part + 128]
        if places[s] % 128 == 0:
            tile = pltpu.roll(tile, BLOCK, axis=1)
        inverse = inverse_factor(jnp.where(lane < BLOCK, identity, tile))
        coupling = dot32(inverse, gram[s], ((1,), (0,)))
        for t in range(s + 1, STEPS):
            gram[t] = gram[t] - dot32(
                coupling[:, places[t] : places[t] + BLOCK], coupling, ((0,), (0,))
            )
        couplings.append(coupling)
    follows = column >= STEPS
    units = 6 * BLOCK
    mine = jnp.concatenate([c[:, 4 * BLOCK : 5 * BLOCK] for c in couplings], axis=0)
    inverse = jnp.concatenate([c[:, units:] for c in couplings], axis=0)
    weight = -dot32(mine, inverse, ((0,), (0,)))
    for s in range(STEPS):
        weight = jnp.where(column == s, couplings[s][:, units:], weight)
    parts = split(weight)
    outs = []
    for step in range(count):
        if step == 0:
            head = jnp.concatenate(
                [head_block(s, core_ref, lead_ref, other_ref) for s in range(STEPS)], axis=0
            )
            block = applied_ref[pl.ds(pl.multiple_of(chip * BLOCK, BLOCK), BLOCK), :]
        else:
            got = got_refs[step - 1]
            first, last = got[0:HALF, :], mate_ref[HALF * (step - 1) : HALF * step, :]
            head = jnp.where(
                second,
                jnp.concatenate([last, first], axis=0),
                jnp.concatenate([first, last], axis=0),
            )
            block = got[HALF:, :]
        head_high, head_low = split(head)
        results[step] = jnp.where(follows, block, 0.0) + dot3(*parts, head_high, head_low)
        source = lax.rem(chip + count - step, count)
        columns = pl.ds(pl.multiple_of(source * CHIP, CHIP), CHIP)
        out = pltpu.make_async_copy(results.at[step], basis_ref.at[:, columns], sems.at[step])
        out.start()
        outs.append(out)
    for out in outs:
        out.wait()


def exchange(value, axes):
    return lax.all_to_all(value, axes, split_axis=0, concat_axis=0, tiled=True)


SMEM = pl.BlockSpec(memory_space=pltpu.SMEM)
RAW = pl.BlockSpec(memory_space=pltpu.HBM)


def call(kernel, name, out_shape, inputs, scratch=(), specs=None, out_specs=None):
    single = not isinstance(out_shape, (tuple, list))
    if specs:
        inputs = [
            pltpu.with_memory_space_constraint(value, pltpu.HBM) if spec is RAW else value
            for value, spec in zip(inputs, specs)
        ]
    return pl.pallas_call(
        kernel,
        out_shape=out_shape,
        in_specs=specs or [VMEM] * len(inputs),
        out_specs=out_specs or VMEM if single else (VMEM,) * len(out_shape),
        scratch_shapes=list(scratch),
        compiler_params=PARAMS,
        name=name,
    )(*inputs)


def on_device(vectors, offsets, counts, labels, cosines, distances):
    chips = ("y", "z", "x")
    plane = ("y", "x")
    chip_count = lax.axis_size(chips)
    planes = lax.axis_size(plane)
    depth = lax.axis_size("z")
    count = lax.axis_size("x")

    def shift(value, step):
        return lax.ppermute(value, chips, [(i, (i + step) % chip_count) for i in range(chip_count)])

    shape = jax.ShapeDtypeStruct
    tables = (cosines, distances, offsets, counts.reshape(1, LOCAL), labels)
    slab = call(
        pack_kernel, "pack", shape((CORES, OWN + TABLE, LOCAL), F32), (vectors, *tables),
        [pltpu.VMEM(t.shape, t.dtype) for t in tables]
        + [pltpu.SemaphoreType.DMA((len(tables),)), pltpu.SemaphoreType.DMA((NV // BLOCK,))],
        [RAW] * 6,
    )
    slab = exchange(slab, "core")
    left = shift(slab, 1)
    right = shift(slab, -1)
    matrix = shape((WIDE, LOCAL), BF16)
    matrices = call(own_matrix_kernel, "own_matrix", (matrix,) * 4, (slab,))
    wide = pltpu.VMEM((WIDE, LOCAL), BF16)
    applied, lead = call(
        apply_kernel,
        "apply_twice",
        (shape((OWN, CHIP), F32), shape((2 * BLOCK, CHIP), F32)),
        (left, slab, right, *matrices),
        [pltpu.VMEM((OWN, 3 * CHIP), BF16)] * 2 + [pltpu.VMEM((OWN, 2 * CHIP), BF16)] * 2 + [wide] * 4,
    )
    other = lax.ppermute(lead, "core", [(0, 1), (1, 0)])
    core = lax.axis_index("core").reshape(1)
    chip = lax.axis_index("x").reshape(1)
    gram = call(
        gram_kernel, "gram", shape((OWN // 128, HEAD, 128), F32),
        (core, lead, other, applied), (), [SMEM] + [VMEM] * 3,
    )
    sent = call(
        share_kernel, "share", (shape((HALF + BLOCK, CHIP), F32),) * (count - 1),
        (core, chip, lead, other, applied), (), [SMEM] * 2 + [VMEM] * 3,
    )
    piece = (OWN // 128) * HEAD // planes
    everyone = planes * CORES
    gram = exchange(gram.reshape(planes, piece, 128), plane)
    gram = call(sum_kernel, "sum_plane", shape((depth, piece, 128), F32), (gram,))
    got = [
        lax.ppermute(value, "x", [(i, (i + step + 1) % count) for i in range(count)])
        for step, value in enumerate(sent)
    ]
    stacked = call(stack_kernel, "stack", shape((HALF * (count - 1), CHIP), F32), got)
    theirs = lax.ppermute(stacked, "core", [(0, 1), (1, 0)])
    gram = exchange(gram, "z")
    gram = call(sum_kernel, "sum_depth", shape((everyone, piece, 128), F32), (gram,))
    gram = exchange(gram, (*plane, "core"))
    gram = gram.reshape(planes, CORES, piece, 128)
    scale = 1.0 / (CHIP * chip_count)
    slab_width = CHIP * count
    return call(
        lambda *refs: finish_kernel(scale, *refs), "finish", shape((BLOCK, slab_width), F32),
        (core, chip, gram, lead, other, applied, theirs, *got),
        [pltpu.VMEM((count, BLOCK, CHIP), F32), pltpu.SemaphoreType.DMA((count,))],
        [SMEM] * 2 + [VMEM] * (4 + count), RAW,
    )


def solution(mesh):
    rows = mesh.shape["rows"]
    cols = mesh.shape["cols"]
    names = ("y", "z", "x", "core")
    cube = Mesh(mesh.devices.reshape(Y_SIZE, rows // Y_SIZE, cols // CORES, CORES), names)
    whole = P(None, names)
    placed = (whole, whole, P(names), whole, whole, whole)
    return jax.shard_map(
        on_device, mesh=cube, in_specs=placed, out_specs=P(("x", "core"), ("y", "z")),
        check_vma=False,
    )
```

```python
import jax
import jax.numpy as jnp
from jax import lax
from jax.experimental import pallas as pl
from jax.experimental.pallas import tpu as pltpu
from jax.sharding import Mesh, PartitionSpec as P

PI_BOND = -1.0
SIGMA_BOND = 0.178
DECAY_LENGTH = 0.319
LAYER_GAP = 2.36
SITE_MASS = 0.4
LAYER_BIAS = 0.25

BLOCK = 64
STEPS = 3
HEAD = BLOCK * STEPS
SLOTS = 16
REACH = 256
NV = 512
LOCAL = 256
WIDE = LOCAL + 2 * REACH
CHUNK = 128
Y_SIZE = 4
CORES = 2
OWN = NV // CORES
TABLE = 40
HALF = HEAD // CORES
CHIP = CORES * LOCAL
F32 = jnp.float32
BF16 = jnp.bfloat16
HIGHEST = lax.Precision.HIGHEST
VMEM = pl.BlockSpec(memory_space=pltpu.VMEM)
PARAMS = pltpu.CompilerParams(vmem_limit_bytes=48 * 1024 * 1024)


def pack_kernel(
    vectors_ref, cosines_ref, distances_ref, offsets_ref, counts_ref, labels_ref, out_ref,
    cosines, distances, offsets, counts, labels, table_sems, block_sems,
):
    tables = (
        (cosines_ref, cosines), (distances_ref, distances), (offsets_ref, offsets),
        (counts_ref, counts), (labels_ref, labels),
    )
    table_copies = [
        pltpu.make_async_copy(source, target, table_sems.at[i])
        for i, (source, target) in enumerate(tables)
    ]
    block_copies = [
        pltpu.make_async_copy(
            vectors_ref.at[pl.ds(BLOCK * (core + CORES * p), BLOCK)],
            out_ref.at[core, pl.ds(BLOCK * p, BLOCK)],
            block_sems.at[core + CORES * p],
        )
        for core in range(CORES)
        for p in range(OWN // BLOCK)
    ]
    for copy in table_copies + block_copies:
        copy.start()
    for copy in table_copies:
        copy.wait()
    square = cosines[...] * cosines[...]
    bond = PI_BOND * jnp.exp(-(distances[...] - 1.0) / DECAY_LENGTH) * (1.0 - square)
    bond = bond + SIGMA_BOND * jnp.exp(-(distances[...] - LAYER_GAP) / DECAY_LENGTH) * square
    slot = lax.broadcasted_iota(jnp.int32, bond.shape, 0)
    hopping = jnp.where(slot < counts[...], bond, 0.0)
    steps = offsets[...].astype(F32)
    merged = jnp.zeros_like(hopping)
    for k in range(SLOTS):
        merged = merged + jnp.where(steps == steps[k : k + 1], hopping[k : k + 1], 0.0)
    sides = labels[...].astype(F32)
    onsite = SITE_MASS * (2.0 * sides[0:1] - 1.0) + LAYER_BIAS * (2.0 * sides[1:2] - 1.0)
    for core in range(CORES):
        out_ref[core, OWN : OWN + 16, :] = merged
        out_ref[core, OWN + 16 : OWN + 32, :] = steps
        out_ref[core, OWN + 32 : OWN + 40, :] = jnp.broadcast_to(onsite, (8, LOCAL))
    for copy in block_copies:
        copy.wait()


def sum_kernel(pieces_ref, out_ref):
    total = pieces_ref[0]
    for i in range(1, pieces_ref.shape[0]):
        total = total + pieces_ref[i]
    for i in range(out_ref.shape[0]):
        out_ref[i] = total


def build_matrix(table, high_ref, low_ref):
    hopping, offsets, onsite = table[0:16], table[16:32], table[32:33]
    lane = lax.broadcasted_iota(jnp.int32, (1, 128), 1).astype(F32)
    row_index = lax.broadcasted_iota(jnp.int32, (CHUNK, 128), 0).astype(F32)
    for half in range(2):
        columns = slice(128 * half, 128 * half + 128)
        empty = 640 * (1 - half)
        high_ref[empty : empty + 128, columns] = jnp.zeros((128, 128), BF16)
        low_ref[empty : empty + 128, columns] = jnp.zeros((128, 128), BF16)
        home = lane + float(REACH)
        targets = [
            jnp.broadcast_to(offsets[k : k + 1, columns] + home, (CHUNK, 128)) for k in range(SLOTS)
        ]
        values = [jnp.broadcast_to(hopping[k : k + 1, columns], (CHUNK, 128)) for k in range(SLOTS)]
        homes = jnp.broadcast_to(home, (CHUNK, 128))
        own = jnp.broadcast_to(onsite[:, columns], (CHUNK, 128))

        def chunk(step, carry):
            base = step * CHUNK
            rows = row_index + base.astype(F32)
            total = jnp.where(homes == rows, own, 0.0)
            for k in range(SLOTS):
                total = jnp.where(targets[k] == rows, values[k], total)
            high = total.astype(BF16)
            low = (total - high.astype(F32)).astype(BF16)
            place = pl.ds(pl.multiple_of(base + 128 * half, 128), CHUNK)
            high_ref[place, columns] = high
            low_ref[place, columns] = low
            return carry

        lax.fori_loop(0, (WIDE - 128) // CHUNK, chunk, 0)


def own_matrix_kernel(slab_ref, *refs):
    for core in range(CORES):
        build_matrix(slab_ref[core, OWN:, :], refs[2 * core], refs[2 * core + 1])


def split(value):
    high = value.astype(BF16)
    return high, (value - high.astype(F32)).astype(BF16)


def dot3(high, low, matrix_high, matrix_low):
    def dot(left, right):
        return jnp.dot(left, right, preferred_element_type=F32)

    return dot(high, matrix_high) + (dot(high, matrix_low) + dot(low, matrix_high))


def apply_kernel(
    left_ref, own_ref, right_ref, first_high_ref, first_low_ref, second_high_ref, second_low_ref,
    applied_ref, lead_ref, high_ref, low_ref, once_high_ref, once_low_ref,
    left_high_ref, left_low_ref, right_high_ref, right_low_ref,
):
    build_matrix(left_ref[1, OWN:, :], left_high_ref, left_low_ref)
    build_matrix(right_ref[0, OWN:, :], right_high_ref, right_low_ref)
    sources = [(ref, core) for ref in (left_ref, own_ref, right_ref) for core in range(CORES)]
    for place, (ref, core) in enumerate(sources):
        columns = slice(LOCAL * place, LOCAL * place + LOCAL)
        high, low = split(ref[core, 0:OWN, :])
        high_ref[:, columns] = high
        low_ref[:, columns] = low
    matrices = (
        (left_high_ref, left_low_ref),
        (first_high_ref, first_low_ref),
        (second_high_ref, second_low_ref),
        (right_high_ref, right_low_ref),
    )
    for place, (matrix_high, matrix_low) in enumerate(matrices):
        window = slice(LOCAL * place, LOCAL * place + WIDE)
        columns = slice(LOCAL * place, LOCAL * place + LOCAL)
        once = dot3(high_ref[:, window], low_ref[:, window], matrix_high[...], matrix_low[...])
        high, low = split(once)
        once_high_ref[:, columns] = high
        once_low_ref[:, columns] = low
    for place, (matrix_high, matrix_low) in enumerate(matrices[1:3]):
        window = slice(LOCAL * place, LOCAL * place + WIDE)
        columns = slice(LOCAL * place, LOCAL * place + LOCAL)
        twice = dot3(
            once_high_ref[:, window], once_low_ref[:, window], matrix_high[...], matrix_low[...]
        )
        applied_ref[:, columns] = twice
        lead_ref[:, columns] = twice[0 : 2 * BLOCK]


def head_block(s, core_ref, lead_ref, other_ref):
    place, core = ((0, 0), (0, 1), (BLOCK, 0))[s]
    mine, theirs = lead_ref[place : place + BLOCK, :], other_ref[place : place + BLOCK, :]
    return jnp.where(core_ref[0] == core, mine, theirs)


def gram_kernel(core_ref, lead_ref, other_ref, applied_ref, gram_ref):
    blocks = [head_block(s, core_ref, lead_ref, other_ref) for s in range(STEPS)]
    gram = dot32(jnp.concatenate(blocks, axis=0), applied_ref[...], ((1,), (1,)))
    for part in range(OWN // 128):
        gram_ref[part] = gram[:, 128 * part : 128 * part + 128]


def share_kernel(core_ref, chip_ref, lead_ref, other_ref, applied_ref, home_ref, *sent_refs):
    count = 1 + len(sent_refs)
    second = core_ref[0] == 1
    head = [head_block(s, core_ref, lead_ref, other_ref) for s in range(STEPS)]
    for s in range(STEPS):
        home_ref[BLOCK * s : BLOCK * s + BLOCK, :] = head[s]
    middle = HALF - BLOCK
    half = (
        jnp.where(second, head[1][middle:], head[0][0 : BLOCK - middle]),
        jnp.where(second, head[2][0:BLOCK], jnp.concatenate(
            [head[0][BLOCK - middle :], head[1][0:middle]], axis=0)),
    )
    for ref in sent_refs:
        ref[0 : BLOCK - middle, :] = half[0]
        ref[BLOCK - middle : HALF, :] = half[1]
    for step, ref in enumerate((home_ref, *sent_refs)):
        start = pl.multiple_of(lax.rem(chip_ref[0] + step, count) * BLOCK, BLOCK)
        ref[ref.shape[0] - BLOCK :, :] = applied_ref[pl.ds(start, BLOCK), :]


def stack_kernel(one_ref, two_ref, three_ref, first_ref, last_ref):
    middle = HALF // 2
    first_ref[0:HALF, :] = one_ref[0:HALF, :]
    first_ref[HALF:, :] = two_ref[0:middle, :]
    last_ref[0:middle, :] = two_ref[middle:HALF, :]
    last_ref[middle:, :] = three_ref[0:HALF, :]


def spread(value):
    return jnp.broadcast_to(value, (8, 128))


def inverse_factor(pair):
    rows = [pair[8 * i : 8 * i + 8] for i in range(BLOCK // 8)]
    sublane = lax.broadcasted_iota(jnp.int32, (8, 128), 0)
    for p in range(BLOCK // 8):
        start = BLOCK + 8 * p
        columns = [
            [spread(rows[i][:, start + b : start + b + 1]) for b in range(8)]
            for i in range(p, BLOCK // 8)
        ]
        for j in range(8):
            inverse = lax.rsqrt(spread(columns[0][j][j : j + 1]))
            pivot_row = spread(rows[p][j : j + 1]) * inverse
            heads = [spread(columns[0][b][j : j + 1]) * inverse for b in range(j + 1, 8)]
            for i in range(p, BLOCK // 8):
                factor = columns[i - p][j] * inverse
                if i == p:
                    factor = jnp.where(sublane > j, factor, 0.0)
                rows[i] = rows[i] - factor * pivot_row
                for b in range(j + 1, 8):
                    columns[i - p][b] = columns[i - p][b] - factor * heads[b - j - 1]
            rows[p] = jnp.where(sublane == j, pivot_row, rows[p])
    return jnp.concatenate(rows, axis=0)[:, 0:BLOCK]


def dot32(left, right, dims):
    return lax.dot_general(
        left, right, (dims, ((), ())), precision=HIGHEST, preferred_element_type=F32
    )


def finish_kernel(scale, core_ref, chip_ref, gram_ref, *refs):
    home_ref, mate_ref, mate_last_ref, *got_refs, basis_ref, results, sems = refs
    count = 1 + len(got_refs)
    middle = HALF // 2
    mates = (
        lambda: mate_ref[0:HALF, :],
        lambda: jnp.concatenate([mate_ref[HALF:, :], mate_last_ref[0:middle, :]], axis=0),
        lambda: mate_last_ref[middle:, :],
    )
    chip, core = chip_ref[0], core_ref[0]
    second = core == 1
    column = CORES * chip + core
    tiles = gram_ref.shape[0] // 2

    def columns_of(part, core):
        return jnp.concatenate([gram_ref[part * tiles + m, core] for m in range(tiles)], axis=0)

    first_pair, second_pair = columns_of(0, 0), columns_of(0, 1)
    low = jnp.where(second, second_pair, first_pair)
    high = jnp.where(second, columns_of(1, 1), columns_of(1, 0))
    mine = jnp.where(chip >= 2, high, low)
    mine = jnp.where(chip % 2 == 1, pltpu.roll(mine, BLOCK, axis=1), mine)
    full = jnp.concatenate([first_pair, second_pair, mine], axis=1) * scale
    gram = [full[BLOCK * s : BLOCK * s + BLOCK] for s in range(STEPS)]
    places = (0, 2 * BLOCK, BLOCK)
    lane = lax.broadcasted_iota(jnp.int32, (BLOCK, 128), 1)
    row = lax.broadcasted_iota(jnp.int32, (BLOCK, 128), 0)
    identity = jnp.where(lane == row, 1.0, 0.0).astype(F32)
    zero = jnp.zeros((BLOCK, BLOCK), F32)
    for s in range(STEPS):
        unit = [identity[:, 0:BLOCK] if t == s else zero for t in range(STEPS)]
        gram[s] = jnp.concatenate([gram[s], *unit], axis=1)
    couplings = []
    for s in range(STEPS):
        part = places[s] // 128
        tile = gram[s][:, 128 * part : 128 * part + 128]
        if places[s] % 128 == 0:
            tile = pltpu.roll(tile, BLOCK, axis=1)
        inverse = inverse_factor(jnp.where(lane < BLOCK, identity, tile))
        coupling = dot32(inverse, gram[s], ((1,), (0,)))
        for t in range(s + 1, STEPS):
            gram[t] = gram[t] - dot32(
                coupling[:, places[t] : places[t] + BLOCK], coupling, ((0,), (0,))
            )
        couplings.append(coupling)
    follows = column >= STEPS
    units = 6 * BLOCK
    mine = jnp.concatenate([c[:, 4 * BLOCK : 5 * BLOCK] for c in couplings], axis=0)
    inverse = jnp.concatenate([c[:, units:] for c in couplings], axis=0)
    weight = -dot32(mine, inverse, ((0,), (0,)))
    for s in range(STEPS):
        weight = jnp.where(column == s, couplings[s][:, units:], weight)
    parts = split(weight)
    outs = []
    for step in range(count):
        if step == 0:
            head, block = home_ref[0:HEAD, :], home_ref[HEAD:, :]
        else:
            got = got_refs[step - 1]
            first, last = got[0:HALF, :], mates[step - 1]()
            head = jnp.where(
                second,
                jnp.concatenate([last, first], axis=0),
                jnp.concatenate([first, last], axis=0),
            )
            block = got[HALF:, :]
        head_high, head_low = split(head)
        results[step] = jnp.where(follows, block, 0.0) + dot3(*parts, head_high, head_low)
        source = lax.rem(chip + count - step, count)
        columns = pl.ds(pl.multiple_of(source * CHIP, CHIP), CHIP)
        out = pltpu.make_async_copy(results.at[step], basis_ref.at[:, columns], sems.at[step])
        out.start()
        outs.append(out)
    for out in outs:
        out.wait()


def exchange(value, axes):
    return lax.all_to_all(value, axes, split_axis=0, concat_axis=0, tiled=True)


SMEM = pl.BlockSpec(memory_space=pltpu.SMEM)
RAW = pl.BlockSpec(memory_space=pltpu.HBM)


def call(kernel, name, out_shape, inputs, scratch=(), specs=None, out_specs=None):
    single = not isinstance(out_shape, (tuple, list))
    if specs:
        inputs = [
            pltpu.with_memory_space_constraint(value, pltpu.HBM) if spec is RAW else value
            for value, spec in zip(inputs, specs)
        ]
    return pl.pallas_call(
        kernel,
        out_shape=out_shape,
        in_specs=specs or [VMEM] * len(inputs),
        out_specs=out_specs or VMEM if single else (VMEM,) * len(out_shape),
        scratch_shapes=list(scratch),
        compiler_params=PARAMS,
        name=name,
    )(*inputs)


def on_device(vectors, offsets, counts, labels, cosines, distances):
    chips = ("y", "z", "x")
    plane = ("y", "x")
    chip_count = lax.axis_size(chips)
    planes = lax.axis_size(plane)
    depth = lax.axis_size("z")
    count = lax.axis_size("x")

    def shift(value, step):
        return lax.ppermute(value, chips, [(i, (i + step) % chip_count) for i in range(chip_count)])

    shape = jax.ShapeDtypeStruct
    tables = (cosines, distances, offsets, counts.reshape(1, LOCAL), labels)
    slab = call(
        pack_kernel, "pack", shape((CORES, OWN + TABLE, LOCAL), F32), (vectors, *tables),
        [pltpu.VMEM(t.shape, t.dtype) for t in tables]
        + [pltpu.SemaphoreType.DMA((len(tables),)), pltpu.SemaphoreType.DMA((NV // BLOCK,))],
        [RAW] * 6,
    )
    slab = exchange(slab, "core")
    left = shift(slab, 1)
    right = shift(slab, -1)
    matrix = shape((WIDE, LOCAL), BF16)
    matrices = call(own_matrix_kernel, "own_matrix", (matrix,) * 4, (slab,))
    wide = pltpu.VMEM((WIDE, LOCAL), BF16)
    applied, lead = call(
        apply_kernel,
        "apply_twice",
        (shape((OWN, CHIP), F32), shape((2 * BLOCK, CHIP), F32)),
        (left, slab, right, *matrices),
        [pltpu.VMEM((OWN, 3 * CHIP), BF16)] * 2 + [pltpu.VMEM((OWN, 2 * CHIP), BF16)] * 2 + [wide] * 4,
    )
    other = lax.ppermute(lead, "core", [(0, 1), (1, 0)])
    core = lax.axis_index("core").reshape(1)
    chip = lax.axis_index("x").reshape(1)
    gram = call(
        gram_kernel, "gram", shape((OWN // 128, HEAD, 128), F32),
        (core, lead, other, applied), (), [SMEM] + [VMEM] * 3,
    )
    home, *sent = call(
        share_kernel, "share",
        (shape((HEAD + BLOCK, CHIP), F32),) + (shape((HALF + BLOCK, CHIP), F32),) * (count - 1),
        (core, chip, lead, other, applied), (), [SMEM] * 2 + [VMEM] * 3,
    )
    piece = (OWN // 128) * HEAD // planes
    everyone = planes * CORES
    gram = exchange(gram.reshape(planes, piece, 128), plane)
    gram = call(sum_kernel, "sum_plane", shape((depth, piece, 128), F32), (gram,))
    got = [
        lax.ppermute(value, "x", [(i, (i + step + 1) % count) for i in range(count)])
        for step, value in enumerate(sent)
    ]
    gram = exchange(gram, "z")
    gram = call(sum_kernel, "sum_depth", shape((everyone, piece, 128), F32), (gram,))
    _, *ready = lax.optimization_barrier((gram, *got))
    stacked = call(
        stack_kernel, "stack", (shape((HALF * (count - 1) // 2, CHIP), F32),) * 2, ready
    )
    theirs = [lax.ppermute(value, "core", [(0, 1), (1, 0)]) for value in stacked]
    gram = exchange(gram, (*plane, "core"))
    gram = gram.reshape(planes, CORES, piece, 128)
    scale = 1.0 / (CHIP * chip_count)
    slab_width = CHIP * count
    return call(
        lambda *refs: finish_kernel(scale, *refs), "finish", shape((BLOCK, slab_width), F32),
        (core, chip, gram, home, *theirs, *got),
        [pltpu.VMEM((count, BLOCK, CHIP), F32), pltpu.SemaphoreType.DMA((count,))],
        [SMEM] * 2 + [VMEM] * (3 + count), RAW,
    )


def solution(mesh):
    rows = mesh.shape["rows"]
    cols = mesh.shape["cols"]
    names = ("y", "z", "x", "core")
    cube = Mesh(mesh.devices.reshape(Y_SIZE, rows // Y_SIZE, cols // CORES, CORES), names)
    whole = P(None, names)
    placed = (whole, whole, P(names), whole, whole, whole)
    return jax.shard_map(
        on_device, mesh=cube, in_specs=placed, out_specs=P(("x", "core"), ("y", "z")),
        check_vma=False,
    )
```

```python
import jax
import jax.numpy as jnp
from jax import lax
from jax.experimental import pallas as pl
from jax.experimental.pallas import tpu as pltpu
from jax.sharding import Mesh, PartitionSpec as P

PI_BOND = -1.0
SIGMA_BOND = 0.178
DECAY_LENGTH = 0.319
LAYER_GAP = 2.36
SITE_MASS = 0.4
LAYER_BIAS = 0.25

BLOCK = 64
STEPS = 3
HEAD = BLOCK * STEPS
SLOTS = 16
REACH = 256
NV = 512
LOCAL = 256
WIDE = LOCAL + 2 * REACH
CHUNK = 128
Y_SIZE = 4
CORES = 2
OWN = NV // CORES
TABLE = 40
HALF = HEAD // CORES
CHIP = CORES * LOCAL
F32 = jnp.float32
BF16 = jnp.bfloat16
HIGHEST = lax.Precision.HIGHEST
VMEM = pl.BlockSpec(memory_space=pltpu.VMEM)
PARAMS = pltpu.CompilerParams(vmem_limit_bytes=48 * 1024 * 1024)


def pack_kernel(
    core_ref, vectors_ref, cosines_ref, distances_ref, offsets_ref, counts_ref, labels_ref,
    own_ref, send_ref, cosines, distances, offsets, counts, labels, table_sems, block_sems,
):
    tables = (
        (cosines_ref, cosines), (distances_ref, distances), (offsets_ref, offsets),
        (counts_ref, counts), (labels_ref, labels),
    )
    table_copies = [
        pltpu.make_async_copy(source, target, table_sems.at[i])
        for i, (source, target) in enumerate(tables)
    ]
    block_copies = []
    for owner, ref in ((core_ref[0], own_ref), (1 - core_ref[0], send_ref)):
        for p in range(OWN // BLOCK):
            start = pl.multiple_of((owner + CORES * p) * BLOCK, BLOCK)
            block_copies.append(
                pltpu.make_async_copy(
                    vectors_ref.at[pl.ds(start, BLOCK)],
                    ref.at[pl.ds(BLOCK * p, BLOCK)],
                    block_sems.at[len(block_copies)],
                )
            )
    for copy in table_copies + block_copies:
        copy.start()
    for copy in table_copies:
        copy.wait()
    square = cosines[...] * cosines[...]
    bond = PI_BOND * jnp.exp(-(distances[...] - 1.0) / DECAY_LENGTH) * (1.0 - square)
    bond = bond + SIGMA_BOND * jnp.exp(-(distances[...] - LAYER_GAP) / DECAY_LENGTH) * square
    slot = lax.broadcasted_iota(jnp.int32, bond.shape, 0)
    hopping = jnp.where(slot < counts[...], bond, 0.0)
    steps = offsets[...].astype(F32)
    merged = jnp.zeros_like(hopping)
    for k in range(SLOTS):
        merged = merged + jnp.where(steps == steps[k : k + 1], hopping[k : k + 1], 0.0)
    sides = labels[...].astype(F32)
    onsite = SITE_MASS * (2.0 * sides[0:1] - 1.0) + LAYER_BIAS * (2.0 * sides[1:2] - 1.0)
    for ref in (own_ref, send_ref):
        ref[OWN : OWN + 16, :] = merged
        ref[OWN + 16 : OWN + 32, :] = steps
        ref[OWN + 32 : OWN + 40, :] = jnp.broadcast_to(onsite, (8, LOCAL))
    for copy in block_copies:
        copy.wait()


def merge_kernel(core_ref, own_ref, mate_ref, slab_ref):
    slab_ref[core_ref[0]] = own_ref[...]
    slab_ref[1 - core_ref[0]] = mate_ref[...]


def sum_kernel(pieces_ref, out_ref):
    total = pieces_ref[0]
    for i in range(1, pieces_ref.shape[0]):
        total = total + pieces_ref[i]
    for i in range(out_ref.shape[0]):
        out_ref[i] = total


def build_matrix(table, high_ref, low_ref):
    hopping, offsets, onsite = table[0:16], table[16:32], table[32:33]
    lane = lax.broadcasted_iota(jnp.int32, (1, 128), 1).astype(F32)
    row_index = lax.broadcasted_iota(jnp.int32, (CHUNK, 128), 0).astype(F32)
    for half in range(2):
        columns = slice(128 * half, 128 * half + 128)
        empty = 640 * (1 - half)
        high_ref[empty : empty + 128, columns] = jnp.zeros((128, 128), BF16)
        low_ref[empty : empty + 128, columns] = jnp.zeros((128, 128), BF16)
        home = lane + float(REACH)
        targets = [
            jnp.broadcast_to(offsets[k : k + 1, columns] + home, (CHUNK, 128)) for k in range(SLOTS)
        ]
        values = [jnp.broadcast_to(hopping[k : k + 1, columns], (CHUNK, 128)) for k in range(SLOTS)]
        homes = jnp.broadcast_to(home, (CHUNK, 128))
        own = jnp.broadcast_to(onsite[:, columns], (CHUNK, 128))

        def chunk(step, carry):
            base = step * CHUNK
            rows = row_index + base.astype(F32)
            total = jnp.where(homes == rows, own, 0.0)
            for k in range(SLOTS):
                total = jnp.where(targets[k] == rows, values[k], total)
            high = total.astype(BF16)
            low = (total - high.astype(F32)).astype(BF16)
            place = pl.ds(pl.multiple_of(base + 128 * half, 128), CHUNK)
            high_ref[place, columns] = high
            low_ref[place, columns] = low
            return carry

        lax.fori_loop(0, (WIDE - 128) // CHUNK, chunk, 0)


def own_matrix_kernel(slab_ref, *refs):
    for core in range(CORES):
        build_matrix(slab_ref[core, OWN:, :], refs[2 * core], refs[2 * core + 1])


def split(value):
    high = value.astype(BF16)
    return high, (value - high.astype(F32)).astype(BF16)


def dot3(high, low, matrix_high, matrix_low):
    def dot(left, right):
        return jnp.dot(left, right, preferred_element_type=F32)

    return dot(high, matrix_high) + (dot(high, matrix_low) + dot(low, matrix_high))


def apply_kernel(
    left_ref, own_ref, right_ref, first_high_ref, first_low_ref, second_high_ref, second_low_ref,
    applied_ref, lead_ref, high_ref, low_ref, once_high_ref, once_low_ref,
    left_high_ref, left_low_ref, right_high_ref, right_low_ref,
):
    build_matrix(left_ref[1, OWN:, :], left_high_ref, left_low_ref)
    build_matrix(right_ref[0, OWN:, :], right_high_ref, right_low_ref)
    sources = [(ref, core) for ref in (left_ref, own_ref, right_ref) for core in range(CORES)]
    for place, (ref, core) in enumerate(sources):
        columns = slice(LOCAL * place, LOCAL * place + LOCAL)
        high, low = split(ref[core, 0:OWN, :])
        high_ref[:, columns] = high
        low_ref[:, columns] = low
    matrices = (
        (left_high_ref, left_low_ref),
        (first_high_ref, first_low_ref),
        (second_high_ref, second_low_ref),
        (right_high_ref, right_low_ref),
    )
    for place, (matrix_high, matrix_low) in enumerate(matrices):
        window = slice(LOCAL * place, LOCAL * place + WIDE)
        columns = slice(LOCAL * place, LOCAL * place + LOCAL)
        once = dot3(high_ref[:, window], low_ref[:, window], matrix_high[...], matrix_low[...])
        high, low = split(once)
        once_high_ref[:, columns] = high
        once_low_ref[:, columns] = low
    for place, (matrix_high, matrix_low) in enumerate(matrices[1:3]):
        window = slice(LOCAL * place, LOCAL * place + WIDE)
        columns = slice(LOCAL * place, LOCAL * place + LOCAL)
        twice = dot3(
            once_high_ref[:, window], once_low_ref[:, window], matrix_high[...], matrix_low[...]
        )
        applied_ref[:, columns] = twice
        lead_ref[:, columns] = twice[0 : 2 * BLOCK]


def head_block(s, core_ref, lead_ref, other_ref):
    place, core = ((0, 0), (0, 1), (BLOCK, 0))[s]
    mine, theirs = lead_ref[place : place + BLOCK, :], other_ref[place : place + BLOCK, :]
    return jnp.where(core_ref[0] == core, mine, theirs)


def gram_kernel(core_ref, lead_ref, other_ref, applied_ref, gram_ref):
    blocks = [head_block(s, core_ref, lead_ref, other_ref) for s in range(STEPS)]
    gram = dot32(jnp.concatenate(blocks, axis=0), applied_ref[...], ((1,), (1,)))
    for part in range(OWN // 128):
        gram_ref[part] = gram[:, 128 * part : 128 * part + 128]


def share_kernel(core_ref, chip_ref, lead_ref, other_ref, applied_ref, home_ref, *sent_refs):
    count = 1 + len(sent_refs)
    second = core_ref[0] == 1
    head = [head_block(s, core_ref, lead_ref, other_ref) for s in range(STEPS)]
    for s in range(STEPS):
        home_ref[BLOCK * s : BLOCK * s + BLOCK, :] = head[s]
    middle = HALF - BLOCK
    half = (
        jnp.where(second, head[1][middle:], head[0][0 : BLOCK - middle]),
        jnp.where(second, head[2][0:BLOCK], jnp.concatenate(
            [head[0][BLOCK - middle :], head[1][0:middle]], axis=0)),
    )
    for ref in sent_refs:
        ref[0 : BLOCK - middle, :] = half[0]
        ref[BLOCK - middle : HALF, :] = half[1]
    for step, ref in enumerate((home_ref, *sent_refs)):
        start = pl.multiple_of(lax.rem(chip_ref[0] + step, count) * BLOCK, BLOCK)
        ref[ref.shape[0] - BLOCK :, :] = applied_ref[pl.ds(start, BLOCK), :]


def stack_kernel(one_ref, two_ref, three_ref, first_ref, last_ref):
    middle = HALF // 2
    first_ref[0:HALF, :] = one_ref[0:HALF, :]
    first_ref[HALF:, :] = two_ref[0:middle, :]
    last_ref[0:middle, :] = two_ref[middle:HALF, :]
    last_ref[middle:, :] = three_ref[0:HALF, :]


def spread(value):
    return jnp.broadcast_to(value, (8, 128))


def inverse_factor(pair):
    rows = [pair[8 * i : 8 * i + 8] for i in range(BLOCK // 8)]
    sublane = lax.broadcasted_iota(jnp.int32, (8, 128), 0)
    for p in range(BLOCK // 8):
        start = BLOCK + 8 * p
        columns = [
            [spread(rows[i][:, start + b : start + b + 1]) for b in range(8)]
            for i in range(p, BLOCK // 8)
        ]
        for j in range(8):
            inverse = lax.rsqrt(spread(columns[0][j][j : j + 1]))
            pivot_row = spread(rows[p][j : j + 1]) * inverse
            heads = [spread(columns[0][b][j : j + 1]) * inverse for b in range(j + 1, 8)]
            for i in range(p, BLOCK // 8):
                factor = columns[i - p][j] * inverse
                if i == p:
                    factor = jnp.where(sublane > j, factor, 0.0)
                rows[i] = rows[i] - factor * pivot_row
                for b in range(j + 1, 8):
                    columns[i - p][b] = columns[i - p][b] - factor * heads[b - j - 1]
            rows[p] = jnp.where(sublane == j, pivot_row, rows[p])
    return jnp.concatenate(rows, axis=0)[:, 0:BLOCK]


def dot32(left, right, dims):
    return lax.dot_general(
        left, right, (dims, ((), ())), precision=HIGHEST, preferred_element_type=F32
    )


def finish_kernel(scale, core_ref, chip_ref, gram_ref, *refs):
    home_ref, mate_ref, mate_last_ref, *got_refs, basis_ref, results, sems = refs
    count = 1 + len(got_refs)
    middle = HALF // 2
    mates = (
        lambda: mate_ref[0:HALF, :],
        lambda: jnp.concatenate([mate_ref[HALF:, :], mate_last_ref[0:middle, :]], axis=0),
        lambda: mate_last_ref[middle:, :],
    )
    chip, core = chip_ref[0], core_ref[0]
    second = core == 1
    column = CORES * chip + core
    tiles = gram_ref.shape[0] // 2

    def columns_of(part, core):
        return jnp.concatenate([gram_ref[part * tiles + m, core] for m in range(tiles)], axis=0)

    first_pair, second_pair = columns_of(0, 0), columns_of(0, 1)
    low = jnp.where(second, second_pair, first_pair)
    high = jnp.where(second, columns_of(1, 1), columns_of(1, 0))
    mine = jnp.where(chip >= 2, high, low)
    mine = jnp.where(chip % 2 == 1, pltpu.roll(mine, BLOCK, axis=1), mine)
    full = jnp.concatenate([first_pair, second_pair, mine], axis=1) * scale
    gram = [full[BLOCK * s : BLOCK * s + BLOCK] for s in range(STEPS)]
    places = (0, 2 * BLOCK, BLOCK)
    lane = lax.broadcasted_iota(jnp.int32, (BLOCK, 128), 1)
    row = lax.broadcasted_iota(jnp.int32, (BLOCK, 128), 0)
    identity = jnp.where(lane == row, 1.0, 0.0).astype(F32)
    zero = jnp.zeros((BLOCK, BLOCK), F32)
    for s in range(STEPS):
        unit = [identity[:, 0:BLOCK] if t == s else zero for t in range(STEPS)]
        gram[s] = jnp.concatenate([gram[s], *unit], axis=1)
    couplings = []
    for s in range(STEPS):
        part = places[s] // 128
        tile = gram[s][:, 128 * part : 128 * part + 128]
        if places[s] % 128 == 0:
            tile = pltpu.roll(tile, BLOCK, axis=1)
        inverse = inverse_factor(jnp.where(lane < BLOCK, identity, tile))
        coupling = dot32(inverse, gram[s], ((1,), (0,)))
        for t in range(s + 1, STEPS):
            gram[t] = gram[t] - dot32(
                coupling[:, places[t] : places[t] + BLOCK], coupling, ((0,), (0,))
            )
        couplings.append(coupling)
    follows = column >= STEPS
    units = 6 * BLOCK
    mine = jnp.concatenate([c[:, 4 * BLOCK : 5 * BLOCK] for c in couplings], axis=0)
    inverse = jnp.concatenate([c[:, units:] for c in couplings], axis=0)
    weight = -dot32(mine, inverse, ((0,), (0,)))
    for s in range(STEPS):
        weight = jnp.where(column == s, couplings[s][:, units:], weight)
    parts = split(weight)
    outs = []
    for step in range(count):
        if step == 0:
            head, block = home_ref[0:HEAD, :], home_ref[HEAD:, :]
        else:
            got = got_refs[step - 1]
            first, last = got[0:HALF, :], mates[step - 1]()
            head = jnp.where(
                second,
                jnp.concatenate([last, first], axis=0),
                jnp.concatenate([first, last], axis=0),
            )
            block = got[HALF:, :]
        head_high, head_low = split(head)
        results[step] = jnp.where(follows, block, 0.0) + dot3(*parts, head_high, head_low)
        source = lax.rem(chip + count - step, count)
        columns = pl.ds(pl.multiple_of(source * CHIP, CHIP), CHIP)
        out = pltpu.make_async_copy(results.at[step], basis_ref.at[:, columns], sems.at[step])
        out.start()
        outs.append(out)
    for out in outs:
        out.wait()


def exchange(value, axes):
    return lax.all_to_all(value, axes, split_axis=0, concat_axis=0, tiled=True)


SMEM = pl.BlockSpec(memory_space=pltpu.SMEM)
RAW = pl.BlockSpec(memory_space=pltpu.HBM)


def call(kernel, name, out_shape, inputs, scratch=(), specs=None, out_specs=None):
    single = not isinstance(out_shape, (tuple, list))
    if specs:
        inputs = [
            pltpu.with_memory_space_constraint(value, pltpu.HBM) if spec is RAW else value
            for value, spec in zip(inputs, specs)
        ]
    return pl.pallas_call(
        kernel,
        out_shape=out_shape,
        in_specs=specs or [VMEM] * len(inputs),
        out_specs=out_specs or VMEM if single else (VMEM,) * len(out_shape),
        scratch_shapes=list(scratch),
        compiler_params=PARAMS,
        name=name,
    )(*inputs)


def on_device(vectors, offsets, counts, labels, cosines, distances):
    chips = ("y", "z", "x")
    plane = ("y", "x")
    chip_count = lax.axis_size(chips)
    planes = lax.axis_size(plane)
    depth = lax.axis_size("z")
    count = lax.axis_size("x")

    def shift(value, step):
        return lax.ppermute(value, chips, [(i, (i + step) % chip_count) for i in range(chip_count)])

    shape = jax.ShapeDtypeStruct
    tables = (cosines, distances, offsets, counts.reshape(1, LOCAL), labels)
    core = lax.axis_index("core").reshape(1)
    part = shape((OWN + TABLE, LOCAL), F32)
    own, send = call(
        pack_kernel, "pack", (part, part), (core, vectors, *tables),
        [pltpu.VMEM(t.shape, t.dtype) for t in tables]
        + [pltpu.SemaphoreType.DMA((len(tables),)), pltpu.SemaphoreType.DMA((NV // BLOCK,))],
        [SMEM] + [RAW] * 6,
    )
    mate = lax.ppermute(send, "core", [(0, 1), (1, 0)])
    slab = call(
        merge_kernel, "merge", shape((CORES, OWN + TABLE, LOCAL), F32), (core, own, mate), (),
        [SMEM, VMEM, VMEM],
    )
    left = shift(slab, 1)
    right = shift(slab, -1)
    matrix = shape((WIDE, LOCAL), BF16)
    matrices = call(own_matrix_kernel, "own_matrix", (matrix,) * 4, (slab,))
    wide = pltpu.VMEM((WIDE, LOCAL), BF16)
    applied, lead = call(
        apply_kernel,
        "apply_twice",
        (shape((OWN, CHIP), F32), shape((2 * BLOCK, CHIP), F32)),
        (left, slab, right, *matrices),
        [pltpu.VMEM((OWN, 3 * CHIP), BF16)] * 2 + [pltpu.VMEM((OWN, 2 * CHIP), BF16)] * 2 + [wide] * 4,
    )
    other = lax.ppermute(lead, "core", [(0, 1), (1, 0)])
    chip = lax.axis_index("x").reshape(1)
    gram = call(
        gram_kernel, "gram", shape((OWN // 128, HEAD, 128), F32),
        (core, lead, other, applied), (), [SMEM] + [VMEM] * 3,
    )
    home, *sent = call(
        share_kernel, "share",
        (shape((HEAD + BLOCK, CHIP), F32),) + (shape((HALF + BLOCK, CHIP), F32),) * (count - 1),
        (core, chip, lead, other, applied), (), [SMEM] * 2 + [VMEM] * 3,
    )
    piece = (OWN // 128) * HEAD // planes
    everyone = planes * CORES
    gram = exchange(gram.reshape(planes, piece, 128), plane)
    gram = call(sum_kernel, "sum_plane", shape((depth, piece, 128), F32), (gram,))
    got = [
        lax.ppermute(value, "x", [(i, (i + step + 1) % count) for i in range(count)])
        for step, value in enumerate(sent)
    ]
    gram = exchange(gram, "z")
    gram = call(sum_kernel, "sum_depth", shape((everyone, piece, 128), F32), (gram,))
    _, *ready = lax.optimization_barrier((gram, *got))
    stacked = call(
        stack_kernel, "stack", (shape((HALF * (count - 1) // 2, CHIP), F32),) * 2, ready
    )
    theirs = [lax.ppermute(value, "core", [(0, 1), (1, 0)]) for value in stacked]
    gram = exchange(gram, (*plane, "core"))
    gram = gram.reshape(planes, CORES, piece, 128)
    scale = 1.0 / (CHIP * chip_count)
    slab_width = CHIP * count
    return call(
        lambda *refs: finish_kernel(scale, *refs), "finish", shape((BLOCK, slab_width), F32),
        (core, chip, gram, home, *theirs, *got),
        [pltpu.VMEM((count, BLOCK, CHIP), F32), pltpu.SemaphoreType.DMA((count,))],
        [SMEM] * 2 + [VMEM] * (3 + count), RAW,
    )


def solution(mesh):
    rows = mesh.shape["rows"]
    cols = mesh.shape["cols"]
    names = ("y", "z", "x", "core")
    cube = Mesh(mesh.devices.reshape(Y_SIZE, rows // Y_SIZE, cols // CORES, CORES), names)
    whole = P(None, names)
    placed = (whole, whole, P(names), whole, whole, whole)
    return jax.shard_map(
        on_device, mesh=cube, in_specs=placed, out_specs=P(("x", "core"), ("y", "z")),
        check_vma=False,
    )
```

```python
import jax
import jax.numpy as jnp
from jax import lax
from jax.experimental import pallas as pl
from jax.experimental.pallas import tpu as pltpu
from jax.sharding import Mesh, PartitionSpec as P

PI_BOND = -1.0
SIGMA_BOND = 0.178
DECAY_LENGTH = 0.319
LAYER_GAP = 2.36
SITE_MASS = 0.4
LAYER_BIAS = 0.25

BLOCK = 64
STEPS = 3
HEAD = BLOCK * STEPS
SLOTS = 16
REACH = 256
NV = 512
LOCAL = 256
WIDE = LOCAL + 2 * REACH
CHUNK = 128
Y_SIZE = 4
CORES = 2
OWN = NV // CORES
TABLE = 40
HALF = HEAD // CORES
CHIP = CORES * LOCAL
F32 = jnp.float32
BF16 = jnp.bfloat16
HIGHEST = lax.Precision.HIGHEST
VMEM = pl.BlockSpec(memory_space=pltpu.VMEM)
PARAMS = pltpu.CompilerParams(vmem_limit_bytes=48 * 1024 * 1024)


def pack_kernel(
    core_ref, vectors_ref, cosines_ref, distances_ref, offsets_ref, counts_ref, labels_ref,
    own_ref, send_ref, cosines, distances, offsets, counts, labels, table_sems, block_sems,
):
    tables = (
        (cosines_ref, cosines), (distances_ref, distances), (offsets_ref, offsets),
        (counts_ref, counts), (labels_ref, labels),
    )
    table_copies = [
        pltpu.make_async_copy(source, target, table_sems.at[i])
        for i, (source, target) in enumerate(tables)
    ]
    block_copies = []
    for owner, ref in ((core_ref[0], own_ref), (1 - core_ref[0], send_ref)):
        for p in range(OWN // BLOCK):
            start = pl.multiple_of((owner + CORES * p) * BLOCK, BLOCK)
            block_copies.append(
                pltpu.make_async_copy(
                    vectors_ref.at[pl.ds(start, BLOCK)],
                    ref.at[pl.ds(BLOCK * p, BLOCK)],
                    block_sems.at[len(block_copies)],
                )
            )
    for copy in table_copies + block_copies:
        copy.start()
    for copy in table_copies:
        copy.wait()
    square = cosines[...] * cosines[...]
    bond = PI_BOND * jnp.exp(-(distances[...] - 1.0) / DECAY_LENGTH) * (1.0 - square)
    bond = bond + SIGMA_BOND * jnp.exp(-(distances[...] - LAYER_GAP) / DECAY_LENGTH) * square
    slot = lax.broadcasted_iota(jnp.int32, bond.shape, 0)
    hopping = jnp.where(slot < counts[...], bond, 0.0)
    steps = offsets[...].astype(F32)
    merged = jnp.zeros_like(hopping)
    for k in range(SLOTS):
        merged = merged + jnp.where(steps == steps[k : k + 1], hopping[k : k + 1], 0.0)
    sides = labels[...].astype(F32)
    onsite = SITE_MASS * (2.0 * sides[0:1] - 1.0) + LAYER_BIAS * (2.0 * sides[1:2] - 1.0)
    for ref in (own_ref, send_ref):
        ref[OWN : OWN + 16, :] = merged
        ref[OWN + 16 : OWN + 32, :] = steps
        ref[OWN + 32 : OWN + 40, :] = jnp.broadcast_to(onsite, (8, LOCAL))
    for copy in block_copies:
        copy.wait()


def merge_kernel(core_ref, own_ref, mate_ref, slab_ref):
    slab_ref[core_ref[0]] = own_ref[...]
    slab_ref[1 - core_ref[0]] = mate_ref[...]


def sum_kernel(pieces_ref, out_ref):
    total = pieces_ref[0]
    for i in range(1, pieces_ref.shape[0]):
        total = total + pieces_ref[i]
    for i in range(out_ref.shape[0]):
        out_ref[i] = total


def build_matrix(table, high_ref, low_ref):
    hopping, offsets, onsite = table[0:16], table[16:32], table[32:33]
    lane = lax.broadcasted_iota(jnp.int32, (1, 128), 1).astype(F32)
    row_index = lax.broadcasted_iota(jnp.int32, (CHUNK, 128), 0).astype(F32)
    for half in range(2):
        columns = slice(128 * half, 128 * half + 128)
        empty = 640 * (1 - half)
        high_ref[empty : empty + 128, columns] = jnp.zeros((128, 128), BF16)
        low_ref[empty : empty + 128, columns] = jnp.zeros((128, 128), BF16)
        home = lane + float(REACH)
        targets = [
            jnp.broadcast_to(offsets[k : k + 1, columns] + home, (CHUNK, 128)) for k in range(SLOTS)
        ]
        values = [jnp.broadcast_to(hopping[k : k + 1, columns], (CHUNK, 128)) for k in range(SLOTS)]
        homes = jnp.broadcast_to(home, (CHUNK, 128))
        own = jnp.broadcast_to(onsite[:, columns], (CHUNK, 128))

        def chunk(step, carry):
            base = step * CHUNK
            rows = row_index + base.astype(F32)
            total = jnp.where(homes == rows, own, 0.0)
            for k in range(SLOTS):
                total = jnp.where(targets[k] == rows, values[k], total)
            high = total.astype(BF16)
            low = (total - high.astype(F32)).astype(BF16)
            place = pl.ds(pl.multiple_of(base + 128 * half, 128), CHUNK)
            high_ref[place, columns] = high
            low_ref[place, columns] = low
            return carry

        lax.fori_loop(0, (WIDE - 128) // CHUNK, chunk, 0)


def own_matrix_kernel(slab_ref, *refs):
    for core in range(CORES):
        build_matrix(slab_ref[core, OWN:, :], refs[2 * core], refs[2 * core + 1])


def split(value):
    high = value.astype(BF16)
    return high, (value - high.astype(F32)).astype(BF16)


def dot3(high, low, matrix_high, matrix_low):
    def dot(left, right):
        return jnp.dot(left, right, preferred_element_type=F32)

    return dot(high, matrix_high) + (dot(high, matrix_low) + dot(low, matrix_high))


def apply_kernel(
    left_ref, own_ref, right_ref, first_high_ref, first_low_ref, second_high_ref, second_low_ref,
    applied_ref, lead_ref, high_ref, low_ref, once_high_ref, once_low_ref,
    left_high_ref, left_low_ref, right_high_ref, right_low_ref,
):
    build_matrix(left_ref[1, OWN:, :], left_high_ref, left_low_ref)
    build_matrix(right_ref[0, OWN:, :], right_high_ref, right_low_ref)
    sources = [(ref, core) for ref in (left_ref, own_ref, right_ref) for core in range(CORES)]
    for place, (ref, core) in enumerate(sources):
        columns = slice(LOCAL * place, LOCAL * place + LOCAL)
        high, low = split(ref[core, 0:OWN, :])
        high_ref[:, columns] = high
        low_ref[:, columns] = low
    matrices = (
        (left_high_ref, left_low_ref),
        (first_high_ref, first_low_ref),
        (second_high_ref, second_low_ref),
        (right_high_ref, right_low_ref),
    )
    for place, (matrix_high, matrix_low) in enumerate(matrices):
        window = slice(LOCAL * place, LOCAL * place + WIDE)
        columns = slice(LOCAL * place, LOCAL * place + LOCAL)
        once = dot3(high_ref[:, window], low_ref[:, window], matrix_high[...], matrix_low[...])
        high, low = split(once)
        once_high_ref[:, columns] = high
        once_low_ref[:, columns] = low
    for place, (matrix_high, matrix_low) in enumerate(matrices[1:3]):
        window = slice(LOCAL * place, LOCAL * place + WIDE)
        columns = slice(LOCAL * place, LOCAL * place + LOCAL)
        twice = dot3(
            once_high_ref[:, window], once_low_ref[:, window], matrix_high[...], matrix_low[...]
        )
        applied_ref[:, columns] = twice
        lead_ref[:, columns] = twice[0 : 2 * BLOCK]


def head_block(s, core_ref, lead_ref, other_ref):
    place, core = ((0, 0), (0, 1), (BLOCK, 0))[s]
    mine, theirs = lead_ref[place : place + BLOCK, :], other_ref[place : place + BLOCK, :]
    return jnp.where(core_ref[0] == core, mine, theirs)


def gram_kernel(core_ref, lead_ref, other_ref, applied_ref, gram_ref):
    blocks = [head_block(s, core_ref, lead_ref, other_ref) for s in range(STEPS)]
    gram = dot32(jnp.concatenate(blocks, axis=0), applied_ref[...], ((1,), (1,)))
    for part in range(OWN // 128):
        gram_ref[part] = gram[:, 128 * part : 128 * part + 128]


def share_kernel(core_ref, chip_ref, lead_ref, other_ref, applied_ref, home_ref, *sent_refs):
    count = 1 + len(sent_refs)
    second = core_ref[0] == 1
    head = [head_block(s, core_ref, lead_ref, other_ref) for s in range(STEPS)]
    for s in range(STEPS):
        home_ref[BLOCK * s : BLOCK * s + BLOCK, :] = head[s]
    middle = HALF - BLOCK
    half = (
        jnp.where(second, head[1][middle:], head[0][0 : BLOCK - middle]),
        jnp.where(second, head[2][0:BLOCK], jnp.concatenate(
            [head[0][BLOCK - middle :], head[1][0:middle]], axis=0)),
    )
    for ref in sent_refs:
        ref[0 : BLOCK - middle, :] = half[0]
        ref[BLOCK - middle : HALF, :] = half[1]
    for step, ref in enumerate((home_ref, *sent_refs)):
        start = pl.multiple_of(lax.rem(chip_ref[0] + step, count) * BLOCK, BLOCK)
        ref[ref.shape[0] - BLOCK :, :] = applied_ref[pl.ds(start, BLOCK), :]


def stack_kernel(one_ref, two_ref, three_ref, first_ref, last_ref):
    middle = HALF // 2
    first_ref[0:HALF, :] = one_ref[0:HALF, :]
    first_ref[HALF:, :] = two_ref[0:middle, :]
    last_ref[0:middle, :] = two_ref[middle:HALF, :]
    last_ref[middle:, :] = three_ref[0:HALF, :]


def spread(value):
    return jnp.broadcast_to(value, (8, 128))


def inverse_factor(pair):
    rows = [pair[8 * i : 8 * i + 8] for i in range(BLOCK // 8)]
    sublane = lax.broadcasted_iota(jnp.int32, (8, 128), 0)
    for p in range(BLOCK // 8):
        start = BLOCK + 8 * p
        columns = [
            [spread(rows[i][:, start + b : start + b + 1]) for b in range(8)]
            for i in range(p, BLOCK // 8)
        ]
        for j in range(8):
            inverse = lax.rsqrt(spread(columns[0][j][j : j + 1]))
            pivot_row = spread(rows[p][j : j + 1]) * inverse
            heads = [spread(columns[0][b][j : j + 1]) * inverse for b in range(j + 1, 8)]
            for i in range(p, BLOCK // 8):
                factor = columns[i - p][j] * inverse
                if i == p:
                    factor = jnp.where(sublane > j, factor, 0.0)
                rows[i] = rows[i] - factor * pivot_row
                for b in range(j + 1, 8):
                    columns[i - p][b] = columns[i - p][b] - factor * heads[b - j - 1]
            rows[p] = jnp.where(sublane == j, pivot_row, rows[p])
    return jnp.concatenate(rows, axis=0)[:, 0:BLOCK]


def dot32(left, right, dims):
    return lax.dot_general(
        left, right, (dims, ((), ())), precision=HIGHEST, preferred_element_type=F32
    )


def finish_kernel(scale, core_ref, chip_ref, gram_ref, *refs):
    home_ref, mate_ref, mate_last_ref, *got_refs, basis_ref, results, sems = refs
    count = 1 + len(got_refs)
    middle = HALF // 2
    mates = (
        lambda: mate_ref[0:HALF, :],
        lambda: jnp.concatenate([mate_ref[HALF:, :], mate_last_ref[0:middle, :]], axis=0),
        lambda: mate_last_ref[middle:, :],
    )
    chip, core = chip_ref[0], core_ref[0]
    second = core == 1
    column = CORES * chip + core
    tiles = gram_ref.shape[0] // 2

    def columns_of(part, core):
        return jnp.concatenate([gram_ref[part * tiles + m, core] for m in range(tiles)], axis=0)

    first_pair, second_pair = columns_of(0, 0), columns_of(0, 1)
    low = jnp.where(second, second_pair, first_pair)
    high = jnp.where(second, columns_of(1, 1), columns_of(1, 0))
    mine = jnp.where(chip >= 2, high, low)
    mine = jnp.where(chip % 2 == 1, pltpu.roll(mine, BLOCK, axis=1), mine)
    full = jnp.concatenate([first_pair, second_pair, mine], axis=1) * scale
    gram = [full[BLOCK * s : BLOCK * s + BLOCK] for s in range(STEPS)]
    places = (0, 2 * BLOCK, BLOCK)
    lane = lax.broadcasted_iota(jnp.int32, (BLOCK, 128), 1)
    row = lax.broadcasted_iota(jnp.int32, (BLOCK, 128), 0)
    identity = jnp.where(lane == row, 1.0, 0.0).astype(F32)
    zero = jnp.zeros((BLOCK, BLOCK), F32)
    for s in range(STEPS):
        unit = [identity[:, 0:BLOCK] if t == s else zero for t in range(STEPS)]
        gram[s] = jnp.concatenate([gram[s], *unit], axis=1)
    couplings = []
    for s in range(STEPS):
        part = places[s] // 128
        tile = gram[s][:, 128 * part : 128 * part + 128]
        if places[s] % 128 == 0:
            tile = pltpu.roll(tile, BLOCK, axis=1)
        inverse = inverse_factor(jnp.where(lane < BLOCK, identity, tile))
        coupling = dot32(inverse, gram[s], ((1,), (0,)))
        for t in range(s + 1, STEPS):
            gram[t] = gram[t] - dot32(
                coupling[:, places[t] : places[t] + BLOCK], coupling, ((0,), (0,))
            )
        couplings.append(coupling)
    follows = column >= STEPS
    units = 6 * BLOCK
    mine = jnp.concatenate([c[:, 4 * BLOCK : 5 * BLOCK] for c in couplings], axis=0)
    inverse = jnp.concatenate([c[:, units:] for c in couplings], axis=0)
    weight = -dot32(mine, inverse, ((0,), (0,)))
    for s in range(STEPS):
        weight = jnp.where(column == s, couplings[s][:, units:], weight)
    parts = split(weight)
    outs = []
    for step in range(count):
        if step == 0:
            head, block = home_ref[0:HEAD, :], home_ref[HEAD:, :]
        else:
            got = got_refs[step - 1]
            first, last = got[0:HALF, :], mates[step - 1]()
            head = jnp.where(
                second,
                jnp.concatenate([last, first], axis=0),
                jnp.concatenate([first, last], axis=0),
            )
            block = got[HALF:, :]
        head_high, head_low = split(head)
        results[step] = jnp.where(follows, block, 0.0) + dot3(*parts, head_high, head_low)
        source = lax.rem(chip + count - step, count)
        columns = pl.ds(pl.multiple_of(source * CHIP, CHIP), CHIP)
        out = pltpu.make_async_copy(results.at[step], basis_ref.at[:, columns], sems.at[step])
        out.start()
        outs.append(out)
    for out in outs:
        out.wait()


def exchange(value, axes):
    return lax.all_to_all(value, axes, split_axis=0, concat_axis=0, tiled=True)


SMEM = pl.BlockSpec(memory_space=pltpu.SMEM)
RAW = pl.BlockSpec(memory_space=pltpu.HBM)


def call(kernel, name, out_shape, inputs, scratch=(), specs=None, out_specs=None):
    single = not isinstance(out_shape, (tuple, list))
    if specs:
        inputs = [
            pltpu.with_memory_space_constraint(value, pltpu.HBM) if spec is RAW else value
            for value, spec in zip(inputs, specs)
        ]
    return pl.pallas_call(
        kernel,
        out_shape=out_shape,
        in_specs=specs or [VMEM] * len(inputs),
        out_specs=out_specs or VMEM if single else (VMEM,) * len(out_shape),
        scratch_shapes=list(scratch),
        compiler_params=PARAMS,
        name=name,
    )(*inputs)


def on_device(vectors, offsets, counts, labels, cosines, distances):
    chips = ("y", "z", "x")
    plane = ("y", "x")
    chip_count = lax.axis_size(chips)
    planes = lax.axis_size(plane)
    depth = lax.axis_size("z")
    count = lax.axis_size("x")

    def shift(value, step):
        return lax.ppermute(value, chips, [(i, (i + step) % chip_count) for i in range(chip_count)])

    shape = jax.ShapeDtypeStruct
    tables = (cosines, distances, offsets, counts.reshape(1, LOCAL), labels)
    core = lax.axis_index("core").reshape(1)
    part = shape((OWN + TABLE, LOCAL), F32)
    own, send = call(
        pack_kernel, "pack", (part, part), (core, vectors, *tables),
        [pltpu.VMEM(t.shape, t.dtype) for t in tables]
        + [pltpu.SemaphoreType.DMA((len(tables),)), pltpu.SemaphoreType.DMA((NV // BLOCK,))],
        [SMEM] + [RAW] * 6,
    )
    mate = lax.ppermute(send, "core", [(0, 1), (1, 0)])
    slab = call(
        merge_kernel, "merge", shape((CORES, OWN + TABLE, LOCAL), F32), (core, own, mate), (),
        [SMEM, VMEM, VMEM],
    )
    left = shift(slab, 1)
    right = shift(slab, -1)
    matrix = shape((WIDE, LOCAL), BF16)
    matrices = call(own_matrix_kernel, "own_matrix", (matrix,) * 4, (slab,))
    wide = pltpu.VMEM((WIDE, LOCAL), BF16)
    applied, lead = call(
        lambda right, own, left, *rest: apply_kernel(left, own, right, *rest),
        "apply_twice",
        (shape((OWN, CHIP), F32), shape((2 * BLOCK, CHIP), F32)),
        (right, slab, left, *matrices),
        [pltpu.VMEM((OWN, 3 * CHIP), BF16)] * 2 + [pltpu.VMEM((OWN, 2 * CHIP), BF16)] * 2 + [wide] * 4,
    )
    other = lax.ppermute(lead, "core", [(0, 1), (1, 0)])
    chip = lax.axis_index("x").reshape(1)
    gram = call(
        gram_kernel, "gram", shape((OWN // 128, HEAD, 128), F32),
        (core, lead, other, applied), (), [SMEM] + [VMEM] * 3,
    )
    home, *sent = call(
        share_kernel, "share",
        (shape((HEAD + BLOCK, CHIP), F32),) + (shape((HALF + BLOCK, CHIP), F32),) * (count - 1),
        (core, chip, lead, other, applied), (), [SMEM] * 2 + [VMEM] * 3,
    )
    piece = (OWN // 128) * HEAD // planes
    everyone = planes * CORES
    gram = exchange(gram.reshape(planes, piece, 128), plane)
    gram = call(sum_kernel, "sum_plane", shape((depth, piece, 128), F32), (gram,))
    got = [
        lax.ppermute(value, "x", [(i, (i + step + 1) % count) for i in range(count)])
        for step, value in enumerate(sent)
    ]
    gram = exchange(gram, "z")
    gram = call(sum_kernel, "sum_depth", shape((everyone, piece, 128), F32), (gram,))
    _, *ready = lax.optimization_barrier((gram, *got))
    stacked = call(
        stack_kernel, "stack", (shape((HALF * (count - 1) // 2, CHIP), F32),) * 2, ready
    )
    theirs = [lax.ppermute(value, "core", [(0, 1), (1, 0)]) for value in stacked]
    gram = exchange(gram, (*plane, "core"))
    gram = gram.reshape(planes, CORES, piece, 128)
    scale = 1.0 / (CHIP * chip_count)
    slab_width = CHIP * count
    return call(
        lambda *refs: finish_kernel(scale, *refs), "finish", shape((BLOCK, slab_width), F32),
        (core, chip, gram, home, *theirs, *got),
        [pltpu.VMEM((count, BLOCK, CHIP), F32), pltpu.SemaphoreType.DMA((count,))],
        [SMEM] * 2 + [VMEM] * (3 + count), RAW,
    )


def solution(mesh):
    rows = mesh.shape["rows"]
    cols = mesh.shape["cols"]
    names = ("y", "z", "x", "core")
    cube = Mesh(mesh.devices.reshape(Y_SIZE, rows // Y_SIZE, cols // CORES, CORES), names)
    whole = P(None, names)
    placed = (whole, whole, P(names), whole, whole, whole)
    return jax.shard_map(
        on_device, mesh=cube, in_specs=placed, out_specs=P(("x", "core"), ("y", "z")),
        check_vma=False,
    )
```

```python
import jax
import jax.numpy as jnp
from jax import lax
from jax.experimental import pallas as pl
from jax.experimental.pallas import tpu as pltpu
from jax.sharding import Mesh, PartitionSpec as P

PI_BOND = -1.0
SIGMA_BOND = 0.178
DECAY_LENGTH = 0.319
LAYER_GAP = 2.36
SITE_MASS = 0.4
LAYER_BIAS = 0.25

BLOCK = 64
STEPS = 3
HEAD = BLOCK * STEPS
SLOTS = 16
REACH = 256
NV = 512
LOCAL = 256
WIDE = LOCAL + 2 * REACH
CHUNK = 128
Y_SIZE = 4
CORES = 2
OWN = NV // CORES
TABLE = 40
HALF = HEAD // CORES
CHIP = CORES * LOCAL
F32 = jnp.float32
BF16 = jnp.bfloat16
HIGHEST = lax.Precision.HIGHEST
VMEM = pl.BlockSpec(memory_space=pltpu.VMEM)
PARAMS = pltpu.CompilerParams(vmem_limit_bytes=48 * 1024 * 1024)


def pack_kernel(
    core_ref, vectors_ref, cosines_ref, distances_ref, offsets_ref, counts_ref, labels_ref,
    own_ref, send_ref, cosines, distances, offsets, counts, labels, table_sems, block_sems,
):
    tables = (
        (cosines_ref, cosines), (distances_ref, distances), (offsets_ref, offsets),
        (counts_ref, counts), (labels_ref, labels),
    )
    table_copies = [
        pltpu.make_async_copy(source, target, table_sems.at[i])
        for i, (source, target) in enumerate(tables)
    ]
    block_copies = []
    for owner, ref in ((core_ref[0], own_ref), (1 - core_ref[0], send_ref)):
        for p in range(OWN // BLOCK):
            start = pl.multiple_of((owner + CORES * p) * BLOCK, BLOCK)
            block_copies.append(
                pltpu.make_async_copy(
                    vectors_ref.at[pl.ds(start, BLOCK)],
                    ref.at[pl.ds(BLOCK * p, BLOCK)],
                    block_sems.at[len(block_copies)],
                )
            )
    for copy in table_copies + block_copies:
        copy.start()
    for copy in table_copies:
        copy.wait()
    square = cosines[...] * cosines[...]
    bond = PI_BOND * jnp.exp(-(distances[...] - 1.0) / DECAY_LENGTH) * (1.0 - square)
    bond = bond + SIGMA_BOND * jnp.exp(-(distances[...] - LAYER_GAP) / DECAY_LENGTH) * square
    slot = lax.broadcasted_iota(jnp.int32, bond.shape, 0)
    hopping = jnp.where(slot < counts[...], bond, 0.0)
    steps = offsets[...].astype(F32)
    merged = jnp.zeros_like(hopping)
    for k in range(SLOTS):
        merged = merged + jnp.where(steps == steps[k : k + 1], hopping[k : k + 1], 0.0)
    sides = labels[...].astype(F32)
    onsite = SITE_MASS * (2.0 * sides[0:1] - 1.0) + LAYER_BIAS * (2.0 * sides[1:2] - 1.0)
    for ref in (own_ref, send_ref):
        ref[OWN : OWN + 16, :] = merged
        ref[OWN + 16 : OWN + 32, :] = steps
        ref[OWN + 32 : OWN + 40, :] = jnp.broadcast_to(onsite, (8, LOCAL))
    for copy in block_copies:
        copy.wait()


def merge_kernel(core_ref, own_ref, mate_ref, slab_ref):
    slab_ref[core_ref[0]] = own_ref[...]
    slab_ref[1 - core_ref[0]] = mate_ref[...]


def sum_kernel(pieces_ref, out_ref):
    total = pieces_ref[0]
    for i in range(1, pieces_ref.shape[0]):
        total = total + pieces_ref[i]
    for i in range(out_ref.shape[0]):
        out_ref[i] = total


def build_matrix(table, high_ref, low_ref):
    hopping, offsets, onsite = table[0:16], table[16:32], table[32:33]
    lane = lax.broadcasted_iota(jnp.int32, (1, 128), 1).astype(F32)
    row_index = lax.broadcasted_iota(jnp.int32, (CHUNK, 128), 0).astype(F32)
    for half in range(2):
        columns = slice(128 * half, 128 * half + 128)
        empty = 640 * (1 - half)
        high_ref[empty : empty + 128, columns] = jnp.zeros((128, 128), BF16)
        low_ref[empty : empty + 128, columns] = jnp.zeros((128, 128), BF16)
        home = lane + float(REACH)
        targets = [
            jnp.broadcast_to(offsets[k : k + 1, columns] + home, (CHUNK, 128)) for k in range(SLOTS)
        ]
        values = [jnp.broadcast_to(hopping[k : k + 1, columns], (CHUNK, 128)) for k in range(SLOTS)]
        homes = jnp.broadcast_to(home, (CHUNK, 128))
        own = jnp.broadcast_to(onsite[:, columns], (CHUNK, 128))

        def chunk(step, carry):
            base = step * CHUNK
            rows = row_index + base.astype(F32)
            total = jnp.where(homes == rows, own, 0.0)
            for k in range(SLOTS):
                total = jnp.where(targets[k] == rows, values[k], total)
            high = total.astype(BF16)
            low = (total - high.astype(F32)).astype(BF16)
            place = pl.ds(pl.multiple_of(base + 128 * half, 128), CHUNK)
            high_ref[place, columns] = high
            low_ref[place, columns] = low
            return carry

        lax.fori_loop(0, (WIDE - 128) // CHUNK, chunk, 0)


def own_matrix_kernel(slab_ref, *refs):
    for core in range(CORES):
        build_matrix(slab_ref[core, OWN:, :], refs[2 * core], refs[2 * core + 1])


def split(value):
    high = value.astype(BF16)
    return high, (value - high.astype(F32)).astype(BF16)


def dot3(high, low, matrix_high, matrix_low):
    def dot(left, right):
        return jnp.dot(left, right, preferred_element_type=F32)

    return dot(high, matrix_high) + (dot(high, matrix_low) + dot(low, matrix_high))


def apply_kernel(
    left_ref, own_ref, right_ref, first_high_ref, first_low_ref, second_high_ref, second_low_ref,
    applied_ref, lead_ref, high_ref, low_ref, once_high_ref, once_low_ref,
    left_high_ref, left_low_ref, right_high_ref, right_low_ref,
):
    build_matrix(left_ref[1, OWN:, :], left_high_ref, left_low_ref)
    build_matrix(right_ref[0, OWN:, :], right_high_ref, right_low_ref)
    sources = [(ref, core) for ref in (left_ref, own_ref, right_ref) for core in range(CORES)]
    for place, (ref, core) in enumerate(sources):
        columns = slice(LOCAL * place, LOCAL * place + LOCAL)
        high, low = split(ref[core, 0:OWN, :])
        high_ref[:, columns] = high
        low_ref[:, columns] = low
    matrices = (
        (left_high_ref, left_low_ref),
        (first_high_ref, first_low_ref),
        (second_high_ref, second_low_ref),
        (right_high_ref, right_low_ref),
    )
    for place, (matrix_high, matrix_low) in enumerate(matrices):
        window = slice(LOCAL * place, LOCAL * place + WIDE)
        columns = slice(LOCAL * place, LOCAL * place + LOCAL)
        once = dot3(high_ref[:, window], low_ref[:, window], matrix_high[...], matrix_low[...])
        high, low = split(once)
        once_high_ref[:, columns] = high
        once_low_ref[:, columns] = low
    for place, (matrix_high, matrix_low) in enumerate(matrices[1:3]):
        window = slice(LOCAL * place, LOCAL * place + WIDE)
        columns = slice(LOCAL * place, LOCAL * place + LOCAL)
        twice = dot3(
            once_high_ref[:, window], once_low_ref[:, window], matrix_high[...], matrix_low[...]
        )
        applied_ref[:, columns] = twice
        lead_ref[:, columns] = twice[0 : 2 * BLOCK]


def head_block(s, core_ref, lead_ref, other_ref):
    place, core = ((0, 0), (0, 1), (BLOCK, 0))[s]
    mine, theirs = lead_ref[place : place + BLOCK, :], other_ref[place : place + BLOCK, :]
    return jnp.where(core_ref[0] == core, mine, theirs)


def gram_kernel(core_ref, lead_ref, other_ref, applied_ref, gram_ref):
    blocks = [head_block(s, core_ref, lead_ref, other_ref) for s in range(STEPS)]
    gram = dot32(jnp.concatenate(blocks, axis=0), applied_ref[...], ((1,), (1,)))
    for part in range(OWN // 128):
        gram_ref[part] = gram[:, 128 * part : 128 * part + 128]


def share_kernel(core_ref, chip_ref, lead_ref, other_ref, applied_ref, *sent_refs):
    count = 1 + len(sent_refs)
    second = core_ref[0] == 1
    head = [head_block(s, core_ref, lead_ref, other_ref) for s in range(STEPS)]
    middle = HALF - BLOCK
    rest = BLOCK - middle
    top = jnp.where(second, head[1][middle:], head[0][0:rest])
    bottom = jnp.where(
        second, head[2], jnp.concatenate([head[0][rest:], head[1][0:middle]], axis=0)
    )
    for step, ref in enumerate(sent_refs):
        ref[0:rest, :] = top
        ref[rest:HALF, :] = bottom
        start = pl.multiple_of(lax.rem(chip_ref[0] + step + 1, count) * BLOCK, BLOCK)
        ref[HALF:, :] = applied_ref[pl.ds(start, BLOCK), :]


def stack_kernel(
    core_ref, chip_ref, lead_ref, other_ref, applied_ref, one_ref, two_ref, three_ref,
    first_ref, last_ref, home_ref,
):
    middle = HALF // 2
    first_ref[0:HALF, :] = one_ref[0:HALF, :]
    first_ref[HALF:, :] = two_ref[0:middle, :]
    last_ref[0:middle, :] = two_ref[middle:HALF, :]
    last_ref[middle:, :] = three_ref[0:HALF, :]
    for s in range(STEPS):
        block = head_block(s, core_ref, lead_ref, other_ref)
        home_ref[BLOCK * s : BLOCK * s + BLOCK, :] = block
    start = pl.multiple_of(chip_ref[0] * BLOCK, BLOCK)
    home_ref[HEAD:, :] = applied_ref[pl.ds(start, BLOCK), :]


def spread(value):
    return jnp.broadcast_to(value, (8, 128))


def inverse_factor(pair):
    rows = [pair[8 * i : 8 * i + 8] for i in range(BLOCK // 8)]
    sublane = lax.broadcasted_iota(jnp.int32, (8, 128), 0)
    for p in range(BLOCK // 8):
        start = BLOCK + 8 * p
        columns = [
            [spread(rows[i][:, start + b : start + b + 1]) for b in range(8)]
            for i in range(p, BLOCK // 8)
        ]
        for j in range(8):
            inverse = lax.rsqrt(spread(columns[0][j][j : j + 1]))
            pivot_row = spread(rows[p][j : j + 1]) * inverse
            heads = [spread(columns[0][b][j : j + 1]) * inverse for b in range(j + 1, 8)]
            for i in range(p, BLOCK // 8):
                factor = columns[i - p][j] * inverse
                if i == p:
                    factor = jnp.where(sublane > j, factor, 0.0)
                rows[i] = rows[i] - factor * pivot_row
                for b in range(j + 1, 8):
                    columns[i - p][b] = columns[i - p][b] - factor * heads[b - j - 1]
            rows[p] = jnp.where(sublane == j, pivot_row, rows[p])
    return jnp.concatenate(rows, axis=0)[:, 0:BLOCK]


def dot32(left, right, dims):
    return lax.dot_general(
        left, right, (dims, ((), ())), precision=HIGHEST, preferred_element_type=F32
    )


def finish_kernel(scale, core_ref, chip_ref, gram_ref, *refs):
    home_ref, mate_ref, mate_last_ref, *got_refs, basis_ref, results, sems = refs
    count = 1 + len(got_refs)
    middle = HALF // 2
    mates = (
        lambda: mate_ref[0:HALF, :],
        lambda: jnp.concatenate([mate_ref[HALF:, :], mate_last_ref[0:middle, :]], axis=0),
        lambda: mate_last_ref[middle:, :],
    )
    chip, core = chip_ref[0], core_ref[0]
    second = core == 1
    column = CORES * chip + core
    tiles = gram_ref.shape[0] // 2

    def columns_of(part, core):
        return jnp.concatenate([gram_ref[part * tiles + m, core] for m in range(tiles)], axis=0)

    first_pair, second_pair = columns_of(0, 0), columns_of(0, 1)
    low = jnp.where(second, second_pair, first_pair)
    high = jnp.where(second, columns_of(1, 1), columns_of(1, 0))
    mine = jnp.where(chip >= 2, high, low)
    mine = jnp.where(chip % 2 == 1, pltpu.roll(mine, BLOCK, axis=1), mine)
    full = jnp.concatenate([first_pair, second_pair, mine], axis=1) * scale
    gram = [full[BLOCK * s : BLOCK * s + BLOCK] for s in range(STEPS)]
    places = (0, 2 * BLOCK, BLOCK)
    lane = lax.broadcasted_iota(jnp.int32, (BLOCK, 128), 1)
    row = lax.broadcasted_iota(jnp.int32, (BLOCK, 128), 0)
    identity = jnp.where(lane == row, 1.0, 0.0).astype(F32)
    zero = jnp.zeros((BLOCK, BLOCK), F32)
    for s in range(STEPS):
        unit = [identity[:, 0:BLOCK] if t == s else zero for t in range(STEPS)]
        gram[s] = jnp.concatenate([gram[s], *unit], axis=1)
    couplings = []
    for s in range(STEPS):
        part = places[s] // 128
        tile = gram[s][:, 128 * part : 128 * part + 128]
        if places[s] % 128 == 0:
            tile = pltpu.roll(tile, BLOCK, axis=1)
        inverse = inverse_factor(jnp.where(lane < BLOCK, identity, tile))
        coupling = dot32(inverse, gram[s], ((1,), (0,)))
        for t in range(s + 1, STEPS):
            gram[t] = gram[t] - dot32(
                coupling[:, places[t] : places[t] + BLOCK], coupling, ((0,), (0,))
            )
        couplings.append(coupling)
    follows = column >= STEPS
    units = 6 * BLOCK
    mine = jnp.concatenate([c[:, 4 * BLOCK : 5 * BLOCK] for c in couplings], axis=0)
    inverse = jnp.concatenate([c[:, units:] for c in couplings], axis=0)
    weight = -dot32(mine, inverse, ((0,), (0,)))
    for s in range(STEPS):
        weight = jnp.where(column == s, couplings[s][:, units:], weight)
    parts = split(weight)
    outs = []
    for step in range(count):
        if step == 0:
            head, block = home_ref[0:HEAD, :], home_ref[HEAD:, :]
        else:
            got = got_refs[step - 1]
            first, last = got[0:HALF, :], mates[step - 1]()
            head = jnp.where(
                second,
                jnp.concatenate([last, first], axis=0),
                jnp.concatenate([first, last], axis=0),
            )
            block = got[HALF:, :]
        head_high, head_low = split(head)
        results[step] = jnp.where(follows, block, 0.0) + dot3(*parts, head_high, head_low)
        source = lax.rem(chip + count - step, count)
        columns = pl.ds(pl.multiple_of(source * CHIP, CHIP), CHIP)
        out = pltpu.make_async_copy(results.at[step], basis_ref.at[:, columns], sems.at[step])
        out.start()
        outs.append(out)
    for out in outs:
        out.wait()


def exchange(value, axes):
    return lax.all_to_all(value, axes, split_axis=0, concat_axis=0, tiled=True)


SMEM = pl.BlockSpec(memory_space=pltpu.SMEM)
RAW = pl.BlockSpec(memory_space=pltpu.HBM)


def call(kernel, name, out_shape, inputs, scratch=(), specs=None, out_specs=None):
    single = not isinstance(out_shape, (tuple, list))
    if specs:
        inputs = [
            pltpu.with_memory_space_constraint(value, pltpu.HBM) if spec is RAW else value
            for value, spec in zip(inputs, specs)
        ]
    return pl.pallas_call(
        kernel,
        out_shape=out_shape,
        in_specs=specs or [VMEM] * len(inputs),
        out_specs=out_specs or VMEM if single else (VMEM,) * len(out_shape),
        scratch_shapes=list(scratch),
        compiler_params=PARAMS,
        name=name,
    )(*inputs)


def on_device(vectors, offsets, counts, labels, cosines, distances):
    chips = ("y", "z", "x")
    plane = ("y", "x")
    chip_count = lax.axis_size(chips)
    planes = lax.axis_size(plane)
    depth = lax.axis_size("z")
    count = lax.axis_size("x")

    def shift(value, step):
        return lax.ppermute(value, chips, [(i, (i + step) % chip_count) for i in range(chip_count)])

    shape = jax.ShapeDtypeStruct
    tables = (cosines, distances, offsets, counts.reshape(1, LOCAL), labels)
    core = lax.axis_index("core").reshape(1)
    part = shape((OWN + TABLE, LOCAL), F32)
    own, send = call(
        pack_kernel, "pack", (part, part), (core, vectors, *tables),
        [pltpu.VMEM(t.shape, t.dtype) for t in tables]
        + [pltpu.SemaphoreType.DMA((len(tables),)), pltpu.SemaphoreType.DMA((NV // BLOCK,))],
        [SMEM] + [RAW] * 6,
    )
    mate = lax.ppermute(send, "core", [(0, 1), (1, 0)])
    slab = call(
        merge_kernel, "merge", shape((CORES, OWN + TABLE, LOCAL), F32), (core, own, mate), (),
        [SMEM, VMEM, VMEM],
    )
    left = shift(slab, 1)
    right = shift(slab, -1)
    matrix = shape((WIDE, LOCAL), BF16)
    matrices = call(own_matrix_kernel, "own_matrix", (matrix,) * 4, (slab,))
    wide = pltpu.VMEM((WIDE, LOCAL), BF16)
    applied, lead = call(
        lambda right, own, left, *rest: apply_kernel(left, own, right, *rest),
        "apply_twice",
        (shape((OWN, CHIP), F32), shape((2 * BLOCK, CHIP), F32)),
        (right, slab, left, *matrices),
        [pltpu.VMEM((OWN, 3 * CHIP), BF16)] * 2 + [pltpu.VMEM((OWN, 2 * CHIP), BF16)] * 2 + [wide] * 4,
    )
    other = lax.ppermute(lead, "core", [(0, 1), (1, 0)])
    chip = lax.axis_index("x").reshape(1)
    gram = call(
        gram_kernel, "gram", shape((OWN // 128, HEAD, 128), F32),
        (core, lead, other, applied), (), [SMEM] + [VMEM] * 3,
    )
    sent = call(
        share_kernel, "share", (shape((HALF + BLOCK, CHIP), F32),) * (count - 1),
        (core, chip, lead, other, applied), (), [SMEM] * 2 + [VMEM] * 3,
    )
    piece = (OWN // 128) * HEAD // planes
    everyone = planes * CORES
    gram = exchange(gram.reshape(planes, piece, 128), plane)
    gram = call(sum_kernel, "sum_plane", shape((depth, piece, 128), F32), (gram,))
    got = [
        lax.ppermute(value, "x", [(i, (i + step + 1) % count) for i in range(count)])
        for step, value in enumerate(sent)
    ]
    gram = exchange(gram, "z")
    gram = call(sum_kernel, "sum_depth", shape((everyone, piece, 128), F32), (gram,))
    _, *ready = lax.optimization_barrier((gram, *got))
    *stacked, home = call(
        stack_kernel, "stack",
        (shape((HALF * (count - 1) // 2, CHIP), F32),) * 2 + (shape((HEAD + BLOCK, CHIP), F32),),
        (core, chip, lead, other, applied, *ready), (), [SMEM] * 2 + [VMEM] * (2 + count),
    )
    theirs = [lax.ppermute(value, "core", [(0, 1), (1, 0)]) for value in stacked]
    gram = exchange(gram, (*plane, "core"))
    gram = gram.reshape(planes, CORES, piece, 128)
    scale = 1.0 / (CHIP * chip_count)
    slab_width = CHIP * count
    return call(
        lambda *refs: finish_kernel(scale, *refs), "finish", shape((BLOCK, slab_width), F32),
        (core, chip, gram, home, *theirs, *got),
        [pltpu.VMEM((count, BLOCK, CHIP), F32), pltpu.SemaphoreType.DMA((count,))],
        [SMEM] * 2 + [VMEM] * (3 + count), RAW,
    )


def solution(mesh):
    rows = mesh.shape["rows"]
    cols = mesh.shape["cols"]
    names = ("y", "z", "x", "core")
    cube = Mesh(mesh.devices.reshape(Y_SIZE, rows // Y_SIZE, cols // CORES, CORES), names)
    whole = P(None, names)
    placed = (whole, whole, P(names), whole, whole, whole)
    return jax.shard_map(
        on_device, mesh=cube, in_specs=placed, out_specs=P(("x", "core"), ("y", "z")),
        check_vma=False,
    )
```
